256 devices in a mesh: req: 32 (over y, x, z_lo), seq: 8 (over z_hi, core).
Axes of the slice: x: 4, y: 4, z: 8 (z_hi: 4, z_lo: 2; z = z_hi * 2 + z_lo), core: 2. Of those that a mesh axis runs over, the one named last changes fastest.
Arguments:
- hidden: bfloat16 [32, 256, 2048], P('req', 'seq'), may hold values from -6 to 6
- project_weight: bfloat16 [2048, 3072], P(None, ('req', 'seq')), may hold values from -0.125 to 0.125
- output_weight: bfloat16 [1024, 2048], P(None, ('req', 'seq')), may hold values from -0.75 to 0.75
- cache_pool: bfloat16 [32, 8, 8, 128, 2048], P('req', 'seq'), may hold values from -81 to 81, as said below
- page_table: int32 [32, 64], P('req', 'seq'), may hold values from 0 to 7, as said below
- cache_length: int32 [32], replicated, may hold values from 4 to 8192, as said below
- target_slot: int32 [32], replicated, may hold values from 0 to 31, as said below
Outputs:
- attention_out: bfloat16 [32, 256, 2048], P('req', 'seq')
- arrived_cache: bfloat16 [32, 8192, 2048], P('req', 'seq')
The draws below stay inside these ranges and needn't reach their ends.
Inputs may be any that keep to these rules, and one draw needn't show every extreme that they name: `cache_pool`: pool pages reach the ends of the range in the hidden draw. `cache_length`: in each group of 1 request at most one has 2048 or more cached positions. `page_table`: for request r and lane d, the entries d * 8 + j with j * 8 + d < ceil(cache_length[r] / 128) name pages of that group's pool on lane d, no page serving two of them within a group; all other entries are arbitrary pages. `target_slot`: A permutation made of disjoint swaps, each between a slot of group g and a slot of group (g + n / 2) mod n, n = 32, at most one swap for each such pair of groups.
All inputs are finite; a program needn't handle non-finite values.
Results may differ from the reference program's by a relative error of at most 0.0109.
The reference program's roundings to bfloat16 on the way count: a program that leaves them out, or rounds other values in their place, can miss the bound.
Values may be sent and summed in bfloat16 or wider, within the bound.
A program may use at most 128 MiB of HBM per device.

```python
import math
import jax
import jax.numpy as jnp
from jax import lax

D = 2048
HEADS = 8
HEAD = 128
PAGE = 128
MAXPG_DEV = 8
STRETCH = 256
REQ_DEV = 1
KVW = 1024
LANES = 8
REQUESTS = 32
MAXLEN = 8192
SHORT_MAX = 2048
PAGES_DEV = 8
N_REQ = 32


def draw_cache_length(key, part):
    groups = REQUESTS // REQ_DEV
    base_key = jax.random.fold_in(key, 11)
    key_list = jax.random.split(base_key, 6)
    long_slot = jax.random.randint(key_list[0], (groups,), 0, REQ_DEV)
    long_low = int(PAGE * LANES).bit_length() - 1
    long_high = int(MAXLEN).bit_length() - 1
    long_power = jax.random.randint(key_list[1], (groups,), long_low, long_high)
    long_base = jnp.left_shift(jnp.ones((groups,), jnp.int32), long_power)
    long_length = jax.random.randint(key_list[2], (groups,), long_base, 2 * long_base)
    topmost = jax.random.randint(key_list[3], (), 0, groups)
    long_length = jnp.where(jnp.arange(groups) == topmost, MAXLEN, long_length)
    short_high = int(SHORT_MAX).bit_length() - 1
    short_power = jax.random.randint(key_list[4], (groups, REQ_DEV), 2, short_high)
    short_base = jnp.left_shift(jnp.ones((groups, REQ_DEV), jnp.int32), short_power)
    short_length = jax.random.randint(key_list[5], (groups, REQ_DEV), short_base, 2 * short_base)
    lengths = jnp.where(jnp.arange(REQ_DEV)[None, :] == long_slot[:, None], long_length[:, None], short_length)
    return lengths.reshape(REQUESTS).astype(jnp.int32)


def draw_page_table(key, part):
    groups = REQUESTS // REQ_DEV
    lengths = draw_cache_length(key, part).reshape(groups, REQ_DEV)
    page_count = (lengths + PAGE - 1) // PAGE
    lane_iota = jnp.arange(LANES, dtype=jnp.int32)
    on_device = jnp.maximum(page_count[:, :, None] - lane_iota[None, None, :] + LANES - 1, 0) // LANES
    offsets = jnp.cumsum(on_device, axis=1) - on_device
    scores = jax.random.randint(jax.random.fold_in(key, 23), (groups, LANES, PAGES_DEV), 0, 1 << 20) * PAGES_DEV + jnp.arange(PAGES_DEV, dtype=jnp.int32)
    shuffled = jnp.argsort(scores, axis=-1, stable=True).astype(jnp.int32)
    page_iota = jnp.arange(MAXPG_DEV, dtype=jnp.int32)
    wanted = (offsets[:, :, :, None] + page_iota) % PAGES_DEV
    spread = jnp.broadcast_to(shuffled[:, None], (groups, REQ_DEV, LANES, PAGES_DEV))
    page_slots = jnp.take_along_axis(spread, wanted, axis=-1)
    return page_slots.reshape(REQUESTS, LANES * MAXPG_DEV).astype(jnp.int32)


def draw_target_slot(key, part):
    groups = REQUESTS // REQ_DEV
    halfway = groups // 2
    key_list = jax.random.split(jax.random.fold_in(key, 37), 3)
    swapped = jax.random.randint(key_list[0], (halfway,), 0, 4) > 0
    slot_low = jax.random.randint(key_list[1], (halfway,), 0, REQ_DEV)
    slot_high = jax.random.randint(key_list[2], (halfway,), 0, REQ_DEV)
    pair_iota = jnp.arange(halfway, dtype=jnp.int32)
    first_slot = pair_iota * REQ_DEV + slot_low
    second_slot = (pair_iota + halfway) * REQ_DEV + slot_high
    identity = jnp.arange(REQUESTS, dtype=jnp.int32)
    target = identity.at[first_slot].set(jnp.where(swapped, second_slot, first_slot))
    target = target.at[second_slot].set(jnp.where(swapped, first_slot, second_slot))
    return target.astype(jnp.int32)


def draw_cache_pool(key, part):
    groups = REQUESTS // REQ_DEV
    pool_shape = (groups, LANES, PAGES_DEV, PAGE, 2 * KVW)
    key_list = jax.random.split(jax.random.fold_in(key, 53), 1)
    entries = jax.random.truncated_normal(key_list[0], -6.0, 6.0, pool_shape)
    return entries.astype(jnp.float32).astype(jnp.bfloat16)


def block_scale(own_key, shape, cuts, smallest, high):
    loudness = 1.0
    for dim, blocks in cuts:
        steps = jax.random.uniform(jax.random.fold_in(jax.random.fold_in(own_key, 6), dim), (blocks,), jnp.float32, smallest / len(cuts), high / len(cuts))
        loudness = loudness * jnp.repeat(jnp.exp(steps), shape[dim] // blocks).reshape((-1,) + (1,) * (len(shape) - 1 - dim))
    return loudness


def noise(own_key, dims, scale, limit, cuts=(), held_as=jnp.bfloat16):
    level = block_scale(own_key, dims, cuts, -0.22, 0.18) if cuts else 1.0
    array = jax.random.normal(own_key, dims, jnp.float32) * scale * level
    return jnp.minimum(jnp.maximum(array, -limit), limit).astype(held_as)


def setup_inputs(seed: int = 0) -> dict:
    seeds = jax.random.split(jax.random.key(seed), 8)
    return {
        "hidden": noise(seeds[0], (REQUESTS, STRETCH, D), 1.0, 6.0, ((0, 32), (1, 8))),
        "project_weight": noise(seeds[1], (D, 3 * KVW), D ** -0.5, 0.125, ((1, 256),)),
        "output_weight": noise(seeds[2], (KVW, D), (KVW // 16) ** -0.5, 0.75, ((1, 256),)),
        "cache_pool": draw_cache_pool(jax.random.fold_in(seeds[7], 71), 0),
        "page_table": draw_page_table(jax.random.fold_in(seeds[7], 71), 0),
        "cache_length": draw_cache_length(jax.random.fold_in(seeds[7], 71), 0),
        "target_slot": draw_target_slot(jax.random.fold_in(seeds[7], 71), 0),
    }


norm_epsilon = 1e-05
masked_score = -1e+30

def layer_norm(row_block):
    row_mean = lax.optimization_barrier(jnp.mean(row_block, axis=-1, keepdims=True))
    centred = row_block - row_mean
    variance = lax.optimization_barrier(jnp.mean(centred * centred, axis=-1, keepdims=True))
    return centred / jnp.sqrt(variance + norm_epsilon)

def rotate(head_block, positions):
    half_size = head_block.shape[-1] // 2
    frequency = jnp.exp(-math.log(10000.0) * 2.0 * jnp.arange(half_size, dtype=jnp.float32) / head_block.shape[-1])
    angles = positions.astype(jnp.float32)[..., None] * frequency
    cosine = jnp.cos(angles)
    sine_value = jnp.sin(angles)
    first_half = head_block[..., :half_size]
    second_half = head_block[..., half_size:]
    return jnp.concatenate([first_half * cosine - second_half * sine_value, second_half * cosine + first_half * sine_value], axis=-1)

def cache_rows(cache_pool, page_table, request, length, positions):
    group_index = request // REQ_DEV
    page_number = positions // PAGE
    lane_index = page_number % LANES
    local_page = page_number // LANES
    pool_slot = page_table[request][lane_index * MAXPG_DEV + local_page]
    row_block = cache_pool[group_index, lane_index, pool_slot, positions % PAGE]
    return jnp.where((positions < length)[:, None], row_block, jnp.zeros_like(row_block))

def reference(hidden, project_weight, output_weight, cache_pool, page_table, cache_length, target_slot):
    slot_iota = jnp.arange(REQUESTS, dtype=jnp.int32)
    source = jnp.zeros((REQUESTS,), jnp.int32).at[target_slot].set(slot_iota)
    moved_tokens = hidden[source]
    moved_len = cache_length[source]
    all_positions = jnp.arange(MAXLEN, dtype=jnp.int32)
    stretch_iota = jnp.arange(STRETCH, dtype=jnp.int32)
    score_scale = HEAD ** (-0.5)

    def attend_slot(inputs):
        token_rows, request, length = inputs
        normed = layer_norm(token_rows.astype(jnp.float32)).astype(jnp.bfloat16)
        projected = jnp.dot(normed, project_weight, preferred_element_type=jnp.float32).reshape(STRETCH, 3, HEADS, HEAD)
        positions = (length + stretch_iota)[:, None]
        queries = rotate(projected[:, 0], positions).astype(jnp.bfloat16)
        new_keys = rotate(projected[:, 1], positions).astype(jnp.bfloat16)
        new_values = projected[:, 2].astype(jnp.bfloat16)
        stored = cache_rows(cache_pool, page_table, request, length, all_positions)
        key_rows = jnp.concatenate([stored[:, :KVW].reshape(MAXLEN, HEADS, HEAD), new_keys], axis=0)
        value_rows = jnp.concatenate([stored[:, KVW:].reshape(MAXLEN, HEADS, HEAD), new_values], axis=0)
        cache_allowed = jnp.broadcast_to((all_positions < length)[None, :], (STRETCH, MAXLEN))
        allowed = jnp.concatenate([cache_allowed, stretch_iota[None, :] <= stretch_iota[:, None]], axis=1)
        scores = jnp.einsum('qhd,khd->hqk', queries.astype(jnp.float32), key_rows.astype(jnp.float32)) * score_scale
        scores = jnp.where(allowed[None], scores, masked_score)
        highest = lax.optimization_barrier(jnp.max(scores, axis=-1, keepdims=True))
        exponent = jnp.where(allowed[None], jnp.exp(scores - highest), 0.0)
        totals = lax.optimization_barrier(jnp.sum(exponent, axis=-1))
        lowered = lax.optimization_barrier(exponent.astype(jnp.bfloat16)).astype(jnp.float32)
        summed = jnp.einsum('hqk,khd->hqd', lowered, value_rows.astype(jnp.float32))
        attended = (summed / totals[:, :, None]).astype(jnp.bfloat16)
        attended = attended.transpose(1, 0, 2).reshape(STRETCH, KVW)
        return jnp.dot(attended, output_weight, preferred_element_type=jnp.float32).astype(jnp.bfloat16)
    attention_out = lax.map(attend_slot, (moved_tokens, source, moved_len))
    lane_rows = MAXPG_DEV * PAGE
    order_iota = jnp.arange(LANES * lane_rows, dtype=jnp.int32)
    lane_of_row = order_iota // lane_rows
    rest_rows = order_iota % lane_rows
    lane_positions = (rest_rows // PAGE * LANES + lane_of_row) * PAGE + rest_rows % PAGE
    member_iota = jnp.arange(REQ_DEV, dtype=jnp.int32)

    def arrive_group(group_index):
        slots = group_index * REQ_DEV + member_iota
        came = (source[slots] // REQ_DEV != group_index).astype(jnp.int32)
        chosen = group_index * REQ_DEV + jnp.sum(came * member_iota)
        row_block = cache_rows(cache_pool, page_table, source[chosen], cache_length[source[chosen]], lane_positions)
        return jnp.where(jnp.sum(came) > 0, row_block, jnp.zeros_like(row_block))
    arrived_cache = lax.map(arrive_group, jnp.arange(N_REQ, dtype=jnp.int32))
    return (attention_out, arrived_cache)
```

```python
import functools
import math

import jax
import jax.numpy as jnp
from jax import lax
from jax.experimental import pallas as pl
from jax.experimental.pallas import tpu as pltpu
from jax.sharding import PartitionSpec as P

HEAD = 128
HEADS = 8
MESH = pl.DeviceIdType.MESH
EPSILON = 1e-05
MASKED = -1e30
VMEM = pl.BlockSpec(memory_space=pltpu.VMEM)
DMA = pltpu.SemaphoreType.DMA


def place():
    req = lax.axis_index("req")
    seq = lax.axis_index("seq")
    return req, seq


def meet(devices):
    barrier = pltpu.get_barrier_semaphore()
    for req, seq in devices:
        pl.semaphore_signal(barrier, inc=1, device_id=(req, seq), device_id_type=MESH)
    pl.semaphore_wait(barrier, len(devices))


def remote(src, dst, send, recv, req, seq):
    return pltpu.make_async_remote_copy(
        src_ref=src, dst_ref=dst, send_sem=send, recv_sem=recv,
        device_id=(req, seq), device_id_type=MESH,
    )


def landed(dst, sem):
    pltpu.make_async_copy(dst, dst, sem).wait()


def spread(own, out, req, seq, send, recv):
    zh, c = seq // 2, seq % 2
    other = 2 * zh + 1 - c
    copies = []
    for dz in (2, 1, 3):
        copies.append(remote(own, out.at[seq], send.at[dz - 1], recv.at[seq], req, (zh + dz) % 4 * 2 + c))
    copies.append(remote(own, out.at[seq], send.at[3], recv.at[seq], req, other))
    for copy in copies:
        copy.start()
    kept = pltpu.make_async_copy(own, out.at[seq], recv.at[seq])
    kept.start()
    return copies


def pass_on(out, req, seq, send, recv):
    zh, c = seq // 2, seq % 2
    other = 2 * zh + 1 - c
    copies = []
    for dz in (1, 3, 2):
        source = (zh + dz) % 4 * 2 + c
        landed(out.at[source], recv.at[source])
        copy = remote(out.at[source], out.at[source], send.at[3 + dz], recv.at[source], req, other)
        copy.start()
        copies.append(copy)
    landed(out.at[seq], recv.at[seq])
    for dz in range(4):
        source = (zh + dz) % 4 * 2 + 1 - c
        landed(out.at[source], recv.at[source])
    return copies


def gather_kernel(
    piece, tok, w, toks, ybuf, y_send, y_recv, z_send, z_recv, x_send, x_recv, t_send, t_recv
):
    req, seq = place()
    y, x, zl = req // 8, req // 2 % 4, req % 2
    zh, c = seq // 2, seq % 2
    line = zl * 8 + seq
    base = y * 8 + x * 2
    partners = [((req + 8 * dy) % 32, seq) for dy in (1, 2, 3)]
    partners += [(y * 8 + (x + dx) % 4 * 2 + zl, seq) for dx in (1, 2, 3)]
    for k in range(1, 16):
        there = (line + k) % 16
        partners.append((base + there // 8, there % 8))
    meet(partners)

    sends = []
    for dy in (2, 1, 3):
        copy = remote(piece, ybuf.at[y], y_send.at[dy - 1], y_recv.at[y], (req + 8 * dy) % 32, seq)
        copy.start()
        sends.append(copy)
    kept = pltpu.make_async_copy(piece, ybuf.at[y], y_recv.at[y])
    kept.start()
    sends += spread(tok, toks, req, seq, t_send, t_recv)

    half = x % 2
    core = x // 2
    slot = half * 16 + line
    for dy in range(4):
        yy = (y + dy) % 4
        landed(ybuf.at[yy], y_recv.at[yy])
        target = yy * 2 + core
        for b in range(2):
            there = base + (zl + b) % 2
            copy = remote(
                ybuf.at[yy], w.at[slot], z_send.at[dy * 2 + b], z_recv.at[line], there, target
            )
            if b == 1:
                copy.start()
                sends.append(copy)
            else:

                @pl.when(target == seq)
                def _():
                    pltpu.make_async_copy(ybuf.at[yy], w.at[slot], z_recv.at[line]).start()

                @pl.when(target != seq)
                def _():
                    copy.start()

    sends += pass_on(toks, req, seq, t_send, t_recv)

    @pl.when(c == core)
    def _():
        for k in range(4):
            for n in range(4):
                landed(w.at[half * 16 + 4 * k + n], z_recv.at[4 * k + n])
            block = w.at[pl.ds(half * 16 + 4 * k, 4)]
            for dx in (2, 1, 3):
                remote(
                    block, block, x_send.at[(dx - 1) * 4 + k], x_recv.at[half * 4 + k],
                    y * 8 + (x + dx) % 4 * 2 + zl, seq,
                ).start()

    for h in range(2):

        @pl.when(2 * c + h != x)
        def _():
            for k in range(4):
                landed(w.at[pl.ds(h * 16 + 4 * k, 4)], x_recv.at[h * 4 + k])

    for copy in sends:
        copy.wait_send()
    for dy in range(4):
        yy = (y + dy) % 4

        @pl.when(yy * 2 + core != seq)
        def _():
            remote(
                ybuf.at[yy], w.at[slot], z_send.at[dy * 2], z_recv.at[line], req, yy * 2 + core
            ).wait_send()

    @pl.when(c == core)
    def _():
        for k in range(4):
            block = w.at[pl.ds(half * 16 + 4 * k, 4)]
            for dx in (2, 1, 3):
                remote(
                    block, block, x_send.at[(dx - 1) * 4 + k], x_recv.at[half * 4 + k],
                    y * 8 + (x + dx) % 4 * 2 + zl, seq,
                ).wait_send()


def seq_partners(req, seq):
    return [(req, (seq + dp) % 8) for dp in range(1, 8)]


def qkv_kernel(qkv, q, kv, q_send, f_send, q_recv, kv_send, kv_recv):
    req, seq = place()
    zh, c = seq // 2, seq % 2
    other = 2 * zh + 1 - c
    meet(seq_partners(req, seq))

    def q_copies(j, head):
        copies = [
            remote(qkv.at[j], q.at[head], q_send.at[j * 4 + dz - 1], q_recv.at[head], req, (zh + dz) % 4 * 2 + c)
            for dz in (2, 1, 3)
        ]
        return copies + [remote(qkv.at[j], q.at[head], q_send.at[j * 4 + 3], q_recv.at[head], req, other)]

    def kv_copies(j, slot):
        copies = []
        for dp in range(1, 8):
            p = (seq + dp) % 8
            rows = pl.ds(pl.multiple_of(32 * p, 32), 32)
            copies.append(
                remote(qkv.at[j, rows], kv.at[slot], kv_send.at[j * 7 + dp - 1], kv_recv.at[slot], req, p)
            )
        return copies

    for j in range(3):
        slot = 3 * seq + j

        @pl.when(slot < HEADS)
        def _():
            for copy in q_copies(j, slot):
                copy.start()
            pltpu.make_async_copy(qkv.at[j], q.at[slot], q_recv.at[slot]).start()

        @pl.when(slot >= HEADS)
        def _():
            for copy in kv_copies(j, slot - HEADS):
                copy.start()
            rows = pl.ds(pl.multiple_of(32 * seq, 32), 32)
            pltpu.make_async_copy(qkv.at[j, rows], kv.at[slot - HEADS], kv_recv.at[slot - HEADS]).start()

    for head in range(HEADS):
        owner = head // 3
        landed(q.at[head], q_recv.at[head])

        @pl.when((c == owner % 2) & (zh != owner // 2))
        def _():
            remote(q.at[head], q.at[head], f_send.at[head], q_recv.at[head], req, other).start()

    for slot in range(2 * HEADS):
        landed(kv.at[slot], kv_recv.at[slot])

    for j in range(3):
        slot = 3 * seq + j

        @pl.when(slot < HEADS)
        def _():
            for copy in q_copies(j, slot):
                copy.wait_send()

        @pl.when(slot >= HEADS)
        def _():
            for copy in kv_copies(j, slot - HEADS):
                copy.wait_send()

    for head in range(HEADS):
        owner = head // 3

        @pl.when((c == owner % 2) & (zh != owner // 2))
        def _():
            remote(q.at[head], q.at[head], f_send.at[head], q_recv.at[head], req, other).wait_send()


def deal_kernel(o, ml, o_all, ml_all, o_send, o_recv, ml_send, ml_recv):
    req, seq = place()
    meet(seq_partners(req, seq))
    copies = []
    for dp in (4, 3, 5, 2, 6, 1, 7):
        p = (seq + dp) % 8
        copies.append(remote(ml.at[p], ml_all.at[seq], ml_send.at[dp - 1], ml_recv.at[seq], req, p))
        copies.append(remote(o.at[p], o_all.at[seq], o_send.at[dp - 1], o_recv.at[seq], req, p))
    for copy in copies:
        copy.start()
    pltpu.make_async_copy(o.at[seq], o_all.at[seq], o_recv.at[seq]).start()
    pltpu.make_async_copy(ml.at[seq], ml_all.at[seq], ml_recv.at[seq]).start()
    for lane in range(8):
        landed(o_all.at[lane], o_recv.at[lane])
        landed(ml_all.at[lane], ml_recv.at[lane])
    for copy in copies:
        copy.wait_send()


def attended_kernel(own, out, send, recv):
    req, seq = place()
    meet(seq_partners(req, seq))
    copies = spread(own, out, req, seq, send, recv)
    copies += pass_on(out, req, seq, send, recv)
    for copy in copies:
        copy.wait_send()


def out_kernel(out, here, there, h_send, h_recv, t_send, t_recv):
    req, seq = place()
    far = (req + 16) % 32
    meet(seq_partners(req, seq) + [(far, (seq + dp) % 8) for dp in range(8)])
    columns = pl.ds(pl.multiple_of(256 * seq, 256), 256)
    copies = []
    for dp in (4, 3, 5, 2, 6, 1, 7, 0):
        p = (seq + dp) % 8
        rows = pl.ds(pl.multiple_of(32 * p, 32), 32)
        copies.append(remote(out.at[rows], there.at[:, columns], t_send.at[dp], t_recv.at[seq], far, p))
        if dp:
            copies.append(remote(out.at[rows], here.at[:, columns], h_send.at[dp], h_recv.at[seq], req, p))
    for copy in copies:
        copy.start()
    rows = pl.ds(pl.multiple_of(32 * seq, 32), 32)
    pltpu.make_async_copy(out.at[rows], here.at[:, columns], h_recv.at[seq]).start()
    for lane in range(8):
        columns = pl.ds(256 * lane, 256)
        landed(here.at[:, columns], h_recv.at[lane])
        landed(there.at[:, columns], t_recv.at[lane])
    for copy in copies:
        copy.wait_send()


def pages_kernel(table, limit, page, out):
    j = pl.program_id(0)
    left = limit[j]
    row = lax.broadcasted_iota(jnp.int32, (128, 2048), 0)
    out[0] = jnp.where(row < left, page[0], jnp.zeros_like(page[0]))


def attention_kernel(q, k, v, kn, vn, bias, fresh, o, ml):
    across = (((1,), (1,)), ((), ()))
    down = (((0,), (0,)), ((), ()))
    scale = HEAD ** (-0.5)
    s = lax.dot_general(k[...], q[0], across, preferred_element_type=jnp.float32) * scale + bias[...]
    sn = lax.dot_general(kn[0], q[0], across, preferred_element_type=jnp.float32) * scale + fresh[...]
    highest = jnp.maximum(jnp.max(s, axis=0, keepdims=True), jnp.max(sn, axis=0, keepdims=True))
    p = jnp.exp(s - highest)
    pn = jnp.exp(sn - highest)
    totals = jnp.sum(p, axis=0, keepdims=True) + jnp.sum(pn, axis=0, keepdims=True)
    summed = lax.dot_general(v[...], p.astype(jnp.bfloat16), down, preferred_element_type=jnp.float32)
    summed += lax.dot_general(vn[0], pn.astype(jnp.bfloat16), down, preferred_element_type=jnp.float32)
    o[0] = summed.astype(jnp.bfloat16)
    ml[0] = jnp.concatenate([highest, totals, jnp.zeros((6, 256), jnp.float32)], axis=0)


def shape(dims, dtype=jnp.bfloat16):
    return jax.ShapeDtypeStruct(dims, dtype)


def exchange(kernel, number, outs, scratch, *operands):
    return pl.pallas_call(
        kernel,
        out_shape=outs,
        in_specs=[VMEM] * len(operands),
        out_specs=jax.tree.map(lambda _: VMEM, outs),
        scratch_shapes=scratch,
        compiler_params=pltpu.CompilerParams(collective_id=number, has_side_effects=True),
    )(*operands)


def layer_norm(row_block):
    row_mean = jnp.mean(row_block, axis=-1, keepdims=True)
    centred = row_block - row_mean
    variance = jnp.mean(centred * centred, axis=-1, keepdims=True)
    return centred / jnp.sqrt(variance + EPSILON)


def local(hidden, project_weight, output_weight, cache_pool, page_table, cache_length, target_slot):
    req, seq = place()
    length = cache_length[req]
    leaving = target_slot[req] != req
    pool = cache_pool.reshape(8, 128, 2048)
    table = page_table[0]
    page_start = (jnp.arange(8, dtype=jnp.int32) * 8 + seq) * 128

    limit = jnp.where(leaving, length, 0) - page_start
    outgoing = pl.pallas_call(
        pages_kernel,
        out_shape=shape((8, 128, 2048)),
        grid_spec=pltpu.PrefetchScalarGridSpec(
            num_scalar_prefetch=2,
            grid=(8,),
            in_specs=[pl.BlockSpec((1, 128, 2048), lambda j, table, limit: (table[j], 0, 0))],
            out_specs=pl.BlockSpec((1, 128, 2048), lambda j, table, limit: (j, 0, 0)),
        ),
        name="pages",
    )(table, limit, pool)

    normed = layer_norm(hidden[0].astype(jnp.float32)).astype(jnp.bfloat16)
    piece = jnp.concatenate([project_weight.T, output_weight.T.reshape(4, 2048)], axis=0)
    outgoing, normed, piece = lax.optimization_barrier((outgoing, normed, piece))
    arrived = lax.ppermute(outgoing, "req", [(i, (i + 16) % 32) for i in range(32)])

    w, tokens = exchange(
        gather_kernel, 1, (shape((32, 16, 2048)), shape((8, 32, 2048))),
        [pltpu.VMEM((4, 16, 2048), jnp.bfloat16), DMA((3,)), DMA((4,)), DMA((8,)), DMA((16,)),
         DMA((12,)), DMA((8,)), DMA((7,)), DMA((8,))],
        piece, normed,
    )
    columns = w[:, :12].reshape(384, 2048)
    projected = lax.dot_general(
        tokens.reshape(256, 2048), columns, (((1,), (1,)), ((), ())), preferred_element_type=jnp.float32
    )
    query_iota = jnp.arange(256, dtype=jnp.int32)
    frequency = jnp.exp(-math.log(10000.0) * 2.0 * jnp.arange(64, dtype=jnp.float32) / HEAD)
    angles = (length + query_iota).astype(jnp.float32)[:, None] * frequency
    cosine, sine = jnp.cos(angles), jnp.sin(angles)
    blocks = []
    for j in range(3):
        block = projected[:, j * HEAD : (j + 1) * HEAD]
        u, v = block[:, :64], block[:, 64:]
        turned = jnp.concatenate([u * cosine - v * sine, v * cosine + u * sine], axis=-1)
        blocks.append(jnp.where(3 * seq + j < 2 * HEADS, turned, block))
    qkv = jnp.stack(blocks).astype(jnp.bfloat16)

    q, kv = exchange(
        qkv_kernel, 2, (shape((8, 256, 128)), shape((16, 32, 128))),
        [DMA((12,)), DMA((8,)), DMA((8,)), DMA((21,)), DMA((16,))],
        qkv,
    )

    row = jnp.arange(128, dtype=jnp.int32)
    held = (table[None, :] == jnp.arange(8, dtype=jnp.int32)[:, None])[:, :, None] & (
        (page_start[:, None] + row[None, :] < length)[None]
    )
    bias = jnp.where(jnp.any(held, axis=1), 0.0, MASKED).astype(jnp.float32).reshape(1024, 1)
    key_token = seq * 32 + jnp.arange(32, dtype=jnp.int32)
    fresh = jnp.where(key_token[:, None] <= query_iota[None, :], 0.0, MASKED).astype(jnp.float32)
    rows = pool.reshape(1024, 2048)
    o, ml = pl.pallas_call(
        attention_kernel,
        out_shape=(shape((8, 128, 256)), shape((8, 8, 256), jnp.float32)),
        grid=(8,),
        in_specs=[
            pl.BlockSpec((1, 256, 128), lambda h: (h, 0, 0)),
            pl.BlockSpec((1024, 128), lambda h: (0, h)),
            pl.BlockSpec((1024, 128), lambda h: (0, h + 8)),
            pl.BlockSpec((1, 32, 128), lambda h: (h, 0, 0)),
            pl.BlockSpec((1, 32, 128), lambda h: (h + 8, 0, 0)),
            pl.BlockSpec((1024, 1), lambda h: (0, 0)),
            pl.BlockSpec((32, 256), lambda h: (0, 0)),
        ],
        out_specs=(
            pl.BlockSpec((1, 128, 256), lambda h: (h, 0, 0)),
            pl.BlockSpec((1, 8, 256), lambda h: (h, 0, 0)),
        ),
        name="attention",
    )(q, rows, rows, kv, kv, bias, fresh)

    o_all, ml_all = exchange(
        deal_kernel, 3, (shape((8, 128, 256)), shape((8, 8, 256), jnp.float32)),
        [DMA((7,)), DMA((8,)), DMA((7,)), DMA((8,))],
        o, ml,
    )
    highest, totals = ml_all[:, 0], ml_all[:, 1]
    weight = jnp.exp(highest - jnp.max(highest, axis=0, keepdims=True))
    total = jnp.sum(weight * totals, axis=0)
    summed = jnp.sum(weight[:, None, :] * o_all.astype(jnp.float32), axis=0)
    attended = (summed / total[None, :]).astype(jnp.bfloat16)
    attended_all = exchange(attended_kernel, 4, shape((8, 128, 256)), [DMA((7,)), DMA((8,))], attended)
    out_columns = w[:, 12:].reshape(256, 1024)
    out = lax.dot_general(
        attended_all.reshape(1024, 256), out_columns, (((0,), (1,)), ((), ())),
        preferred_element_type=jnp.float32,
    ).astype(jnp.bfloat16)
    here, there = exchange(
        out_kernel, 5, (shape((32, 2048)), shape((32, 2048))),
        [DMA((8,)), DMA((8,)), DMA((8,)), DMA((8,))],
        out,
    )
    attention_out = jnp.where(leaving, there, here)
    return attention_out[None], arrived.reshape(1, 1024, 2048)


def solution(mesh):
    placed = (
        P("req", "seq", None),
        P(None, ("req", "seq")),
        P(None, ("req", "seq")),
        P("req", "seq", None, None, None),
        P("req", "seq"),
        P(),
        P(),
    )
    return jax.shard_map(
        local,
        mesh=mesh,
        in_specs=placed,
        out_specs=(P("req", "seq", None), P("req", "seq", None)),
        check_vma=False,
    )
```

```python
import functools
import math

import jax
import jax.numpy as jnp
from jax import lax
from jax.experimental import pallas as pl
from jax.experimental.pallas import tpu as pltpu
from jax.sharding import PartitionSpec as P

HEAD = 128
HEADS = 8
MESH = pl.DeviceIdType.MESH
EPSILON = 1e-05
MASKED = -1e30
VMEM = pl.BlockSpec(memory_space=pltpu.VMEM)
DMA = pltpu.SemaphoreType.DMA


def place():
    return lax.axis_index("req"), lax.axis_index("seq")


def greet(devices):
    barrier = pltpu.get_barrier_semaphore()
    for req, seq in devices:
        pl.semaphore_signal(barrier, inc=1, device_id=(req, seq), device_id_type=MESH)
    return lambda: pl.semaphore_wait(barrier, len(devices))


def remote(src, dst, send, recv, req, seq):
    return pltpu.make_async_remote_copy(
        src_ref=src, dst_ref=dst, send_sem=send, recv_sem=recv,
        device_id=(req, seq), device_id_type=MESH,
    )


def landed(dst, sem):
    pltpu.make_async_copy(dst, dst, sem).wait()


def begin(copies):
    for copy in copies:
        copy.start()
    return copies


def finish(copies):
    for copy in copies:
        copy.wait_send()


def spread(own, out, req, seq, send, recv):
    zh, c = seq // 2, seq % 2
    copies = [
        remote(own, out.at[seq], send.at[dz - 1], recv.at[seq], req, (zh + dz) % 4 * 2 + c)
        for dz in (2, 1, 3)
    ]
    copies.append(remote(own, out.at[seq], send.at[3], recv.at[seq], req, 2 * zh + 1 - c))
    begin(copies)
    pltpu.make_async_copy(own, out.at[seq], recv.at[seq]).start()
    return copies


def pass_on(out, req, seq, send, recv):
    zh, c = seq // 2, seq % 2
    copies = []
    for dz in (1, 3, 2):
        source = (zh + dz) % 4 * 2 + c
        landed(out.at[source], recv.at[source])
        copies += begin(
            [remote(out.at[source], out.at[source], send.at[3 + dz], recv.at[source], req, 2 * zh + 1 - c)]
        )
    for dz in (0, 1, 3, 2):
        source = (zh + dz) % 4 * 2 + 1 - c
        landed(out.at[source], recv.at[source])
    landed(out.at[seq], recv.at[seq])
    return copies


class Weights:
    def __init__(self, pieces, w, z_send, z_recv, x_send, x_recv):
        self.pieces, self.w = pieces, w
        self.z_send, self.z_recv, self.x_send, self.x_recv = z_send, z_recv, x_send, x_recv
        self.req, self.seq = req, seq = place()
        self.y, self.x, self.zl, self.c = req // 8, req // 2 % 4, req % 2, seq % 2
        self.line = self.zl * 8 + seq
        self.slot = self.x % 2 * 16 + self.line

    def partners(self):
        found = [(self.y * 8 + (self.x + dx) % 4 * 2 + self.zl, self.seq) for dx in (1, 2, 3)]
        for k in range(1, 16):
            there = (self.line + k) % 16
            found.append((self.y * 8 + self.x * 2 + there // 8, there % 8))
        return found

    def piece(self, d):
        return self.pieces.at[(self.y - d) % 4]

    def z_copy(self, d, b):
        target = (self.y - d) % 4 * 2 + self.x // 2
        there = self.y * 8 + self.x * 2 + (self.zl + b) % 2
        copy = remote(
            self.piece(d), self.w.at[self.slot], self.z_send.at[d * 2 + b], self.z_recv.at[self.line], there, target
        )
        return copy, target

    def along_z(self):
        for d in (2, 1, 3, 0):
            self.z_copy(d, 1)[0].start()
            copy, target = self.z_copy(d, 0)

            @pl.when(target == self.seq)
            def _():
                pltpu.make_async_copy(self.piece(d), self.w.at[self.slot], self.z_recv.at[self.line]).start()

            @pl.when(target != self.seq)
            def _():
                copy.start()

    def x_copy(self, h, k, step):
        block = self.w.at[pl.ds(h * 16 + 4 * k, 4)]
        there = self.y * 8 + (self.x + step) % 4 * 2 + self.zl
        return remote(block, block, self.x_send.at[(step + 1) // 2 * 8 + h * 4 + k], self.x_recv.at[h * 4 + k], there, self.seq)

    def arrived(self, h, k):
        landed(self.w.at[pl.ds(h * 16 + 4 * k, 4)], self.x_recv.at[h * 4 + k])

    def along_x(self):
        for h in range(2):

            @pl.when((self.x - 2 * self.c - h) % 4 == 0)
            def _():
                for k in range(4):
                    for n in range(4):
                        landed(self.w.at[h * 16 + 4 * k + n], self.z_recv.at[4 * k + n])
                    self.x_copy(h, k, 1).start()
                    self.x_copy(h, k, -1).start()

        for k in range(4):
            step = 1 if k % 2 == 0 else -1
            for h in range(2):
                hops = (self.x - 2 * self.c - h) % 4

                @pl.when((hops == 1) | (hops == 3))
                def _():
                    self.arrived(h, k)

                @pl.when(hops == step % 4)
                def _():
                    self.x_copy(h, k, step).start()

        for h in range(2):

            @pl.when((self.x - 2 * self.c - h) % 4 == 2)
            def _():
                for k in range(4):
                    self.arrived(h, k)

    def finish(self):
        for d in range(4):
            self.z_copy(d, 1)[0].wait_send()
            copy, target = self.z_copy(d, 0)

            @pl.when(target != self.seq)
            def _():
                copy.wait_send()

        for h in range(2):
            hops = (self.x - 2 * self.c - h) % 4
            for k in range(4):
                step = 1 if k % 2 == 0 else -1

                @pl.when((hops == 0) | (hops == step % 4))
                def _():
                    self.x_copy(h, k, step).wait_send()

                @pl.when(hops == 0)
                def _():
                    self.x_copy(h, k, -step).wait_send()


WEIGHT_SEMS = [DMA((8,)), DMA((16,)), DMA((16,)), DMA((8,))]


def layer_norm(row_block):
    row_mean = jnp.mean(row_block, axis=-1, keepdims=True)
    centred = row_block - row_mean
    variance = jnp.mean(centred * centred, axis=-1, keepdims=True)
    return centred / jnp.sqrt(variance + EPSILON)


def rows_kernel(own, out_own, hidden, pieces, out_pieces, normed, send, recv, out_send, out_recv):
    req, seq = place()
    y = req // 8
    met = greet([((req + 8 * d) % 32, seq) for d in (1, 2, 3)])
    met()
    copies = []
    for d in (2, 1, 3):
        there = (req + 8 * d) % 32
        copies.append(remote(own, pieces.at[y], send.at[d - 1], recv.at[y], there, seq))
        copies.append(remote(out_own, out_pieces.at[y], out_send.at[d - 1], out_recv.at[y], there, seq))
    begin(copies)
    pltpu.make_async_copy(own, pieces.at[y], recv.at[y]).start()
    pltpu.make_async_copy(out_own, out_pieces.at[y], out_recv.at[y]).start()
    normed[...] = layer_norm(hidden[...].astype(jnp.float32)).astype(jnp.bfloat16)
    for d in range(4):
        landed(pieces.at[d], recv.at[d])
        landed(out_pieces.at[d], out_recv.at[d])
    finish(copies)


def gather_kernel(pieces, normed, w, toks, *sems):
    req, seq = place()
    weights = Weights(pieces, w, *sems[:4])
    t_send, t_recv = sems[4:]
    greet(weights.partners())()
    weights.along_z()
    copies = spread(normed, toks, req, seq, t_send, t_recv)
    weights.along_x()
    copies += pass_on(toks, req, seq, t_send, t_recv)
    finish(copies)
    weights.finish()


def attend_kernel(
    qkv, pool, bias, fresh, pieces, here, there,
    wo, rows, q, kv, o, ml, o_all, ml_all, own, att, out, pool_sem,
    q_send, f_send, q_recv, kv_send, kv_recv, o_send, o_recv, ml_send, ml_recv,
    a_send, a_recv, h_send, h_recv, t_send, t_recv, *weight_sems,
):
    req, seq = place()
    zh, c = seq // 2, seq % 2
    other = 2 * zh + 1 - c
    far = (req + 16) % 32
    weights = Weights(pieces, wo, *weight_sems)
    met = greet(weights.partners() + [(far, (seq + dp) % 8) for dp in range(8)])
    loading = pltpu.make_async_copy(pool, rows, pool_sem)
    loading.start()
    met()

    def q_copies(j, head):
        copies = [
            remote(qkv.at[j], q.at[head], q_send.at[j * 4 + dz - 1], q_recv.at[head], req, (zh + dz) % 4 * 2 + c)
            for dz in (2, 1, 3)
        ]
        return copies + [remote(qkv.at[j], q.at[head], q_send.at[j * 4 + 3], q_recv.at[head], req, other)]

    def kv_copies(j, slot):
        copies = []
        for dp in range(1, 8):
            p = (seq + dp) % 8
            part = pl.ds(pl.multiple_of(32 * p, 32), 32)
            copies.append(
                remote(qkv.at[j, part], kv.at[slot], kv_send.at[j * 7 + dp - 1], kv_recv.at[slot], req, p)
            )
        return copies

    for j in range(3):
        slot = 3 * seq + j

        @pl.when(slot < HEADS)
        def _():
            begin(q_copies(j, slot))
            pltpu.make_async_copy(qkv.at[j], q.at[slot], q_recv.at[slot]).start()

        @pl.when(slot >= HEADS)
        def _():
            begin(kv_copies(j, slot - HEADS))
            part = pl.ds(pl.multiple_of(32 * seq, 32), 32)
            pltpu.make_async_copy(qkv.at[j, part], kv.at[slot - HEADS], kv_recv.at[slot - HEADS]).start()

    weights.along_z()
    loading.wait()

    def head_of(k):
        return k % 3 * 3 + k // 3

    def forward(head):
        return remote(q.at[head], q.at[head], f_send.at[head], q_recv.at[head], req, other)

    def passes(head):
        owner = head // 3
        return (c == owner % 2) & (zh != owner // 2)

    def o_copies(head):
        return [
            remote(ml.at[head], ml_all.at[seq], ml_send.at[head], ml_recv.at[seq], req, head),
            remote(o.at[head], o_all.at[seq], o_send.at[head], o_recv.at[seq], req, head),
        ]

    def deal(head):
        @pl.when(head == seq)
        def _():
            pltpu.make_async_copy(ml.at[head], ml_all.at[seq], ml_recv.at[seq]).start()
            pltpu.make_async_copy(o.at[head], o_all.at[seq], o_recv.at[seq]).start()

        @pl.when(head != seq)
        def _():
            begin(o_copies(head))

    across = (((1,), (1,)), ((), ()))
    down = (((0,), (0,)), ((), ()))
    scale = HEAD ** (-0.5)

    def attend(k, _):
        head = head_of(k)
        landed(q.at[head], q_recv.at[head])

        @pl.when(passes(head))
        def _():
            forward(head).start()

        landed(kv.at[head], kv_recv.at[head])
        landed(kv.at[head + 8], kv_recv.at[head + 8])
        keys = rows[:, pl.ds(pl.multiple_of(head * 128, 128), 128)]
        values = rows[:, pl.ds(pl.multiple_of(head * 128 + 1024, 128), 128)]
        query = q[head]
        s = lax.dot_general(keys, query, across, preferred_element_type=jnp.float32) * scale + bias[...]
        sn = lax.dot_general(kv[head], query, across, preferred_element_type=jnp.float32) * scale + fresh[...]
        highest = jnp.maximum(jnp.max(s, axis=0, keepdims=True), jnp.max(sn, axis=0, keepdims=True))
        p = jnp.exp(s - highest)
        pn = jnp.exp(sn - highest)
        totals = jnp.sum(p, axis=0, keepdims=True) + jnp.sum(pn, axis=0, keepdims=True)
        summed = lax.dot_general(values, p.astype(jnp.bfloat16), down, preferred_element_type=jnp.float32)
        summed += lax.dot_general(kv[head + 8], pn.astype(jnp.bfloat16), down, preferred_element_type=jnp.float32)
        o[head] = summed.astype(jnp.bfloat16)
        ml[head] = jnp.concatenate([highest, totals, jnp.zeros((6, 256), jnp.float32)], axis=0)

        @pl.when(k > 0)
        def _():
            deal(head_of(k - 1))

        return 0

    lax.fori_loop(0, HEADS, attend, 0)
    weights.along_x()
    deal(head_of(7))

    for lane in range(8):
        landed(ml_all.at[lane], ml_recv.at[lane])
    top = ml_all[0, 0:1]
    for lane in range(1, 8):
        top = jnp.maximum(top, ml_all[lane, 0:1])
    summed = jnp.zeros((128, 256), jnp.float32)
    total = jnp.zeros((1, 256), jnp.float32)
    for lane in range(8):
        landed(o_all.at[lane], o_recv.at[lane])
        factor = jnp.exp(ml_all[lane, 0:1] - top)
        total += factor * ml_all[lane, 1:2]
        summed += factor * o_all[lane].astype(jnp.float32)
    own[...] = (summed / total).astype(jnp.bfloat16)
    for head in range(HEADS):
        @pl.when(passes(head))
        def _():
            forward(head).wait_send()

        @pl.when(head != seq)
        def _():
            finish(o_copies(head))

    copies = spread(own, att, req, seq, a_send, a_recv)
    copies += pass_on(att, req, seq, a_send, a_recv)

    columns = wo[...].reshape(256, 1024)
    out[...] = lax.dot_general(
        att[...].reshape(1024, 256), columns, (((0,), (1,)), ((), ())), preferred_element_type=jnp.float32
    ).astype(jnp.bfloat16)
    finish(copies)
    for j in range(3):
        slot = 3 * seq + j

        @pl.when(slot < HEADS)
        def _():
            finish(q_copies(j, slot))

        @pl.when(slot >= HEADS)
        def _():
            finish(kv_copies(j, slot - HEADS))

    weights.finish()

    mine = pl.ds(pl.multiple_of(256 * seq, 256), 256)
    copies = []
    for dp in (4, 3, 5, 2, 6, 1, 7, 0):
        p = (seq + dp) % 8
        part = pl.ds(pl.multiple_of(32 * p, 32), 32)
        copies.append(remote(out.at[part], there.at[:, mine], t_send.at[dp], t_recv.at[seq], far, p))
        if dp:
            copies.append(remote(out.at[part], here.at[:, mine], h_send.at[dp], h_recv.at[seq], req, p))
    begin(copies)
    part = pl.ds(pl.multiple_of(32 * seq, 32), 32)
    pltpu.make_async_copy(out.at[part], here.at[:, mine], h_recv.at[seq]).start()
    for lane in range(8):
        theirs = pl.ds(256 * lane, 256)
        landed(here.at[:, theirs], h_recv.at[lane])
        landed(there.at[:, theirs], t_recv.at[lane])
    finish(copies)


def pages_kernel(table, lengths, targets, pool, out, buf, read_sem, write_sem):
    req, seq = place()
    length = jnp.where(targets[req] != req, lengths[req], 0)
    for j in range(8):

        @pl.when(length > (j * 8 + seq) * 128)
        def _():
            pltpu.make_async_copy(pool.at[table[0, j]], buf.at[j], read_sem.at[j]).start()

    for j in range(8):
        left = length - (j * 8 + seq) * 128

        @pl.when(left > 0)
        def _():
            pltpu.make_async_copy(pool.at[0], buf.at[j], read_sem.at[j]).wait()

        @pl.when((left > 0) & (left < 128))
        def _():
            row = lax.broadcasted_iota(jnp.int32, (128, 2048), 0)
            buf[j] = jnp.where(row < left, buf[j], jnp.zeros((128, 2048), jnp.bfloat16))

        @pl.when(left <= 0)
        def _():
            buf[j] = jnp.zeros((128, 2048), jnp.bfloat16)

        pltpu.make_async_copy(buf.at[j], out.at[j], write_sem.at[j]).start()
    for j in range(8):
        pltpu.make_async_copy(buf.at[j], out.at[j], write_sem.at[j]).wait()


def shape(dims, dtype=jnp.bfloat16):
    return jax.ShapeDtypeStruct(dims, dtype)


def vmem(*dims, dtype=jnp.bfloat16):
    return pltpu.VMEM(dims, dtype)


def exchange(kernel, number, outs, scratch, *operands, specs=None):
    return pl.pallas_call(
        kernel,
        out_shape=outs,
        in_specs=specs or [VMEM] * len(operands),
        out_specs=jax.tree.map(lambda _: VMEM, outs),
        scratch_shapes=scratch,
        compiler_params=pltpu.CompilerParams(collective_id=number, has_side_effects=True),
    )(*operands)


def local(hidden, project_weight, output_weight, cache_pool, page_table, cache_length, target_slot):
    req, seq = place()
    pool = cache_pool.reshape(8, 128, 2048)
    table = page_table[0]

    pieces, out_pieces, normed = exchange(
        rows_kernel, 3, (shape((4, 12, 2048)), shape((4, 8, 1024)), shape((32, 2048))),
        [DMA((3,)), DMA((4,)), DMA((3,)), DMA((4,))],
        project_weight.T, output_weight.T, hidden[0],
    )
    outgoing = pl.pallas_call(
        pages_kernel,
        out_shape=shape((8, 128, 2048)),
        in_specs=[pl.BlockSpec(memory_space=pltpu.SMEM)] * 3 + [pl.BlockSpec(memory_space=pl.ANY)],
        out_specs=pl.BlockSpec(memory_space=pl.ANY),
        scratch_shapes=[vmem(8, 128, 2048), DMA((8,)), DMA((8,))],
        name="pages",
    )(page_table, cache_length, target_slot, pool)
    outgoing, pieces, normed = lax.optimization_barrier((outgoing, pieces, normed))
    arrived = lax.ppermute(outgoing, "req", [(i, (i + 16) % 32) for i in range(32)])

    w, tokens = exchange(
        gather_kernel, 1, (shape((32, 12, 2048)), shape((8, 32, 2048))),
        WEIGHT_SEMS + [DMA((7,)), DMA((8,))],
        pieces, normed,
    )
    length = cache_length[req]
    leaving = target_slot[req] != req
    columns = w.reshape(384, 2048)
    projected = lax.dot_general(
        tokens.reshape(256, 2048), columns, (((1,), (1,)), ((), ())), preferred_element_type=jnp.float32
    )
    query_iota = jnp.arange(256, dtype=jnp.int32)
    frequency = jnp.exp(-math.log(10000.0) * 2.0 * jnp.arange(64, dtype=jnp.float32) / HEAD)
    angles = (length + query_iota).astype(jnp.float32)[:, None] * frequency
    cosine, sine = jnp.cos(angles), jnp.sin(angles)
    blocks = []
    for j in range(3):
        block = projected[:, j * HEAD : (j + 1) * HEAD]
        u, v = block[:, :64], block[:, 64:]
        turned = jnp.concatenate([u * cosine - v * sine, v * cosine + u * sine], axis=-1)
        blocks.append(jnp.where(3 * seq + j < 2 * HEADS, turned, block))
    qkv = jnp.stack(blocks).astype(jnp.bfloat16)

    page_start = (jnp.arange(8, dtype=jnp.int32) * 8 + seq) * 128
    row = jnp.arange(128, dtype=jnp.int32)
    held = (table[None, :] == jnp.arange(8, dtype=jnp.int32)[:, None])[:, :, None] & (
        (page_start[:, None] + row[None, :] < length)[None]
    )
    bias = jnp.where(jnp.any(held, axis=1), 0.0, MASKED).astype(jnp.float32).reshape(1024, 1)
    key_token = seq * 32 + jnp.arange(32, dtype=jnp.int32)
    fresh = jnp.where(key_token[:, None] <= query_iota[None, :], 0.0, MASKED).astype(jnp.float32)
    here, there = exchange(
        attend_kernel, 2, (shape((32, 2048)), shape((32, 2048))),
        [
            vmem(32, 8, 1024), vmem(1024, 2048), vmem(8, 256, 128), vmem(16, 32, 128),
            vmem(8, 128, 256), vmem(8, 8, 256, dtype=jnp.float32),
            vmem(8, 128, 256), vmem(8, 8, 256, dtype=jnp.float32),
            vmem(128, 256), vmem(8, 128, 256), vmem(256, 256), DMA,
            DMA((12,)), DMA((8,)), DMA((8,)), DMA((21,)), DMA((16,)),
            DMA((8,)), DMA((8,)), DMA((8,)), DMA((8,)),
            DMA((7,)), DMA((8,)), DMA((8,)), DMA((8,)), DMA((8,)), DMA((8,)),
        ] + WEIGHT_SEMS,
        qkv, pool.reshape(1024, 2048), bias, fresh, out_pieces,
        specs=[VMEM, pl.BlockSpec(memory_space=pl.ANY)] + [VMEM] * 3,
    )
    attention_out = jnp.where(leaving, there, here)
    return attention_out[None], arrived.reshape(1, 1024, 2048)


def solution(mesh):
    placed = (
        P("req", "seq", None),
        P(None, ("req", "seq")),
        P(None, ("req", "seq")),
        P("req", "seq", None, None, None),
        P("req", "seq"),
        P(),
        P(),
    )
    return jax.shard_map(
        local,
        mesh=mesh,
        in_specs=placed,
        out_specs=(P("req", "seq", None), P("req", "seq", None)),
        check_vma=False,
    )
```

```python
import functools
import math

import jax
import jax.numpy as jnp
import numpy as np
from jax import lax
from jax.experimental import pallas as pl
from jax.experimental.pallas import tpu as pltpu
from jax.sharding import PartitionSpec as P

HEAD = 128
HEADS = 8
MESH = pl.DeviceIdType.MESH
EPSILON = 1e-05
MASKED = -1e30
VMEM = pl.BlockSpec(memory_space=pltpu.VMEM)
DMA = pltpu.SemaphoreType.DMA


def place():
    return lax.axis_index("req"), lax.axis_index("seq")


def greet(devices):
    barrier = pltpu.get_barrier_semaphore()
    for req, seq in devices:
        pl.semaphore_signal(barrier, inc=1, device_id=(req, seq), device_id_type=MESH)
    return lambda: pl.semaphore_wait(barrier, len(devices))


def remote(src, dst, send, recv, req, seq):
    return pltpu.make_async_remote_copy(
        src_ref=src, dst_ref=dst, send_sem=send, recv_sem=recv,
        device_id=(req, seq), device_id_type=MESH,
    )


def landed(dst, sem):
    pltpu.make_async_copy(dst, dst, sem).wait()


def begin(copies):
    for copy in copies:
        copy.start()
    return copies


def finish(copies):
    for copy in copies:
        copy.wait_send()


def spread(own, out, req, seq, send, recv):
    zh, c = seq // 2, seq % 2
    copies = [
        remote(own, out.at[seq], send.at[dz - 1], recv.at[seq], req, (zh + dz) % 4 * 2 + c)
        for dz in (2, 1, 3)
    ]
    copies.append(remote(own, out.at[seq], send.at[3], recv.at[seq], req, 2 * zh + 1 - c))
    begin(copies)
    pltpu.make_async_copy(own, out.at[seq], recv.at[seq]).start()
    return copies


def pass_on(out, req, seq, send, recv):
    zh, c = seq // 2, seq % 2
    copies = []
    for dz in (1, 3, 2):
        source = (zh + dz) % 4 * 2 + c
        landed(out.at[source], recv.at[source])
        copies += begin(
            [remote(out.at[source], out.at[source], send.at[3 + dz], recv.at[source], req, 2 * zh + 1 - c)]
        )
    for dz in (0, 1, 3, 2):
        source = (zh + dz) % 4 * 2 + 1 - c
        landed(out.at[source], recv.at[source])
    landed(out.at[seq], recv.at[seq])
    return copies


NEAREST = (0, 1, 3, 2)


class Weights:
    def __init__(self, pieces, w, z_send, z_recv, x_send, x_recv):
        self.pieces, self.w = pieces, w
        self.z_send, self.z_recv, self.x_send, self.x_recv = z_send, z_recv, x_send, x_recv
        self.req, self.seq = req, seq = place()
        self.y, self.x, self.zl = req // 8, req // 2 % 4, req % 2
        self.zh, self.c = seq // 2, seq % 2
        self.line = self.zh * 4 + self.zl * 2 + self.c
        self.slot = self.x % 2 * 16 + self.line

    def partners(self):
        found = [(self.y * 8 + (self.x + dx) % 4 * 2 + self.zl, self.seq) for dx in (1, 2, 3)]
        for k in range(1, 16):
            there = (self.zl * 8 + self.seq + k) % 16
            found.append((self.y * 8 + self.x * 2 + there // 8, there % 8))
        return found

    def z_copy(self, e, b):
        zh = (self.zh + e) % 4
        target = zh * 2 + self.x // 2
        there = self.y * 8 + self.x * 2 + (self.zl + b) % 2
        copy = remote(
            self.pieces.at[zh], self.w.at[self.slot], self.z_send.at[e * 2 + b], self.z_recv.at[self.line], there, target
        )
        return copy, target

    def along_z(self):
        for e in NEAREST:
            copy, target = self.z_copy(e, 0)
            if e:
                copy.start()
            else:

                @pl.when(target == self.seq)
                def _():
                    pltpu.make_async_copy(
                        self.pieces.at[self.zh], self.w.at[self.slot], self.z_recv.at[self.line]
                    ).start()

                @pl.when(target != self.seq)
                def _():
                    copy.start()

            self.z_copy(e, 1)[0].start()

    def chunk(self, i):
        return (self.zh - NEAREST[i]) % 4

    def x_copy(self, h, i, step):
        k = self.chunk(i)
        block = self.w.at[pl.ds(h * 16 + 4 * k, 4)]
        there = self.y * 8 + (self.x + step) % 4 * 2 + self.zl
        return remote(block, block, self.x_send.at[(step + 1) // 2 * 8 + h * 4 + i], self.x_recv.at[h * 4 + k], there, self.seq)

    def arrived(self, h, i):
        k = self.chunk(i)
        landed(self.w.at[pl.ds(h * 16 + 4 * k, 4)], self.x_recv.at[h * 4 + k])

    def hops(self, h):
        return (self.x - 2 * self.c - h) % 4

    def along_x(self):
        for h in range(2):

            @pl.when(self.hops(h) == 0)
            def _():
                for i in range(4):
                    k = self.chunk(i)
                    for n in range(4):
                        landed(self.w.at[h * 16 + 4 * k + n], self.z_recv.at[4 * k + n])
                    self.x_copy(h, i, 1).start()
                    self.x_copy(h, i, -1).start()

        for i in range(4):
            step = 1 if i % 2 == 0 else -1
            for h in range(2):

                @pl.when((self.hops(h) == 1) | (self.hops(h) == 3))
                def _():
                    self.arrived(h, i)

                @pl.when(self.hops(h) == step % 4)
                def _():
                    self.x_copy(h, i, step).start()

        for h in range(2):

            @pl.when(self.hops(h) == 2)
            def _():
                for i in range(4):
                    self.arrived(h, i)

    def finish(self):
        for e in range(4):
            self.z_copy(e, 1)[0].wait_send()
            copy, target = self.z_copy(e, 0)
            if e:
                copy.wait_send()
            else:

                @pl.when(target != self.seq)
                def _():
                    copy.wait_send()

        for h in range(2):
            for i in range(4):
                step = 1 if i % 2 == 0 else -1

                @pl.when((self.hops(h) == 0) | (self.hops(h) == step % 4))
                def _():
                    self.x_copy(h, i, step).wait_send()

                @pl.when(self.hops(h) == 0)
                def _():
                    self.x_copy(h, i, -step).wait_send()


WEIGHT_SEMS = [DMA((8,)), DMA((16,)), DMA((16,)), DMA((8,))]


def layer_norm(row_block):
    row_mean = jnp.mean(row_block, axis=-1, keepdims=True)
    centred = row_block - row_mean
    variance = jnp.mean(centred * centred, axis=-1, keepdims=True)
    return centred / jnp.sqrt(variance + EPSILON)


def rows_kernel(
    own, out_own, hidden, lengths, targets, frequency,
    pieces, out_pieces, normed, angles, flag, send, recv, out_send, out_recv,
):
    req, seq = place()
    y = req // 8
    met = greet([((req + 8 * d) % 32, seq) for d in (1, 2, 3)])
    met()
    copies = []
    for d in (2, 1, 3):
        there = (req + 8 * d) % 32
        copies.append(remote(own, pieces.at[y], send.at[d - 1], recv.at[y], there, seq))
        copies.append(remote(out_own, out_pieces.at[y], out_send.at[d - 1], out_recv.at[y], there, seq))
    begin(copies)
    pltpu.make_async_copy(own, pieces.at[y], recv.at[y]).start()
    pltpu.make_async_copy(out_own, out_pieces.at[y], out_recv.at[y]).start()
    normed[...] = layer_norm(hidden[...].astype(jnp.float32)).astype(jnp.bfloat16)
    position = lengths[req] + lax.broadcasted_iota(jnp.int32, (256, 64), 0)
    angles[...] = position.astype(jnp.float32) * frequency[...]
    flag[...] = jnp.broadcast_to(jnp.where(targets[req] != req, 1.0, 0.0), (8, 128))
    for d in range(4):
        landed(pieces.at[d], recv.at[d])
        landed(out_pieces.at[d], out_recv.at[d])
    finish(copies)


def gather_kernel(pieces, normed, w, toks, *sems):
    req, seq = place()
    weights = Weights(pieces, w, *sems[:4])
    t_send, t_recv = sems[4:]
    greet(weights.partners())()
    weights.along_z()
    copies = spread(normed, toks, req, seq, t_send, t_recv)
    weights.along_x()
    copies += pass_on(toks, req, seq, t_send, t_recv)
    finish(copies)
    weights.finish()


def attend_kernel(
    qkv, pool, table, lengths, pieces, here,
    wo, rows, bias, fresh, q, kv, keep, keep_ml, lend, lend_ml, lent, lent_ml, pair, pair_ml,
    o_all, ml_all, own, att, out, pool_sem,
    q_send, f_send, q_recv, kv_send, kv_recv, l_send, l_recv, lm_send, lm_recv, o_send, o_recv, ml_send, ml_recv,
    a_send, a_recv, h_send, h_recv, *weight_sems,
):
    req, seq = place()
    zh, c = seq // 2, seq % 2
    other = 2 * zh + 1 - c
    weights = Weights(pieces, wo, *weight_sems)
    met = greet(weights.partners())
    loading = pltpu.make_async_copy(pool, rows, pool_sem)
    loading.start()
    length = lengths[req]
    for page in range(8):
        left = jnp.int32(0)
        for j in range(8):
            left = jnp.where(table[0, j] == page, jnp.maximum(left, length - (j * 8 + seq) * 128), left)
        bias[page * 128 : page * 128 + 128] = jnp.where(
            lax.broadcasted_iota(jnp.int32, (128, 1), 0) < left, 0.0, MASKED
        ).astype(jnp.float32)
    token = seq * 32 + lax.broadcasted_iota(jnp.int32, (32, 256), 0)
    fresh[...] = jnp.where(token <= lax.broadcasted_iota(jnp.int32, (32, 256), 1), 0.0, MASKED).astype(jnp.float32)
    met()

    def q_copies(j, head):
        copies = [
            remote(qkv.at[j], q.at[head], q_send.at[j * 4 + dz - 1], q_recv.at[head], req, (zh + dz) % 4 * 2 + c)
            for dz in (2, 1, 3)
        ]
        return copies + [remote(qkv.at[j], q.at[head], q_send.at[j * 4 + 3], q_recv.at[head], req, other)]

    def kv_copies(j, slot):
        copies = []
        for dp in range(1, 8):
            p = (seq + dp) % 8
            part = pl.ds(pl.multiple_of(32 * p, 32), 32)
            copies.append(
                remote(qkv.at[j, part], kv.at[slot], kv_send.at[j * 7 + dp - 1], kv_recv.at[slot], req, p)
            )
        return copies

    for j in range(3):
        slot = 3 * seq + j

        @pl.when(slot < HEADS)
        def _():
            begin(q_copies(j, slot))
            pltpu.make_async_copy(qkv.at[j], q.at[slot], q_recv.at[slot]).start()

        @pl.when(slot >= HEADS)
        def _():
            begin(kv_copies(j, slot - HEADS))
            part = pl.ds(pl.multiple_of(32 * seq, 32), 32)
            pltpu.make_async_copy(qkv.at[j, part], kv.at[slot - HEADS], kv_recv.at[slot - HEADS]).start()

    weights.along_z()
    loading.wait()

    def head_of(k):
        return k % 3 * 3 + k // 3

    def forward(head):
        return remote(q.at[head], q.at[head], f_send.at[head], q_recv.at[head], req, other)

    def passes(head):
        owner = head // 3
        return (c == owner % 2) & (zh != owner // 2)

    def loans(g):
        return [
            remote(lend_ml.at[g], lent_ml.at[g], lm_send.at[g], lm_recv.at[g], req, other),
            remote(lend.at[g], lent.at[g], l_send.at[g], l_recv.at[g], req, other),
        ]

    def o_copies(g):
        lane = 2 * g + c
        return [
            remote(pair_ml.at[g], ml_all.at[zh], ml_send.at[g], ml_recv.at[zh], req, lane),
            remote(pair.at[g], o_all.at[zh], o_send.at[g], o_recv.at[zh], req, lane),
        ]

    def deal(g):
        @pl.when(g == zh)
        def _():
            pltpu.make_async_copy(pair_ml.at[g], ml_all.at[zh], ml_recv.at[zh]).start()
            pltpu.make_async_copy(pair.at[g], o_all.at[zh], o_recv.at[zh]).start()

        @pl.when(g != zh)
        def _():
            begin(o_copies(g))

    def join(g):
        landed(lent_ml.at[g], lm_recv.at[g])
        landed(lent.at[g], l_recv.at[g])
        first, second = keep_ml[g], lent_ml[g]
        top = jnp.maximum(first[0:1], second[0:1])
        mine, theirs = jnp.exp(first[0:1] - top), jnp.exp(second[0:1] - top)
        pair[g] = (mine * keep[g] + theirs * lent[g].astype(jnp.float32)).astype(jnp.bfloat16)
        pair_ml[g] = jnp.concatenate(
            [top, mine * first[1:2] + theirs * second[1:2], jnp.zeros((6, 256), jnp.float32)], axis=0
        )

    across = (((1,), (1,)), ((), ()))
    down = (((0,), (0,)), ((), ()))
    scale = HEAD ** (-0.5)

    def attend(head):
        landed(q.at[head], q_recv.at[head])

        @pl.when(passes(head))
        def _():
            forward(head).start()

        landed(kv.at[head], kv_recv.at[head])
        landed(kv.at[head + 8], kv_recv.at[head + 8])
        keys = rows[:, pl.ds(pl.multiple_of(head * 128, 128), 128)]
        values = rows[:, pl.ds(pl.multiple_of(head * 128 + 1024, 128), 128)]
        query = q[head]
        s = lax.dot_general(keys, query, across, preferred_element_type=jnp.float32) * scale + bias[...]
        sn = lax.dot_general(kv[head], query, across, preferred_element_type=jnp.float32) * scale + fresh[...]
        highest = jnp.maximum(jnp.max(s, axis=0, keepdims=True), jnp.max(sn, axis=0, keepdims=True))
        p = jnp.exp(s - highest)
        pn = jnp.exp(sn - highest)
        totals = jnp.sum(p, axis=0, keepdims=True) + jnp.sum(pn, axis=0, keepdims=True)
        summed = lax.dot_general(values, p.astype(jnp.bfloat16), down, preferred_element_type=jnp.float32)
        summed += lax.dot_general(kv[head + 8], pn.astype(jnp.bfloat16), down, preferred_element_type=jnp.float32)
        state = jnp.concatenate([highest, totals, jnp.zeros((6, 256), jnp.float32)], axis=0)
        g = head // 2

        @pl.when(head % 2 == c)
        def _():
            keep[g] = summed
            keep_ml[g] = state

        @pl.when(head % 2 != c)
        def _():
            lend[g] = summed.astype(jnp.bfloat16)
            lend_ml[g] = state

    def step(k, _):
        @pl.when(k < 8)
        def _():
            attend(head_of(k))

        def head_at(lag):
            return head_of(jnp.clip(k - lag, 0, 7))

        def due(lag, ours):
            mine = head_at(lag) % 2 == c
            return (k >= lag) & (k < 8 + lag) & (mine if ours else jnp.logical_not(mine))

        @pl.when(due(1, False))
        def _():
            begin(loans(head_at(1) // 2))

        @pl.when(due(3, True))
        def _():
            deal(head_at(3) // 2)

        @pl.when(due(2, True))
        def _():
            join(head_at(2) // 2)

        return 0

    lax.fori_loop(0, 11, step, 0)
    weights.along_x()

    for chip in range(4):
        landed(ml_all.at[chip], ml_recv.at[chip])
        landed(o_all.at[chip], o_recv.at[chip])
    top = ml_all[0, 0:1]
    for chip in range(1, 4):
        top = jnp.maximum(top, ml_all[chip, 0:1])
    summed = jnp.zeros((128, 256), jnp.float32)
    total = jnp.zeros((1, 256), jnp.float32)
    for chip in range(4):
        factor = jnp.exp(ml_all[chip, 0:1] - top)
        total += factor * ml_all[chip, 1:2]
        summed += factor * o_all[chip].astype(jnp.float32)
    own[...] = (summed / total).astype(jnp.bfloat16)
    for head in range(HEADS):
        @pl.when(passes(head))
        def _():
            forward(head).wait_send()

    for g in range(4):
        finish(loans(g))

        @pl.when(g != zh)
        def _():
            finish(o_copies(g))

    copies = spread(own, att, req, seq, a_send, a_recv)
    copies += pass_on(att, req, seq, a_send, a_recv)

    columns = jnp.concatenate(
        [
            wo[half * 16 + h * 4 + low * 2 : half * 16 + h * 4 + low * 2 + 2].reshape(16, 1024)
            for half in range(2) for low in range(2) for h in range(4)
        ],
        axis=0,
    )
    out[...] = lax.dot_general(
        att[...].reshape(1024, 256), columns, (((0,), (1,)), ((), ())), preferred_element_type=jnp.float32
    ).astype(jnp.bfloat16)
    finish(copies)
    for j in range(3):
        slot = 3 * seq + j

        @pl.when(slot < HEADS)
        def _():
            finish(q_copies(j, slot))

        @pl.when(slot >= HEADS)
        def _():
            finish(kv_copies(j, slot - HEADS))

    weights.finish()

    mine = pl.ds(pl.multiple_of(256 * seq, 256), 256)
    copies = []
    for dp in (4, 3, 5, 2, 6, 1, 7):
        p = (seq + dp) % 8
        part = pl.ds(pl.multiple_of(32 * p, 32), 32)
        copies.append(remote(out.at[part], here.at[:, mine], h_send.at[dp], h_recv.at[seq], req, p))
    begin(copies)
    part = pl.ds(pl.multiple_of(32 * seq, 32), 32)
    pltpu.make_async_copy(out.at[part], here.at[:, mine], h_recv.at[seq]).start()
    for lane in range(8):
        landed(here.at[:, pl.ds(256 * lane, 256)], h_recv.at[lane])
    finish(copies)


def pages_kernel(table, lengths, targets, pool, out, buf, read_sem, write_sem):
    req, seq = place()
    length = jnp.where(targets[req] != req, lengths[req], 0)
    for j in range(8):

        @pl.when(length > (j * 8 + seq) * 128)
        def _():
            pltpu.make_async_copy(pool.at[table[0, j]], buf.at[j], read_sem.at[j]).start()

    for j in range(8):
        left = length - (j * 8 + seq) * 128

        @pl.when(left > 0)
        def _():
            pltpu.make_async_copy(pool.at[0], buf.at[j], read_sem.at[j]).wait()

        @pl.when((left > 0) & (left < 128))
        def _():
            row = lax.broadcasted_iota(jnp.int32, (128, 2048), 0)
            buf[j] = jnp.where(row < left, buf[j], jnp.zeros((128, 2048), jnp.bfloat16))

        @pl.when(left <= 0)
        def _():
            buf[j] = jnp.zeros((128, 2048), jnp.bfloat16)

        pltpu.make_async_copy(buf.at[j], out.at[j], write_sem.at[j]).start()
    for j in range(8):
        pltpu.make_async_copy(buf.at[j], out.at[j], write_sem.at[j]).wait()


def shape(dims, dtype=jnp.bfloat16):
    return jax.ShapeDtypeStruct(dims, dtype)


def vmem(*dims, dtype=jnp.bfloat16):
    return pltpu.VMEM(dims, dtype)


def exchange(kernel, number, outs, scratch, *operands, specs=None):
    return pl.pallas_call(
        kernel,
        out_shape=outs,
        in_specs=specs or [VMEM] * len(operands),
        out_specs=jax.tree.map(lambda _: VMEM, outs),
        scratch_shapes=scratch,
        compiler_params=pltpu.CompilerParams(collective_id=number, has_side_effects=True),
    )(*operands)


def local(hidden, project_weight, output_weight, cache_pool, page_table, cache_length, target_slot):
    req, seq = place()
    pool = cache_pool.reshape(8, 128, 2048)

    scalars = pl.BlockSpec(memory_space=pltpu.SMEM)
    frequency = np.exp(-math.log(10000.0) * 2.0 * np.arange(64, dtype=np.float32) / HEAD).astype(np.float32)
    pieces, out_pieces, normed, angles, flag = exchange(
        rows_kernel, 3,
        (shape((4, 16, 1536)), shape((4, 8, 1024)), shape((32, 2048)),
         shape((256, 64), jnp.float32), shape((8, 128), jnp.float32)),
        [DMA((3,)), DMA((4,)), DMA((3,)), DMA((4,))],
        project_weight.T.reshape(16, 1536), output_weight.T, hidden[0], cache_length, target_slot,
        jnp.asarray(frequency)[None],
        specs=[VMEM] * 3 + [scalars] * 2 + [VMEM],
    )
    outgoing = pl.pallas_call(
        pages_kernel,
        out_shape=shape((8, 128, 2048)),
        in_specs=[pl.BlockSpec(memory_space=pltpu.SMEM)] * 3 + [pl.BlockSpec(memory_space=pl.ANY)],
        out_specs=pl.BlockSpec(memory_space=pl.ANY),
        scratch_shapes=[vmem(8, 128, 2048), DMA((8,)), DMA((8,))],
        name="pages",
    )(page_table, cache_length, target_slot, pool)
    outgoing, pieces, normed = lax.optimization_barrier((outgoing, pieces, normed))
    swap = [(i, (i + 16) % 32) for i in range(32)]
    arrived = lax.ppermute(outgoing, "req", swap)

    w, tokens = exchange(
        gather_kernel, 1, (shape((32, 16, 1536)), shape((8, 32, 2048))),
        WEIGHT_SEMS + [DMA((7,)), DMA((8,))],
        pieces, normed,
    )
    columns = w.reshape(2, 4, 2, 2, 16, 1536).transpose(0, 2, 1, 3, 4, 5).reshape(384, 2048)
    projected = lax.dot_general(
        tokens.reshape(256, 2048), columns, (((1,), (1,)), ((), ())), preferred_element_type=jnp.float32
    )
    cosine, sine = jnp.cos(angles), jnp.sin(angles)
    blocks = []
    for j in range(3):
        block = projected[:, j * HEAD : (j + 1) * HEAD]
        u, v = block[:, :64], block[:, 64:]
        turned = jnp.concatenate([u * cosine - v * sine, v * cosine + u * sine], axis=-1)
        blocks.append(jnp.where(3 * seq + j < 2 * HEADS, turned, block))
    qkv = jnp.stack(blocks).astype(jnp.bfloat16)

    here = exchange(
        attend_kernel, 2, shape((32, 2048)),
        [
            vmem(32, 8, 1024), vmem(1024, 2048), vmem(1024, 1, dtype=jnp.float32), vmem(32, 256, dtype=jnp.float32),
            vmem(8, 256, 128), vmem(16, 32, 128),
            vmem(4, 128, 256, dtype=jnp.float32), vmem(4, 8, 256, dtype=jnp.float32),
            vmem(4, 128, 256), vmem(4, 8, 256, dtype=jnp.float32),
            vmem(4, 128, 256), vmem(4, 8, 256, dtype=jnp.float32),
            vmem(4, 128, 256), vmem(4, 8, 256, dtype=jnp.float32),
            vmem(4, 128, 256), vmem(4, 8, 256, dtype=jnp.float32),
            vmem(128, 256), vmem(8, 128, 256), vmem(256, 256), DMA,
            DMA((12,)), DMA((8,)), DMA((8,)), DMA((21,)), DMA((16,)),
            DMA((4,)), DMA((4,)), DMA((4,)), DMA((4,)), DMA((4,)), DMA((4,)), DMA((4,)), DMA((4,)),
            DMA((7,)), DMA((8,)), DMA((8,)), DMA((8,)),
        ] + WEIGHT_SEMS,
        qkv, pool.reshape(1024, 2048), page_table, cache_length, out_pieces,
        specs=[VMEM, pl.BlockSpec(memory_space=pl.ANY), scalars, scalars, VMEM],
    )
    there = lax.ppermute(here, "req", swap)
    attention_out = jnp.where(flag[0, 0] > 0, there, here)
    return attention_out[None], arrived.reshape(1, 1024, 2048)


def solution(mesh):
    placed = (
        P("req", "seq", None),
        P(None, ("req", "seq")),
        P(None, ("req", "seq")),
        P("req", "seq", None, None, None),
        P("req", "seq"),
        P(),
        P(),
    )
    return jax.shard_map(
        local,
        mesh=mesh,
        in_specs=placed,
        out_specs=(P("req", "seq", None), P("req", "seq", None)),
        check_vma=False,
    )
```

```python
import functools
import math

import jax
import jax.numpy as jnp
import numpy as np
from jax import lax
from jax.experimental import pallas as pl
from jax.experimental.pallas import tpu as pltpu
from jax.sharding import PartitionSpec as P

HEAD = 128
HEADS = 8
MESH = pl.DeviceIdType.MESH
EPSILON = 1e-05
MASKED = -1e30
VMEM = pl.BlockSpec(memory_space=pltpu.VMEM)
DMA = pltpu.SemaphoreType.DMA


def place():
    return lax.axis_index("req"), lax.axis_index("seq")


def greet(devices):
    barrier = pltpu.get_barrier_semaphore()
    for req, seq in devices:
        pl.semaphore_signal(barrier, inc=1, device_id=(req, seq), device_id_type=MESH)
    return lambda: pl.semaphore_wait(barrier, len(devices))


def remote(src, dst, send, recv, req, seq):
    return pltpu.make_async_remote_copy(
        src_ref=src, dst_ref=dst, send_sem=send, recv_sem=recv,
        device_id=(req, seq), device_id_type=MESH,
    )


def landed(dst, sem):
    pltpu.make_async_copy(dst, dst, sem).wait()


def begin(copies):
    for copy in copies:
        copy.start()
    return copies


def finish(copies):
    for copy in copies:
        copy.wait_send()


def spread(own, out, req, seq, send, recv, steps=(2, 1, 3), near=True):
    zh, c = seq // 2, seq % 2
    copies = [
        remote(own, out.at[seq], send.at[dz - 1], recv.at[seq], req, (zh + dz) % 4 * 2 + c)
        for dz in steps
    ]
    if near:
        copies.append(remote(own, out.at[seq], send.at[3], recv.at[seq], req, 2 * zh + 1 - c))
        pltpu.make_async_copy(own, out.at[seq], recv.at[seq]).start()
    return begin(copies)


def pass_on(out, req, seq, send, recv):
    zh, c = seq // 2, seq % 2
    copies = []
    for dz in (1, 3, 2):
        source = (zh + dz) % 4 * 2 + c
        landed(out.at[source], recv.at[source])
        copies += begin(
            [remote(out.at[source], out.at[source], send.at[3 + dz], recv.at[source], req, 2 * zh + 1 - c)]
        )
    for dz in (0, 1, 3, 2):
        source = (zh + dz) % 4 * 2 + 1 - c
        landed(out.at[source], recv.at[source])
    landed(out.at[seq], recv.at[seq])
    return copies


NEAREST = (0, 1, 3, 2)


class Weights:
    def __init__(self, pieces, w, z_send, z_recv, x_send, x_recv):
        self.pieces, self.w = pieces, w
        self.z_send, self.z_recv, self.x_send, self.x_recv = z_send, z_recv, x_send, x_recv
        self.req, self.seq = req, seq = place()
        self.y, self.x, self.zl = req // 8, req // 2 % 4, req % 2
        self.zh, self.c = seq // 2, seq % 2
        self.line = self.zh * 4 + self.zl * 2 + self.c
        self.slot = self.x % 2 * 16 + self.line

    def partners(self):
        found = [(self.y * 8 + (self.x + dx) % 4 * 2 + self.zl, self.seq) for dx in (1, 2, 3)]
        for k in range(1, 16):
            there = (self.zl * 8 + self.seq + k) % 16
            found.append((self.y * 8 + self.x * 2 + there // 8, there % 8))
        return found

    def z_copy(self, e, b):
        zh = (self.zh + e) % 4
        target = zh * 2 + self.x // 2
        there = self.y * 8 + self.x * 2 + (self.zl + b) % 2
        copy = remote(
            self.pieces.at[zh], self.w.at[self.slot], self.z_send.at[e * 2 + b], self.z_recv.at[self.line], there, target
        )
        return copy, target

    def along_z(self, y_recv):
        for e in NEAREST:
            zh = (self.zh + e) % 4
            landed(self.pieces.at[zh], y_recv.at[zh])
            copy, target = self.z_copy(e, 0)
            if e:
                copy.start()
            else:

                @pl.when(target == self.seq)
                def _():
                    pltpu.make_async_copy(
                        self.pieces.at[self.zh], self.w.at[self.slot], self.z_recv.at[self.line]
                    ).start()

                @pl.when(target != self.seq)
                def _():
                    copy.start()

            self.z_copy(e, 1)[0].start()

    def chunk(self, i):
        return (self.zh - NEAREST[i]) % 4

    def x_copy(self, h, i, step):
        k = self.chunk(i)
        block = self.w.at[pl.ds(h * 16 + 4 * k, 4)]
        there = self.y * 8 + (self.x + step) % 4 * 2 + self.zl
        return remote(block, block, self.x_send.at[(step + 1) // 2 * 8 + h * 4 + i], self.x_recv.at[h * 4 + k], there, self.seq)

    def arrived(self, h, i):
        k = self.chunk(i)
        landed(self.w.at[pl.ds(h * 16 + 4 * k, 4)], self.x_recv.at[h * 4 + k])

    def hops(self, h):
        return (self.x - 2 * self.c - h) % 4

    def along_x(self):
        for h in range(2):

            @pl.when(self.hops(h) == 0)
            def _():
                for i in range(4):
                    k = self.chunk(i)
                    for n in range(4):
                        landed(self.w.at[h * 16 + 4 * k + n], self.z_recv.at[4 * k + n])
                    self.x_copy(h, i, 1).start()
                    self.x_copy(h, i, -1).start()

        for i in range(4):
            step = 1 if i % 2 == 0 else -1
            for h in range(2):

                @pl.when((self.hops(h) == 1) | (self.hops(h) == 3))
                def _():
                    self.arrived(h, i)

                @pl.when(self.hops(h) == step % 4)
                def _():
                    self.x_copy(h, i, step).start()

        for h in range(2):

            @pl.when(self.hops(h) == 2)
            def _():
                for i in range(4):
                    self.arrived(h, i)

    def finish(self):
        for e in range(4):
            self.z_copy(e, 1)[0].wait_send()
            copy, target = self.z_copy(e, 0)
            if e:
                copy.wait_send()
            else:

                @pl.when(target != self.seq)
                def _():
                    copy.wait_send()

        for h in range(2):
            for i in range(4):
                step = 1 if i % 2 == 0 else -1

                @pl.when((self.hops(h) == 0) | (self.hops(h) == step % 4))
                def _():
                    self.x_copy(h, i, step).wait_send()

                @pl.when(self.hops(h) == 0)
                def _():
                    self.x_copy(h, i, -step).wait_send()


WEIGHT_SEMS = [DMA((8,)), DMA((16,)), DMA((16,)), DMA((8,))]


def layer_norm(row_block):
    row_mean = jnp.mean(row_block, axis=-1, keepdims=True)
    centred = row_block - row_mean
    variance = jnp.mean(centred * centred, axis=-1, keepdims=True)
    return centred / jnp.sqrt(variance + EPSILON)


def layer_kernel(
    hidden, project, out_project, pool, table, lengths, targets, turns, turns_page, pick, pick_out,
    result, raw, far_table,
    joint, normed, pieces, w, toks, wide, qkv, spins,
    rows, bias, fresh, q, kv, keep, keep_ml, lend, lend_ml, lent, lent_ml, pair, pair_ml,
    o_all, ml_all, own, att, out, here, there, own_table, pool_sem, table_send, table_recv,
    y_send, y_recv, m_send, m_recv, k_send, k_recv,
    q_send, f_send, q_recv, kv_send, kv_recv, l_send, l_recv, lm_send, lm_recv, o_send, o_recv, ml_send, ml_recv,
    a_send, a_recv, h_send, h_recv, t_send, t_recv, *weight_sems,
):
    req, seq = place()
    y = req // 8
    zh, c = seq // 2, seq % 2
    other = 2 * zh + 1 - c
    far = (req + 16) % 32
    weights = Weights(pieces, w, *weight_sems)
    met = greet(
        weights.partners()
        + [((req + 8 * d) % 32, seq) for d in (1, 2, 3)]
        + [(far, (seq + dp) % 8) for dp in range(1, 8)]
    )
    loading = pltpu.make_async_copy(pool, rows, pool_sem)
    loading.start()
    joint[...] = jnp.concatenate(
        [
            project[...].astype(jnp.float32),
            jnp.concatenate(
                [out_project[0:4].astype(jnp.float32), out_project[4:8].astype(jnp.float32)], axis=1
            ),
        ],
        axis=0,
    ).astype(jnp.bfloat16)
    normed[...] = layer_norm(hidden[...].astype(jnp.float32)).astype(jnp.bfloat16)
    lane = lax.broadcasted_iota(jnp.int32, (8, 128), 1)
    entries = jnp.zeros((8, 128), jnp.int32)
    for j in range(8):
        entries = jnp.where(lane == j, table[0, j], entries)
    own_table[...] = entries
    length = lengths[req]
    for page in range(8):
        left = jnp.int32(0)
        for j in range(8):
            left = jnp.where(table[0, j] == page, jnp.maximum(left, length - (j * 8 + seq) * 128), left)
        bias[page * 128 : page * 128 + 128] = jnp.where(
            lax.broadcasted_iota(jnp.int32, (128, 1), 0) < left, 0.0, MASKED
        ).astype(jnp.float32)
    coarse, fine = length // 256, length % 256
    cosine_page, sine_page = turns_page[0, pl.ds(coarse, 1)], turns_page[1, pl.ds(coarse, 1)]
    cosine_row, sine_row = turns[0, pl.ds(fine, 1)], turns[1, pl.ds(fine, 1)]
    cosine_start = cosine_page * cosine_row - sine_page * sine_row
    sine_start = sine_page * cosine_row + cosine_page * sine_row
    spins[0] = cosine_start * turns[0] - sine_start * turns[1]
    sine = sine_start * turns[0] + cosine_start * turns[1]
    spins[1] = jnp.where(lax.broadcasted_iota(jnp.int32, (256, 128), 1) < 64, -sine, sine)
    token = seq * 32 + lax.broadcasted_iota(jnp.int32, (32, 256), 0)
    fresh[...] = jnp.where(token <= lax.broadcasted_iota(jnp.int32, (32, 256), 1), 0.0, MASKED).astype(jnp.float32)
    met()

    y_copies = begin(
        [remote(joint, pieces.at[y], y_send.at[d - 1], y_recv.at[y], (req + 8 * d) % 32, seq) for d in (2, 1, 3)]
    )
    pltpu.make_async_copy(joint, pieces.at[y], y_recv.at[y]).start()
    migration = begin([remote(own_table, far_table, table_send, table_recv, far, seq)])
    migration += begin([remote(pool.at[i], raw.at[i], m_send.at[i], m_recv.at[i], far, seq) for i in range(8)])
    copies = spread(normed, toks, req, seq, k_send, k_recv, (1, 3))
    weights.along_z(y_recv)
    copies += spread(normed, toks, req, seq, k_send, k_recv, (2,), False)
    weights.along_x()
    copies += pass_on(toks, req, seq, k_send, k_recv)

    across = (((1,), (1,)), ((), ()))
    down = (((0,), (0,)), ((), ()))
    tokens = toks[...].reshape(256, 2048)

    def multiply(n, _):
        wide[:, pl.ds(pl.multiple_of(n * 128, 128), 128)] = lax.dot_general(
            tokens, w[pl.ds(n * 8, 8)].reshape(128, 2048), across, preferred_element_type=jnp.float32
        )
        return 0

    lax.fori_loop(0, 4, multiply, 0)
    whole = wide[...]
    high = whole.astype(jnp.bfloat16)
    rest = whole - high.astype(jnp.float32)
    middle = rest.astype(jnp.bfloat16)
    low = (rest - middle.astype(jnp.float32)).astype(jnp.bfloat16)
    picked = [jnp.dot(part, pick[...], preferred_element_type=jnp.float32) for part in (middle, low, high)]
    projected = picked[0] + picked[1] + picked[2]
    for j in range(3):
        block = projected[:, j * HEAD : (j + 1) * HEAD]
        turned = block * spins[0] + pltpu.roll(block, 64, 1) * spins[1]
        qkv[j] = jnp.where(3 * seq + j < 2 * HEADS, turned, block).astype(jnp.bfloat16)
    finish(copies)
    finish(y_copies)
    weights.finish()

    def q_copies(j, head):
        copies = [
            remote(qkv.at[j], q.at[head], q_send.at[j * 4 + dz - 1], q_recv.at[head], req, (zh + dz) % 4 * 2 + c)
            for dz in (2, 1, 3)
        ]
        return copies + [remote(qkv.at[j], q.at[head], q_send.at[j * 4 + 3], q_recv.at[head], req, other)]

    def kv_copies(j, slot):
        copies = []
        for dp in range(1, 8):
            p = (seq + dp) % 8
            part = pl.ds(pl.multiple_of(32 * p, 32), 32)
            copies.append(
                remote(qkv.at[j, part], kv.at[slot], kv_send.at[j * 7 + dp - 1], kv_recv.at[slot], req, p)
            )
        return copies

    for j in range(3):
        slot = 3 * seq + j

        @pl.when(slot < HEADS)
        def _():
            begin(q_copies(j, slot))
            pltpu.make_async_copy(qkv.at[j], q.at[slot], q_recv.at[slot]).start()

        @pl.when(slot >= HEADS)
        def _():
            begin(kv_copies(j, slot - HEADS))
            part = pl.ds(pl.multiple_of(32 * seq, 32), 32)
            pltpu.make_async_copy(qkv.at[j, part], kv.at[slot - HEADS], kv_recv.at[slot - HEADS]).start()

    loading.wait()

    def head_of(k):
        return k % 3 * 3 + k // 3

    def forward(head):
        return remote(q.at[head], q.at[head], f_send.at[head], q_recv.at[head], req, other)

    def passes(head):
        owner = head // 3
        return (c == owner % 2) & (zh != owner // 2)

    def loans(g):
        return [
            remote(lend_ml.at[g], lent_ml.at[g], lm_send.at[g], lm_recv.at[g], req, other),
            remote(lend.at[g], lent.at[g], l_send.at[g], l_recv.at[g], req, other),
        ]

    def o_copies(g):
        lane = 2 * g + c
        return [
            remote(pair_ml.at[g], ml_all.at[zh], ml_send.at[g], ml_recv.at[zh], req, lane),
            remote(pair.at[g], o_all.at[zh], o_send.at[g], o_recv.at[zh], req, lane),
        ]

    def deal(g):
        @pl.when(g == zh)
        def _():
            pltpu.make_async_copy(pair_ml.at[g], ml_all.at[zh], ml_recv.at[zh]).start()
            pltpu.make_async_copy(pair.at[g], o_all.at[zh], o_recv.at[zh]).start()

        @pl.when(g != zh)
        def _():
            begin(o_copies(g))

    def join(g):
        landed(lent_ml.at[g], lm_recv.at[g])
        landed(lent.at[g], l_recv.at[g])
        first, second = keep_ml[g], lent_ml[g]
        top = jnp.maximum(first[0:1], second[0:1])
        mine, theirs = jnp.exp(first[0:1] - top), jnp.exp(second[0:1] - top)
        pair[g] = (mine * keep[g] + theirs * lent[g].astype(jnp.float32)).astype(jnp.bfloat16)
        pair_ml[g] = jnp.concatenate(
            [top, mine * first[1:2] + theirs * second[1:2], jnp.zeros((6, 256), jnp.float32)], axis=0
        )

    scale = HEAD ** (-0.5)

    def attend(head):
        landed(q.at[head], q_recv.at[head])

        @pl.when(passes(head))
        def _():
            forward(head).start()

        landed(kv.at[head], kv_recv.at[head])
        landed(kv.at[head + 8], kv_recv.at[head + 8])
        keys = rows[:, :, pl.ds(pl.multiple_of(head * 128, 128), 128)].reshape(1024, 128)
        values = rows[:, :, pl.ds(pl.multiple_of(head * 128 + 1024, 128), 128)].reshape(1024, 128)
        query = q[head]
        s = lax.dot_general(keys, query, across, preferred_element_type=jnp.float32) * scale + bias[...]
        sn = lax.dot_general(kv[head], query, across, preferred_element_type=jnp.float32) * scale + fresh[...]
        highest = jnp.maximum(jnp.max(s, axis=0, keepdims=True), jnp.max(sn, axis=0, keepdims=True))
        p = jnp.exp(s - highest)
        pn = jnp.exp(sn - highest)
        totals = jnp.sum(p, axis=0, keepdims=True) + jnp.sum(pn, axis=0, keepdims=True)
        summed = lax.dot_general(values, p.astype(jnp.bfloat16), down, preferred_element_type=jnp.float32)
        summed += lax.dot_general(kv[head + 8], pn.astype(jnp.bfloat16), down, preferred_element_type=jnp.float32)
        state = jnp.concatenate([highest, totals, jnp.zeros((6, 256), jnp.float32)], axis=0)
        g = head // 2

        @pl.when(head % 2 == c)
        def _():
            keep[g] = summed
            keep_ml[g] = state

        @pl.when(head % 2 != c)
        def _():
            lend[g] = summed.astype(jnp.bfloat16)
            lend_ml[g] = state

    def step(k, _):
        @pl.when(k < 8)
        def _():
            attend(head_of(k))

        def head_at(lag):
            return head_of(jnp.clip(k - lag, 0, 7))

        def due(lag, ours):
            mine = head_at(lag) % 2 == c
            return (k >= lag) & (k < 8 + lag) & (mine if ours else jnp.logical_not(mine))

        @pl.when(due(1, False))
        def _():
            begin(loans(head_at(1) // 2))

        @pl.when(due(3, True))
        def _():
            deal(head_at(3) // 2)

        @pl.when(due(2, True))
        def _():
            join(head_at(2) // 2)

        return 0

    lax.fori_loop(0, 11, step, 0)

    for chip in range(4):
        landed(ml_all.at[chip], ml_recv.at[chip])
        landed(o_all.at[chip], o_recv.at[chip])
    top = ml_all[0, 0:1]
    for chip in range(1, 4):
        top = jnp.maximum(top, ml_all[chip, 0:1])
    summed = jnp.zeros((128, 256), jnp.float32)
    total = jnp.zeros((1, 256), jnp.float32)
    for chip in range(4):
        factor = jnp.exp(ml_all[chip, 0:1] - top)
        total += factor * ml_all[chip, 1:2]
        summed += factor * o_all[chip].astype(jnp.float32)
    own[...] = (summed / total).astype(jnp.bfloat16)
    for head in range(HEADS):
        @pl.when(passes(head))
        def _():
            forward(head).wait_send()

    for g in range(4):
        finish(loans(g))

        @pl.when(g != zh)
        def _():
            finish(o_copies(g))

    copies = spread(own, att, req, seq, a_send, a_recv)
    copies += pass_on(att, req, seq, a_send, a_recv)

    attended = att[...].reshape(1024, 256)
    total = jnp.zeros((256, 256), jnp.float32)
    for half in range(2):
        product = lax.dot_general(
            attended, w[:, :, half * 1024 : half * 1024 + 1024].reshape(512, 1024), (((0,), (1,)), ((), ())),
            preferred_element_type=jnp.float32,
        ).astype(jnp.bfloat16)
        total += jnp.dot(product, pick_out[half], preferred_element_type=jnp.float32)
    out[...] = total.astype(jnp.bfloat16)
    finish(copies)
    for j in range(3):
        slot = 3 * seq + j

        @pl.when(slot < HEADS)
        def _():
            finish(q_copies(j, slot))

        @pl.when(slot >= HEADS)
        def _():
            finish(kv_copies(j, slot - HEADS))

    mine = pl.ds(pl.multiple_of(256 * seq, 256), 256)
    copies = []
    for dp in (4, 3, 5, 2, 6, 1, 7, 0):
        p = (seq + dp) % 8
        part = pl.ds(pl.multiple_of(32 * p, 32), 32)
        copies.append(remote(out.at[part], there.at[:, mine], t_send.at[dp], t_recv.at[seq], far, p))
        if dp:
            copies.append(remote(out.at[part], here.at[:, mine], h_send.at[dp], h_recv.at[seq], req, p))
    begin(copies)
    part = pl.ds(pl.multiple_of(32 * seq, 32), 32)
    pltpu.make_async_copy(out.at[part], here.at[:, mine], h_recv.at[seq]).start()
    landed(far_table, table_recv)
    for i in range(8):
        landed(raw.at[i], m_recv.at[i])
    finish(migration)
    for lane in range(8):
        landed(here.at[:, pl.ds(256 * lane, 256)], h_recv.at[lane])
        landed(there.at[:, pl.ds(256 * lane, 256)], t_recv.at[lane])
    result[...] = jnp.where(targets[req] != req, there[...], here[...])
    finish(copies)


def pages_kernel(table, lengths, targets, pool, out, buf, read_sem, write_sem):
    req, seq = place()
    length = jnp.where(targets[req] != req, lengths[(req + 16) % 32], 0)
    for j in range(8):

        @pl.when(length > (j * 8 + seq) * 128)
        def _():
            pltpu.make_async_copy(pool.at[table[0, j]], buf.at[j], read_sem.at[j]).start()

    for j in range(8):
        left = length - (j * 8 + seq) * 128

        @pl.when(left > 0)
        def _():
            pltpu.make_async_copy(pool.at[0], buf.at[j], read_sem.at[j]).wait()

        @pl.when((left > 0) & (left < 128))
        def _():
            row = lax.broadcasted_iota(jnp.int32, (128, 2048), 0)
            buf[j] = jnp.where(row < left, buf[j], jnp.zeros((128, 2048), jnp.bfloat16))

        @pl.when(left <= 0)
        def _():
            buf[j] = jnp.zeros((128, 2048), jnp.bfloat16)

        pltpu.make_async_copy(buf.at[j], out.at[j], write_sem.at[j]).start()
    for j in range(8):
        pltpu.make_async_copy(buf.at[j], out.at[j], write_sem.at[j]).wait()


def shape(dims, dtype=jnp.bfloat16):
    return jax.ShapeDtypeStruct(dims, dtype)


def vmem(*dims, dtype=jnp.bfloat16):
    return pltpu.VMEM(dims, dtype)


def tables():
    frequency = np.exp(-math.log(10000.0) * 2.0 * np.arange(64) / HEAD)
    frequency = np.concatenate([frequency, frequency])
    step = np.arange(256)[:, None] * frequency
    page = 256.0 * np.arange(40)[:, None] * frequency
    turns = np.stack([np.cos(step), np.sin(step)]).astype(np.float32)
    turns_page = np.stack([np.cos(page), np.sin(page)]).astype(np.float32)
    row = np.arange(512)
    slot, entry = row // 16, row % 16
    piece = slot // 16 * 16 + slot // 2 % 2 * 8 + slot // 4 % 4 * 2 + slot % 2
    column = np.where(entry < 12, piece * 12 + entry, -1)
    pick = column[:, None] == np.arange(384)
    pick_out = [
        np.where(entry >= 12, piece * 8 + half * 4 + entry - 12, -1)[:, None] == np.arange(256) for half in range(2)
    ]
    return turns, turns_page, pick, np.stack(pick_out)


def local(hidden, project_weight, output_weight, cache_pool, page_table, cache_length, target_slot):
    anywhere = pl.BlockSpec(memory_space=pl.ANY)
    scalars = pl.BlockSpec(memory_space=pltpu.SMEM)
    turns, turns_page, pick, pick_out = tables()
    f32 = jnp.float32
    attention_out, raw, far_table = pl.pallas_call(
        layer_kernel,
        out_shape=(shape((32, 2048)), shape((8, 128, 2048)), shape((8, 128), jnp.int32)),
        in_specs=[VMEM] * 3 + [anywhere] + [scalars] * 3 + [VMEM] * 4,
        out_specs=(VMEM, anywhere, VMEM),
        scratch_shapes=[
            vmem(16, 2048), vmem(32, 2048), vmem(4, 16, 2048), vmem(32, 16, 2048), vmem(8, 32, 2048),
            vmem(256, 512, dtype=f32), vmem(3, 256, 128), vmem(2, 256, 128, dtype=f32),
            vmem(8, 128, 2048), vmem(1024, 1, dtype=f32), vmem(32, 256, dtype=f32),
            vmem(8, 256, 128), vmem(16, 32, 128),
            vmem(4, 128, 256, dtype=f32), vmem(4, 8, 256, dtype=f32),
            vmem(4, 128, 256), vmem(4, 8, 256, dtype=f32),
            vmem(4, 128, 256), vmem(4, 8, 256, dtype=f32),
            vmem(4, 128, 256), vmem(4, 8, 256, dtype=f32),
            vmem(4, 128, 256), vmem(4, 8, 256, dtype=f32),
            vmem(128, 256), vmem(8, 128, 256), vmem(256, 256), vmem(32, 2048), vmem(32, 2048),
            vmem(8, 128, dtype=jnp.int32), DMA, DMA, DMA,
            DMA((3,)), DMA((4,)), DMA((8,)), DMA((8,)), DMA((7,)), DMA((8,)),
            DMA((12,)), DMA((8,)), DMA((8,)), DMA((21,)), DMA((16,)),
            DMA((4,)), DMA((4,)), DMA((4,)), DMA((4,)), DMA((4,)), DMA((4,)), DMA((4,)), DMA((4,)),
            DMA((7,)), DMA((8,)), DMA((8,)), DMA((8,)), DMA((8,)), DMA((8,)),
        ] + WEIGHT_SEMS,
        compiler_params=pltpu.CompilerParams(collective_id=1, has_side_effects=True),
        name="layer",
    )(
        hidden[0], project_weight.T, output_weight.T, cache_pool.reshape(8, 128, 2048),
        page_table, cache_length, target_slot,
        jnp.asarray(turns), jnp.asarray(turns_page), jnp.asarray(pick, jnp.bfloat16), jnp.asarray(pick_out, jnp.bfloat16),
    )
    arrived = pl.pallas_call(
        pages_kernel,
        out_shape=shape((8, 128, 2048)),
        in_specs=[scalars] * 3 + [anywhere],
        out_specs=anywhere,
        scratch_shapes=[vmem(8, 128, 2048), DMA((8,)), DMA((8,))],
        name="pages",
    )(far_table, cache_length, target_slot, raw)
    return attention_out[None], arrived.reshape(1, 1024, 2048)


def solution(mesh):
    placed = (
        P("req", "seq", None),
        P(None, ("req", "seq")),
        P(None, ("req", "seq")),
        P("req", "seq", None, None, None),
        P("req", "seq"),
        P(),
        P(),
    )
    return jax.shard_map(
        local,
        mesh=mesh,
        in_specs=placed,
        out_specs=(P("req", "seq", None), P("req", "seq", None)),
        check_vma=False,
    )
```

```python
import functools
import math

import jax
import jax.numpy as jnp
import numpy as np
from jax import lax
from jax.experimental import pallas as pl
from jax.experimental.pallas import tpu as pltpu
from jax.sharding import PartitionSpec as P

HEAD = 128
HEADS = 8
MESH = pl.DeviceIdType.MESH
EPSILON = 1e-05
MASKED = -1e30
HELD = 1
VMEM = pl.BlockSpec(memory_space=pltpu.VMEM)
DMA = pltpu.SemaphoreType.DMA


def place():
    return lax.axis_index("req"), lax.axis_index("seq")


def greet(devices):
    barrier = pltpu.get_barrier_semaphore()
    for req, seq in devices:
        pl.semaphore_signal(barrier, inc=1, device_id=(req, seq), device_id_type=MESH)
    return lambda: pl.semaphore_wait(barrier, len(devices))


def remote(src, dst, send, recv, req, seq):
    return pltpu.make_async_remote_copy(
        src_ref=src, dst_ref=dst, send_sem=send, recv_sem=recv,
        device_id=(req, seq), device_id_type=MESH,
    )


def landed(dst, sem):
    pltpu.make_async_copy(dst, dst, sem).wait()


def begin(copies):
    for copy in copies:
        copy.start()
    return copies


def finish(copies):
    for copy in copies:
        copy.wait_send()


def spread(own, out, req, seq, send, recv, steps=(2, 1, 3), near=True):
    zh, c = seq // 2, seq % 2
    copies = [
        remote(own, out.at[seq], send.at[dz - 1], recv.at[seq], req, (zh + dz) % 4 * 2 + c)
        for dz in steps
    ]
    if near:
        copies.append(remote(own, out.at[seq], send.at[3], recv.at[seq], req, 2 * zh + 1 - c))
        pltpu.make_async_copy(own, out.at[seq], recv.at[seq]).start()
    return begin(copies)


def pass_on(out, req, seq, send, recv):
    zh, c = seq // 2, seq % 2
    copies = []
    for dz in (1, 3, 2):
        source = (zh + dz) % 4 * 2 + c
        landed(out.at[source], recv.at[source])
        copies += begin(
            [remote(out.at[source], out.at[source], send.at[3 + dz], recv.at[source], req, 2 * zh + 1 - c)]
        )
    for dz in (0, 1, 3, 2):
        source = (zh + dz) % 4 * 2 + 1 - c
        landed(out.at[source], recv.at[source])
    landed(out.at[seq], recv.at[seq])
    return copies


NEAREST = (0, 1, 3, 2)


class Weights:
    def __init__(self, pieces, w, z_send, z_recv, x_send, x_recv):
        self.pieces, self.w = pieces, w
        self.z_send, self.z_recv, self.x_send, self.x_recv = z_send, z_recv, x_send, x_recv
        self.req, self.seq = req, seq = place()
        self.y, self.x, self.zl = req // 8, req // 2 % 4, req % 2
        self.zh, self.c = seq // 2, seq % 2
        self.line = self.zh * 4 + self.zl * 2 + self.c
        self.slot = self.x % 2 * 16 + self.line

    def partners(self):
        found = [(self.y * 8 + (self.x + dx) % 4 * 2 + self.zl, self.seq) for dx in (1, 2, 3)]
        for k in range(1, 16):
            there = (self.zl * 8 + self.seq + k) % 16
            found.append((self.y * 8 + self.x * 2 + there // 8, there % 8))
        return found

    def z_copy(self, e, b):
        zh = (self.zh + e) % 4
        target = zh * 2 + self.x // 2
        there = self.y * 8 + self.x * 2 + (self.zl + b) % 2
        copy = remote(
            self.pieces.at[zh], self.w.at[self.slot], self.z_send.at[e * 2 + b], self.z_recv.at[self.line], there, target
        )
        return copy, target

    def along_z(self, y_recv):
        for e in NEAREST:
            zh = (self.zh + e) % 4
            landed(self.pieces.at[zh], y_recv.at[zh])
            copy, target = self.z_copy(e, 0)
            if e:
                copy.start()
            else:

                @pl.when(target == self.seq)
                def _():
                    pltpu.make_async_copy(
                        self.pieces.at[self.zh], self.w.at[self.slot], self.z_recv.at[self.line]
                    ).start()

                @pl.when(target != self.seq)
                def _():
                    copy.start()

            self.z_copy(e, 1)[0].start()

    def chunk(self, i):
        return (self.zh - NEAREST[i]) % 4

    def x_copy(self, h, i, step):
        k = self.chunk(i)
        block = self.w.at[pl.ds(h * 16 + 4 * k, 4)]
        there = self.y * 8 + (self.x + step) % 4 * 2 + self.zl
        return remote(block, block, self.x_send.at[(step + 1) // 2 * 8 + h * 4 + i], self.x_recv.at[h * 4 + k], there, self.seq)

    def arrived(self, h, i):
        k = self.chunk(i)
        landed(self.w.at[pl.ds(h * 16 + 4 * k, 4)], self.x_recv.at[h * 4 + k])

    def hops(self, h):
        return (self.x - 2 * self.c - h) % 4

    def along_x(self):
        for h in range(2):

            @pl.when(self.hops(h) == 0)
            def _():
                for i in range(4):
                    k = self.chunk(i)
                    for n in range(4):
                        landed(self.w.at[h * 16 + 4 * k + n], self.z_recv.at[4 * k + n])
                    self.x_copy(h, i, 1).start()
                    self.x_copy(h, i, -1).start()

        for i in range(4):
            step = 1 if i % 2 == 0 else -1
            for h in range(2):

                @pl.when((self.hops(h) == 1) | (self.hops(h) == 3))
                def _():
                    self.arrived(h, i)

                @pl.when(self.hops(h) == step % 4)
                def _():
                    self.x_copy(h, i, step).start()

        for h in range(2):

            @pl.when(self.hops(h) == 2)
            def _():
                for i in range(4):
                    self.arrived(h, i)

    def finish(self):
        for e in range(4):
            self.z_copy(e, 1)[0].wait_send()
            copy, target = self.z_copy(e, 0)
            if e:
                copy.wait_send()
            else:

                @pl.when(target != self.seq)
                def _():
                    copy.wait_send()

        for h in range(2):
            for i in range(4):
                step = 1 if i % 2 == 0 else -1

                @pl.when((self.hops(h) == 0) | (self.hops(h) == step % 4))
                def _():
                    self.x_copy(h, i, step).wait_send()

                @pl.when(self.hops(h) == 0)
                def _():
                    self.x_copy(h, i, -step).wait_send()


WEIGHT_SEMS = [DMA((8,)), DMA((16,)), DMA((16,)), DMA((8,))]


def layer_norm(row_block):
    row_mean = jnp.mean(row_block, axis=-1, keepdims=True)
    centred = row_block - row_mean
    variance = jnp.mean(centred * centred, axis=-1, keepdims=True)
    return centred / jnp.sqrt(variance + EPSILON)


def layer_kernel(
    hidden, project, out_project, pool, table, lengths, targets, turns_hbm, turns_page_hbm, pick_hbm, pick_out_hbm,
    result, raw, far_table,
    joint, normed, pieces, out_pieces, w, wo, toks, wide, qkv, spins, turns, turns_page, pick, pick_out,
    rows, bias, fresh, q, kv, keep, keep_ml, lend, lend_ml, lent, lent_ml, pair, pair_ml,
    o_all, ml_all, own, att, out, here, there, own_table, load_sem, table_send, table_recv, t_send, t_recv,
    y_send, y_recv, yo_send, yo_recv, m_send, m_recv, k_send, k_recv,
    q_send, f_send, q_recv, kv_send, kv_recv, l_send, l_recv, lm_send, lm_recv, o_send, o_recv, ml_send, ml_recv,
    a_send, a_recv, h_send, h_recv, *weight_sems,
):
    req, seq = place()
    y = req // 8
    zh, c = seq // 2, seq % 2
    other = 2 * zh + 1 - c
    far = (req + 16) % 32
    weights = Weights(pieces, w, *weight_sems[:4])
    out_weights = Weights(out_pieces, wo, *weight_sems[4:])
    met = greet(weights.partners() + [((req + 8 * d) % 32, seq) for d in (1, 2, 3)])
    stored = ((turns_hbm, turns), (turns_page_hbm, turns_page), (pick_hbm, pick), (pick_out_hbm, pick_out), (pool, rows))
    loads = [pltpu.make_async_copy(source, held, load_sem.at[i]) for i, (source, held) in enumerate(stored)]
    for load in loads:
        load.start()
    last = project[8:12].astype(jnp.float32)
    joint[...] = jnp.concatenate(
        [project[0:8].astype(jnp.float32), jnp.concatenate([last[:, :1024], last[:, 1024:]], axis=0)], axis=1
    ).astype(jnp.bfloat16)
    lane = lax.broadcasted_iota(jnp.int32, (8, 128), 1)
    entries = jnp.zeros((8, 128), jnp.int32)
    for j in range(8):
        entries = jnp.where(lane == j, table[0, j], entries)
    own_table[...] = entries
    met()

    order = (2, 1, 3)
    y_copies = begin(
        [remote(joint, pieces.at[y], y_send.at[d - 1], y_recv.at[y], (req + 8 * d) % 32, seq) for d in order]
        + [
            remote(out_project, out_pieces.at[y], yo_send.at[d - 1], yo_recv.at[y], (req + 8 * d) % 32, seq)
            for d in order
        ]
    )
    pages = [remote(pool.at[i], raw.at[i], m_send.at[i], m_recv.at[i], far, seq) for i in range(8)]
    migration = begin([remote(own_table, far_table, table_send, table_recv, far, seq)] + pages[: 8 - HELD])
    pltpu.make_async_copy(joint, pieces.at[y], y_recv.at[y]).start()
    pltpu.make_async_copy(out_project, out_pieces.at[y], yo_recv.at[y]).start()
    normed[...] = layer_norm(hidden[...].astype(jnp.float32)).astype(jnp.bfloat16)
    for load in loads[:4]:
        load.wait()
    length = lengths[req]
    for page in range(8):
        left = jnp.int32(0)
        for j in range(8):
            left = jnp.where(table[0, j] == page, jnp.maximum(left, length - (j * 8 + seq) * 128), left)
        bias[page * 128 : page * 128 + 128] = jnp.where(
            lax.broadcasted_iota(jnp.int32, (128, 1), 0) < left, 0.0, MASKED
        ).astype(jnp.float32)
    coarse, fine = length // 256, length % 256
    cosine_page, sine_page = turns_page[0, pl.ds(coarse, 1)], turns_page[1, pl.ds(coarse, 1)]
    cosine_row, sine_row = turns[0, pl.ds(fine, 1)], turns[1, pl.ds(fine, 1)]
    cosine_start = cosine_page * cosine_row - sine_page * sine_row
    sine_start = sine_page * cosine_row + cosine_page * sine_row
    spins[0] = cosine_start * turns[0] - sine_start * turns[1]
    sine = sine_start * turns[0] + cosine_start * turns[1]
    spins[1] = jnp.where(lax.broadcasted_iota(jnp.int32, (256, 128), 1) < 64, -sine, sine)
    token = seq * 32 + lax.broadcasted_iota(jnp.int32, (32, 256), 0)
    fresh[...] = jnp.where(token <= lax.broadcasted_iota(jnp.int32, (32, 256), 1), 0.0, MASKED).astype(jnp.float32)
    copies = spread(normed, toks, req, seq, k_send, k_recv, (1, 3))
    weights.along_z(y_recv)
    copies += spread(normed, toks, req, seq, k_send, k_recv, (2,), False)
    weights.along_x()
    copies += pass_on(toks, req, seq, k_send, k_recv)

    across = (((1,), (1,)), ((), ()))
    down = (((0,), (0,)), ((), ()))
    f32 = jnp.float32

    def multiply(n, _):
        columns = pl.ds(pl.multiple_of(n * 128, 128), 128)
        some = pl.ds(n * 16, 16)
        tokens = toks[...].reshape(256, 2048)
        tail = w[some, :, 2048:3072].reshape(128, 1024)
        wide[0, :, columns] = lax.dot_general(
            tokens, w[some, :, 0:2048].reshape(128, 2048), across, preferred_element_type=f32
        )
        wide[1, :, columns] = lax.dot_general(tokens[:, :1024], tail, across, preferred_element_type=f32)
        wide[2, :, columns] = lax.dot_general(tokens[:, 1024:], tail, across, preferred_element_type=f32)
        return 0

    lax.fori_loop(0, 2, multiply, 0)
    projected = jnp.zeros((256, 384), f32)
    for part in range(3):
        whole = wide[part]
        high = whole.astype(jnp.bfloat16)
        rest = whole - high.astype(f32)
        middle = rest.astype(jnp.bfloat16)
        low = (rest - middle.astype(f32)).astype(jnp.bfloat16)
        picked = [jnp.dot(piece, pick[part], preferred_element_type=f32) for piece in (middle, low, high)]
        projected += picked[0] + picked[1] + picked[2]
    for j in range(3):
        block = projected[:, j * HEAD : (j + 1) * HEAD]
        turned = block * spins[0] + pltpu.roll(block, 64, 1) * spins[1]
        qkv[j] = jnp.where(3 * seq + j < 2 * HEADS, turned, block).astype(jnp.bfloat16)
    finish(copies)
    finish(y_copies)
    weights.finish()

    def q_copies(j, head):
        copies = [
            remote(qkv.at[j], q.at[head], q_send.at[j * 4 + dz - 1], q_recv.at[head], req, (zh + dz) % 4 * 2 + c)
            for dz in (2, 1, 3)
        ]
        return copies + [remote(qkv.at[j], q.at[head], q_send.at[j * 4 + 3], q_recv.at[head], req, other)]

    def kv_copies(j, slot):
        copies = []
        for dp in range(1, 8):
            p = (seq + dp) % 8
            part = pl.ds(pl.multiple_of(32 * p, 32), 32)
            copies.append(
                remote(qkv.at[j, part], kv.at[slot], kv_send.at[j * 7 + dp - 1], kv_recv.at[slot], req, p)
            )
        return copies

    for j in range(3):
        slot = 3 * seq + j

        @pl.when(slot < HEADS)
        def _():
            begin(q_copies(j, slot))
            pltpu.make_async_copy(qkv.at[j], q.at[slot], q_recv.at[slot]).start()

        @pl.when(slot >= HEADS)
        def _():
            begin(kv_copies(j, slot - HEADS))
            part = pl.ds(pl.multiple_of(32 * seq, 32), 32)
            pltpu.make_async_copy(qkv.at[j, part], kv.at[slot - HEADS], kv_recv.at[slot - HEADS]).start()

    out_weights.along_z(yo_recv)
    loads[4].wait()

    def head_of(k):
        return k % 3 * 3 + k // 3

    def forward(head):
        return remote(q.at[head], q.at[head], f_send.at[head], q_recv.at[head], req, other)

    def passes(head):
        owner = head // 3
        return (c == owner % 2) & (zh != owner // 2)

    def loans(g):
        return [
            remote(lend_ml.at[g], lent_ml.at[g], lm_send.at[g], lm_recv.at[g], req, other),
            remote(lend.at[g], lent.at[g], l_send.at[g], l_recv.at[g], req, other),
        ]

    def o_copies(g):
        lane = 2 * g + c
        return [
            remote(pair_ml.at[g], ml_all.at[zh], ml_send.at[g], ml_recv.at[zh], req, lane),
            remote(pair.at[g], o_all.at[zh], o_send.at[g], o_recv.at[zh], req, lane),
        ]

    def deal(g):
        @pl.when(g == zh)
        def _():
            pltpu.make_async_copy(pair_ml.at[g], ml_all.at[zh], ml_recv.at[zh]).start()
            pltpu.make_async_copy(pair.at[g], o_all.at[zh], o_recv.at[zh]).start()

        @pl.when(g != zh)
        def _():
            begin(o_copies(g))

    def join(g):
        landed(lent_ml.at[g], lm_recv.at[g])
        landed(lent.at[g], l_recv.at[g])
        first, second = keep_ml[g], lent_ml[g]
        top = jnp.maximum(first[0:1], second[0:1])
        mine, theirs = jnp.exp(first[0:1] - top), jnp.exp(second[0:1] - top)
        pair[g] = (mine * keep[g] + theirs * lent[g].astype(jnp.float32)).astype(jnp.bfloat16)
        pair_ml[g] = jnp.concatenate(
            [top, mine * first[1:2] + theirs * second[1:2], jnp.zeros((6, 256), jnp.float32)], axis=0
        )

    scale = HEAD ** (-0.5)

    def attend(head):
        landed(q.at[head], q_recv.at[head])

        @pl.when(passes(head))
        def _():
            forward(head).start()

        landed(kv.at[head], kv_recv.at[head])
        landed(kv.at[head + 8], kv_recv.at[head + 8])
        keys = rows[:, :, pl.ds(pl.multiple_of(head * 128, 128), 128)].reshape(1024, 128)
        values = rows[:, :, pl.ds(pl.multiple_of(head * 128 + 1024, 128), 128)].reshape(1024, 128)
        query = q[head]
        s = lax.dot_general(keys, query, across, preferred_element_type=jnp.float32) * scale + bias[...]
        sn = lax.dot_general(kv[head], query, across, preferred_element_type=jnp.float32) * scale + fresh[...]
        highest = jnp.maximum(jnp.max(s, axis=0, keepdims=True), jnp.max(sn, axis=0, keepdims=True))
        p = jnp.exp(s - highest)
        pn = jnp.exp(sn - highest)
        totals = jnp.sum(p, axis=0, keepdims=True) + jnp.sum(pn, axis=0, keepdims=True)
        summed = lax.dot_general(values, p.astype(jnp.bfloat16), down, preferred_element_type=jnp.float32)
        summed += lax.dot_general(kv[head + 8], pn.astype(jnp.bfloat16), down, preferred_element_type=jnp.float32)
        state = jnp.concatenate([highest, totals, jnp.zeros((6, 256), jnp.float32)], axis=0)
        g = head // 2

        @pl.when(head % 2 == c)
        def _():
            keep[g] = summed
            keep_ml[g] = state

        @pl.when(head % 2 != c)
        def _():
            lend[g] = summed.astype(jnp.bfloat16)
            lend_ml[g] = state

    def step(k, _):
        @pl.when(k < 8)
        def _():
            attend(head_of(k))

        def head_at(lag):
            return head_of(jnp.clip(k - lag, 0, 7))

        def due(lag, ours):
            mine = head_at(lag) % 2 == c
            return (k >= lag) & (k < 8 + lag) & (mine if ours else jnp.logical_not(mine))

        @pl.when(due(1, False))
        def _():
            begin(loans(head_at(1) // 2))

        @pl.when(due(3, True))
        def _():
            deal(head_at(3) // 2)

        @pl.when(due(2, True))
        def _():
            join(head_at(2) // 2)

        return 0

    lax.fori_loop(0, 11, step, 0)
    out_weights.along_x()

    for chip in range(4):
        landed(ml_all.at[chip], ml_recv.at[chip])
        landed(o_all.at[chip], o_recv.at[chip])
    top = ml_all[0, 0:1]
    for chip in range(1, 4):
        top = jnp.maximum(top, ml_all[chip, 0:1])
    summed = jnp.zeros((128, 256), jnp.float32)
    total = jnp.zeros((1, 256), jnp.float32)
    for chip in range(4):
        factor = jnp.exp(ml_all[chip, 0:1] - top)
        total += factor * ml_all[chip, 1:2]
        summed += factor * o_all[chip].astype(jnp.float32)
    own[...] = (summed / total).astype(jnp.bfloat16)
    for head in range(HEADS):
        @pl.when(passes(head))
        def _():
            forward(head).wait_send()

    for g in range(4):
        finish(loans(g))

        @pl.when(g != zh)
        def _():
            finish(o_copies(g))

    copies = spread(own, att, req, seq, a_send, a_recv)
    copies += pass_on(att, req, seq, a_send, a_recv)

    product = lax.dot_general(
        att[...].reshape(1024, 256), wo[...].reshape(256, 1024), (((0,), (1,)), ((), ())), preferred_element_type=f32
    ).astype(jnp.bfloat16)
    out[...] = jnp.dot(product, pick_out[...], preferred_element_type=f32).astype(jnp.bfloat16)
    finish(copies)
    for j in range(3):
        slot = 3 * seq + j

        @pl.when(slot < HEADS)
        def _():
            finish(q_copies(j, slot))

        @pl.when(slot >= HEADS)
        def _():
            finish(kv_copies(j, slot - HEADS))

    out_weights.finish()
    mine = pl.ds(pl.multiple_of(256 * seq, 256), 256)
    copies = []
    for dp in (4, 3, 5, 2, 6, 1, 7):
        p = (seq + dp) % 8
        part = pl.ds(pl.multiple_of(32 * p, 32), 32)
        copies.append(remote(out.at[part], here.at[:, mine], h_send.at[dp], h_recv.at[seq], req, p))
    begin(copies)
    part = pl.ds(pl.multiple_of(32 * seq, 32), 32)
    pltpu.make_async_copy(out.at[part], here.at[:, mine], h_recv.at[seq]).start()
    for lane in range(8):
        landed(here.at[:, pl.ds(256 * lane, 256)], h_recv.at[lane])
    copies += begin([remote(here, there, t_send, t_recv, far, seq)])
    migration += begin(pages[8 - HELD :])
    finish(copies)
    landed(there, t_recv)
    result[...] = jnp.where(targets[req] != req, there[...], here[...])
    landed(far_table, table_recv)
    for i in range(8):
        landed(raw.at[i], m_recv.at[i])
    finish(migration)


def pages_kernel(table, lengths, targets, pool, out, buf, read_sem, write_sem):
    req, seq = place()
    length = jnp.where(targets[req] != req, lengths[(req + 16) % 32], 0)
    for j in range(8):

        @pl.when(length > (j * 8 + seq) * 128)
        def _():
            pltpu.make_async_copy(pool.at[table[0, j]], buf.at[j], read_sem.at[j]).start()

    for j in range(8):
        left = length - (j * 8 + seq) * 128

        @pl.when(left > 0)
        def _():
            pltpu.make_async_copy(pool.at[0], buf.at[j], read_sem.at[j]).wait()

        @pl.when((left > 0) & (left < 128))
        def _():
            row = lax.broadcasted_iota(jnp.int32, (128, 2048), 0)
            buf[j] = jnp.where(row < left, buf[j], jnp.zeros((128, 2048), jnp.bfloat16))

        @pl.when(left <= 0)
        def _():
            buf[j] = jnp.zeros((128, 2048), jnp.bfloat16)

        pltpu.make_async_copy(buf.at[j], out.at[j], write_sem.at[j]).start()
    for j in range(8):
        pltpu.make_async_copy(buf.at[j], out.at[j], write_sem.at[j]).wait()


def shape(dims, dtype=jnp.bfloat16):
    return jax.ShapeDtypeStruct(dims, dtype)


def vmem(*dims, dtype=jnp.bfloat16):
    return pltpu.VMEM(dims, dtype)


def tables():
    frequency = np.exp(-math.log(10000.0) * 2.0 * np.arange(64) / HEAD)
    frequency = np.concatenate([frequency, frequency])
    step = np.arange(256)[:, None] * frequency
    page = 256.0 * np.arange(40)[:, None] * frequency
    turns = np.stack([np.cos(step), np.sin(step)]).astype(np.float32)
    turns_page = np.stack([np.cos(page), np.sin(page)]).astype(np.float32)
    row = np.arange(256)
    slot, entry = row // 8, row % 8
    piece = slot // 16 * 16 + slot // 2 % 2 * 8 + slot // 4 % 4 * 2 + slot % 2
    columns = (
        piece * 12 + entry,
        np.where(entry < 4, piece * 12 + 8 + entry, -1),
        np.where(entry >= 4, piece * 12 + 4 + entry, -1),
    )
    pick = np.stack([column[:, None] == np.arange(384) for column in columns])
    pick_out = (piece * 8 + entry)[:, None] == np.arange(256)
    return turns, turns_page, pick, pick_out


def local(hidden, project_weight, output_weight, cache_pool, page_table, cache_length, target_slot):
    anywhere = pl.BlockSpec(memory_space=pl.ANY)
    scalars = pl.BlockSpec(memory_space=pltpu.SMEM)
    turns, turns_page, pick, pick_out = tables()
    f32 = jnp.float32
    attention_out, raw, far_table = pl.pallas_call(
        layer_kernel,
        out_shape=(shape((32, 2048)), shape((8, 128, 2048)), shape((8, 128), jnp.int32)),
        in_specs=[VMEM] * 3 + [anywhere] + [scalars] * 3 + [anywhere] * 4,
        out_specs=(VMEM, anywhere, VMEM),
        scratch_shapes=[
            vmem(8, 3072), vmem(32, 2048), vmem(4, 8, 3072), vmem(4, 8, 1024),
            vmem(32, 8, 3072), vmem(32, 8, 1024), vmem(8, 32, 2048),
            vmem(3, 256, 256, dtype=f32), vmem(3, 256, 128), vmem(2, 256, 128, dtype=f32),
            vmem(2, 256, 128, dtype=f32), vmem(2, 40, 128, dtype=f32), vmem(3, 256, 384), vmem(256, 256),
            vmem(8, 128, 2048), vmem(1024, 1, dtype=f32), vmem(32, 256, dtype=f32),
            vmem(8, 256, 128), vmem(16, 32, 128),
            vmem(4, 128, 256, dtype=f32), vmem(4, 8, 256, dtype=f32),
            vmem(4, 128, 256), vmem(4, 8, 256, dtype=f32),
            vmem(4, 128, 256), vmem(4, 8, 256, dtype=f32),
            vmem(4, 128, 256), vmem(4, 8, 256, dtype=f32),
            vmem(4, 128, 256), vmem(4, 8, 256, dtype=f32),
            vmem(128, 256), vmem(8, 128, 256), vmem(256, 256), vmem(32, 2048), vmem(32, 2048),
            vmem(8, 128, dtype=jnp.int32), DMA((5,)), DMA, DMA, DMA, DMA,
            DMA((3,)), DMA((4,)), DMA((3,)), DMA((4,)), DMA((8,)), DMA((8,)), DMA((7,)), DMA((8,)),
            DMA((12,)), DMA((8,)), DMA((8,)), DMA((21,)), DMA((16,)),
            DMA((4,)), DMA((4,)), DMA((4,)), DMA((4,)), DMA((4,)), DMA((4,)), DMA((4,)), DMA((4,)),
            DMA((7,)), DMA((8,)), DMA((8,)), DMA((8,)),
        ] + WEIGHT_SEMS * 2,
        compiler_params=pltpu.CompilerParams(collective_id=1, has_side_effects=True),
        name="layer",
    )(
        hidden[0], project_weight.T, output_weight.T, cache_pool.reshape(8, 128, 2048),
        page_table, cache_length, target_slot,
        jnp.asarray(turns), jnp.asarray(turns_page), jnp.asarray(pick, jnp.bfloat16), jnp.asarray(pick_out, jnp.bfloat16),
    )
    arrived = pl.pallas_call(
        pages_kernel,
        out_shape=shape((8, 128, 2048)),
        in_specs=[scalars] * 3 + [anywhere],
        out_specs=anywhere,
        scratch_shapes=[vmem(8, 128, 2048), DMA((8,)), DMA((8,))],
        name="pages",
    )(far_table, cache_length, target_slot, raw)
    return attention_out[None], arrived.reshape(1, 1024, 2048)


def solution(mesh):
    placed = (
        P("req", "seq", None),
        P(None, ("req", "seq")),
        P(None, ("req", "seq")),
        P("req", "seq", None, None, None),
        P("req", "seq"),
        P(),
        P(),
    )
    return jax.shard_map(
        local,
        mesh=mesh,
        in_specs=placed,
        out_specs=(P("req", "seq", None), P("req", "seq", None)),
        check_vma=False,
    )
```

```python
import functools
import math

import jax
import jax.numpy as jnp
import numpy as np
from jax import lax
from jax.experimental import pallas as pl
from jax.experimental.pallas import tpu as pltpu
from jax.sharding import PartitionSpec as P

HEAD = 128
HEADS = 8
MESH = pl.DeviceIdType.MESH
EPSILON = 1e-05
MASKED = -1e30
EARLY = 96
VMEM = pl.BlockSpec(memory_space=pltpu.VMEM)
DMA = pltpu.SemaphoreType.DMA


def place():
    return lax.axis_index("req"), lax.axis_index("seq")


def greet(devices):
    barrier = pltpu.get_barrier_semaphore()
    for req, seq in devices:
        pl.semaphore_signal(barrier, inc=1, device_id=(req, seq), device_id_type=MESH)
    return lambda: pl.semaphore_wait(barrier, len(devices))


def remote(src, dst, send, recv, req, seq):
    return pltpu.make_async_remote_copy(
        src_ref=src, dst_ref=dst, send_sem=send, recv_sem=recv,
        device_id=(req, seq), device_id_type=MESH,
    )


def landed(dst, sem):
    pltpu.make_async_copy(dst, dst, sem).wait()


def begin(copies):
    for copy in copies:
        copy.start()
    return copies


def finish(copies):
    for copy in copies:
        copy.wait_send()


def spread(own, out, req, seq, send, recv, steps=(2, 1, 3), near=True):
    zh, c = seq // 2, seq % 2
    copies = [
        remote(own, out.at[seq], send.at[dz - 1], recv.at[seq], req, (zh + dz) % 4 * 2 + c)
        for dz in steps
    ]
    if near:
        copies.append(remote(own, out.at[seq], send.at[3], recv.at[seq], req, 2 * zh + 1 - c))
        pltpu.make_async_copy(own, out.at[seq], recv.at[seq]).start()
    return begin(copies)


def pass_on(out, req, seq, send, recv):
    zh, c = seq // 2, seq % 2
    copies = []
    for dz in (1, 3, 2):
        source = (zh + dz) % 4 * 2 + c
        landed(out.at[source], recv.at[source])
        copies += begin(
            [remote(out.at[source], out.at[source], send.at[3 + dz], recv.at[source], req, 2 * zh + 1 - c)]
        )
    for dz in (0, 1, 3, 2):
        source = (zh + dz) % 4 * 2 + 1 - c
        landed(out.at[source], recv.at[source])
    landed(out.at[seq], recv.at[seq])
    return copies


NEAREST = (0, 1, 3, 2)


class Weights:
    def __init__(self, pieces, w, z_send, z_recv, x_send, x_recv):
        self.pieces, self.w = pieces, w
        self.z_send, self.z_recv, self.x_send, self.x_recv = z_send, z_recv, x_send, x_recv
        self.req, self.seq = req, seq = place()
        self.y, self.x, self.zl = req // 8, req // 2 % 4, req % 2
        self.zh, self.c = seq // 2, seq % 2
        self.line = self.zh * 4 + self.zl * 2 + self.c
        self.slot = self.x % 2 * 16 + self.line

    def partners(self):
        found = [(self.y * 8 + (self.x + dx) % 4 * 2 + self.zl, self.seq) for dx in (1, 2, 3)]
        for k in range(1, 16):
            there = (self.zl * 8 + self.seq + k) % 16
            found.append((self.y * 8 + self.x * 2 + there // 8, there % 8))
        return found

    def z_copy(self, e, b):
        zh = (self.zh + e) % 4
        target = zh * 2 + self.x // 2
        there = self.y * 8 + self.x * 2 + (self.zl + b) % 2
        copy = remote(
            self.pieces.at[zh], self.w.at[self.slot], self.z_send.at[e * 2 + b], self.z_recv.at[self.line], there, target
        )
        return copy, target

    def along_z(self, y_recv):
        for e in NEAREST:
            zh = (self.zh + e) % 4
            landed(self.pieces.at[zh], y_recv.at[zh])
            copy, target = self.z_copy(e, 0)
            if e:
                copy.start()
            else:

                @pl.when(target == self.seq)
                def _():
                    pltpu.make_async_copy(
                        self.pieces.at[self.zh], self.w.at[self.slot], self.z_recv.at[self.line]
                    ).start()

                @pl.when(target != self.seq)
                def _():
                    copy.start()

            self.z_copy(e, 1)[0].start()

    def chunk(self, i):
        return (self.zh - NEAREST[i]) % 4

    def x_copy(self, h, i, step):
        k = self.chunk(i)
        block = self.w.at[pl.ds(h * 16 + 4 * k, 4)]
        there = self.y * 8 + (self.x + step) % 4 * 2 + self.zl
        return remote(block, block, self.x_send.at[(step + 1) // 2 * 8 + h * 4 + i], self.x_recv.at[h * 4 + k], there, self.seq)

    def arrived(self, h, i):
        k = self.chunk(i)
        landed(self.w.at[pl.ds(h * 16 + 4 * k, 4)], self.x_recv.at[h * 4 + k])

    def hops(self, h):
        return (self.x - 2 * self.c - h) % 4

    def along_x(self):
        for h in range(2):

            @pl.when(self.hops(h) == 0)
            def _():
                for i in range(4):
                    k = self.chunk(i)
                    for n in range(4):
                        landed(self.w.at[h * 16 + 4 * k + n], self.z_recv.at[4 * k + n])
                    self.x_copy(h, i, 1).start()
                    self.x_copy(h, i, -1).start()

        for i in range(4):
            step = 1 if i % 2 == 0 else -1
            for h in range(2):

                @pl.when((self.hops(h) == 1) | (self.hops(h) == 3))
                def _():
                    self.arrived(h, i)

                @pl.when(self.hops(h) == step % 4)
                def _():
                    self.x_copy(h, i, step).start()

        for h in range(2):

            @pl.when(self.hops(h) == 2)
            def _():
                for i in range(4):
                    self.arrived(h, i)

    def finish(self):
        for e in range(4):
            self.z_copy(e, 1)[0].wait_send()
            copy, target = self.z_copy(e, 0)
            if e:
                copy.wait_send()
            else:

                @pl.when(target != self.seq)
                def _():
                    copy.wait_send()

        for h in range(2):
            for i in range(4):
                step = 1 if i % 2 == 0 else -1

                @pl.when((self.hops(h) == 0) | (self.hops(h) == step % 4))
                def _():
                    self.x_copy(h, i, step).wait_send()

                @pl.when(self.hops(h) == 0)
                def _():
                    self.x_copy(h, i, -step).wait_send()


WEIGHT_SEMS = [DMA((8,)), DMA((16,)), DMA((16,)), DMA((8,))]


def layer_norm(row_block):
    row_mean = jnp.mean(row_block, axis=-1, keepdims=True)
    centred = row_block - row_mean
    variance = jnp.mean(centred * centred, axis=-1, keepdims=True)
    return centred / jnp.sqrt(variance + EPSILON)


def layer_kernel(
    hidden, project, out_project, pool, table, lengths, turns_hbm, turns_page_hbm, pick_hbm, pick_out_hbm,
    here, raw, far_table,
    joint, normed, pieces, out_pieces, w, wo, toks, wide, qkv, spins, turns, turns_page, pick, pick_out,
    rows, bias, fresh, q, kv, keep, keep_ml, lend, lend_ml, lent, lent_ml, pair, pair_ml,
    o_all, ml_all, own, att, out, own_table, load_sem, table_send, table_recv,
    y_send, y_recv, yo_send, yo_recv, m_send, m_recv, k_send, k_recv,
    q_send, f_send, q_recv, kv_send, kv_recv, l_send, l_recv, lm_send, lm_recv, o_send, o_recv, ml_send, ml_recv,
    a_send, a_recv, h_send, h_recv, *weight_sems,
):
    req, seq = place()
    y = req // 8
    zh, c = seq // 2, seq % 2
    other = 2 * zh + 1 - c
    far = (req + 16) % 32
    weights = Weights(pieces, w, *weight_sems[:4])
    out_weights = Weights(out_pieces, wo, *weight_sems[4:])
    met = greet(weights.partners() + [((req + 8 * d) % 32, seq) for d in (1, 2, 3)])
    stored = ((turns_hbm, turns), (turns_page_hbm, turns_page), (pick_hbm, pick), (pick_out_hbm, pick_out), (pool, rows))
    loads = [pltpu.make_async_copy(source, held, load_sem.at[i]) for i, (source, held) in enumerate(stored)]
    for load in loads:
        load.start()
    last = project[8:12].astype(jnp.float32)
    joint[...] = jnp.concatenate(
        [project[0:8].astype(jnp.float32), jnp.concatenate([last[:, :1024], last[:, 1024:]], axis=0)], axis=1
    ).astype(jnp.bfloat16)
    lane = lax.broadcasted_iota(jnp.int32, (8, 128), 1)
    entries = jnp.zeros((8, 128), jnp.int32)
    for j in range(8):
        entries = jnp.where(lane == j, table[0, j], entries)
    own_table[...] = entries
    met()

    order = (2, 1, 3)
    y_copies = begin(
        [remote(joint, pieces.at[y], y_send.at[d - 1], y_recv.at[y], (req + 8 * d) % 32, seq) for d in order]
        + [
            remote(out_project, out_pieces.at[y], yo_send.at[d - 1], yo_recv.at[y], (req + 8 * d) % 32, seq)
            for d in order
        ]
    )
    migration = [remote(own_table, far_table, table_send, table_recv, far, seq)]
    later = pl.ds(EARLY, 128 - EARLY)
    migration.append(remote(pool.at[0, later], raw.at[0, later], m_send.at[0], m_recv.at[0], far, seq))
    migration += [remote(pool.at[i], raw.at[i], m_send.at[i], m_recv.at[i], far, seq) for i in range(1, 8)]
    begin(migration)
    pltpu.make_async_copy(joint, pieces.at[y], y_recv.at[y]).start()
    pltpu.make_async_copy(out_project, out_pieces.at[y], yo_recv.at[y]).start()
    normed[...] = layer_norm(hidden[...].astype(jnp.float32)).astype(jnp.bfloat16)
    for load in loads[:4]:
        load.wait()
    length = lengths[req]
    for page in range(8):
        left = jnp.int32(0)
        for j in range(8):
            left = jnp.where(table[0, j] == page, jnp.maximum(left, length - (j * 8 + seq) * 128), left)
        bias[page * 128 : page * 128 + 128] = jnp.where(
            lax.broadcasted_iota(jnp.int32, (128, 1), 0) < left, 0.0, MASKED
        ).astype(jnp.float32)
    coarse, fine = length // 256, length % 256
    cosine_page, sine_page = turns_page[0, pl.ds(coarse, 1)], turns_page[1, pl.ds(coarse, 1)]
    cosine_row, sine_row = turns[0, pl.ds(fine, 1)], turns[1, pl.ds(fine, 1)]
    cosine_start = cosine_page * cosine_row - sine_page * sine_row
    sine_start = sine_page * cosine_row + cosine_page * sine_row
    spins[0] = cosine_start * turns[0] - sine_start * turns[1]
    sine = sine_start * turns[0] + cosine_start * turns[1]
    spins[1] = jnp.where(lax.broadcasted_iota(jnp.int32, (256, 128), 1) < 64, -sine, sine)
    token = seq * 32 + lax.broadcasted_iota(jnp.int32, (32, 256), 0)
    fresh[...] = jnp.where(token <= lax.broadcasted_iota(jnp.int32, (32, 256), 1), 0.0, MASKED).astype(jnp.float32)
    copies = spread(normed, toks, req, seq, k_send, k_recv, (1, 3))
    weights.along_z(y_recv)
    copies += spread(normed, toks, req, seq, k_send, k_recv, (2,), False)
    out_weights.along_z(yo_recv)
    weights.along_x()
    copies += pass_on(toks, req, seq, k_send, k_recv)

    across = (((1,), (1,)), ((), ()))
    down = (((0,), (0,)), ((), ()))
    f32 = jnp.float32

    def multiply(n, _):
        columns = pl.ds(pl.multiple_of(n * 128, 128), 128)
        some = pl.ds(n * 16, 16)
        tokens = toks[...].reshape(256, 2048)
        tail = w[some, :, 2048:3072].reshape(128, 1024)
        wide[0, :, columns] = lax.dot_general(
            tokens, w[some, :, 0:2048].reshape(128, 2048), across, preferred_element_type=f32
        )
        wide[1, :, columns] = lax.dot_general(tokens[:, :1024], tail, across, preferred_element_type=f32)
        wide[2, :, columns] = lax.dot_general(tokens[:, 1024:], tail, across, preferred_element_type=f32)
        return 0

    lax.fori_loop(0, 2, multiply, 0)
    projected = jnp.zeros((256, 384), f32)
    for part in range(3):
        whole = wide[part]
        high = whole.astype(jnp.bfloat16)
        rest = whole - high.astype(f32)
        middle = rest.astype(jnp.bfloat16)
        low = (rest - middle.astype(f32)).astype(jnp.bfloat16)
        picked = [jnp.dot(piece, pick[part], preferred_element_type=f32) for piece in (middle, low, high)]
        projected += picked[0] + picked[1] + picked[2]
    for j in range(3):
        block = projected[:, j * HEAD : (j + 1) * HEAD]
        turned = block * spins[0] + pltpu.roll(block, 64, 1) * spins[1]
        qkv[j] = jnp.where(3 * seq + j < 2 * HEADS, turned, block).astype(jnp.bfloat16)
    finish(copies)
    finish(y_copies)
    weights.finish()

    def q_copies(j, head):
        copies = [
            remote(qkv.at[j], q.at[head], q_send.at[j * 4 + dz - 1], q_recv.at[head], req, (zh + dz) % 4 * 2 + c)
            for dz in (2, 1, 3)
        ]
        return copies + [remote(qkv.at[j], q.at[head], q_send.at[j * 4 + 3], q_recv.at[head], req, other)]

    def kv_copies(j, slot):
        copies = []
        for dp in range(1, 8):
            p = (seq + dp) % 8
            part = pl.ds(pl.multiple_of(32 * p, 32), 32)
            copies.append(
                remote(qkv.at[j, part], kv.at[slot], kv_send.at[j * 7 + dp - 1], kv_recv.at[slot], req, p)
            )
        return copies

    for j in range(3):
        slot = 3 * seq + j

        @pl.when(slot < HEADS)
        def _():
            begin(q_copies(j, slot))
            pltpu.make_async_copy(qkv.at[j], q.at[slot], q_recv.at[slot]).start()

        @pl.when(slot >= HEADS)
        def _():
            begin(kv_copies(j, slot - HEADS))
            part = pl.ds(pl.multiple_of(32 * seq, 32), 32)
            pltpu.make_async_copy(qkv.at[j, part], kv.at[slot - HEADS], kv_recv.at[slot - HEADS]).start()

    out_weights.along_x()
    loads[4].wait()

    def head_of(k):
        return k % 3 * 3 + k // 3

    def forward(head):
        return remote(q.at[head], q.at[head], f_send.at[head], q_recv.at[head], req, other)

    def passes(head):
        owner = head // 3
        return (c == owner % 2) & (zh != owner // 2)

    def loans(g):
        return [
            remote(lend_ml.at[g], lent_ml.at[g], lm_send.at[g], lm_recv.at[g], req, other),
            remote(lend.at[g], lent.at[g], l_send.at[g], l_recv.at[g], req, other),
        ]

    def o_copies(g):
        lane = 2 * g + c
        return [
            remote(pair_ml.at[g], ml_all.at[zh], ml_send.at[g], ml_recv.at[zh], req, lane),
            remote(pair.at[g], o_all.at[zh], o_send.at[g], o_recv.at[zh], req, lane),
        ]

    def deal(g):
        @pl.when(g == zh)
        def _():
            pltpu.make_async_copy(pair_ml.at[g], ml_all.at[zh], ml_recv.at[zh]).start()
            pltpu.make_async_copy(pair.at[g], o_all.at[zh], o_recv.at[zh]).start()

        @pl.when(g != zh)
        def _():
            begin(o_copies(g))

    def join(g):
        landed(lent_ml.at[g], lm_recv.at[g])
        landed(lent.at[g], l_recv.at[g])
        first, second = keep_ml[g], lent_ml[g]
        top = jnp.maximum(first[0:1], second[0:1])
        mine, theirs = jnp.exp(first[0:1] - top), jnp.exp(second[0:1] - top)
        pair[g] = (mine * keep[g] + theirs * lent[g].astype(jnp.float32)).astype(jnp.bfloat16)
        pair_ml[g] = jnp.concatenate(
            [top, mine * first[1:2] + theirs * second[1:2], jnp.zeros((6, 256), jnp.float32)], axis=0
        )

    scale = HEAD ** (-0.5)

    def attend(head):
        landed(q.at[head], q_recv.at[head])

        @pl.when(passes(head))
        def _():
            forward(head).start()

        landed(kv.at[head], kv_recv.at[head])
        landed(kv.at[head + 8], kv_recv.at[head + 8])
        keys = rows[:, :, pl.ds(pl.multiple_of(head * 128, 128), 128)].reshape(1024, 128)
        values = rows[:, :, pl.ds(pl.multiple_of(head * 128 + 1024, 128), 128)].reshape(1024, 128)
        query = q[head]
        s = lax.dot_general(keys, query, across, preferred_element_type=jnp.float32) * scale + bias[...]
        sn = lax.dot_general(kv[head], query, across, preferred_element_type=jnp.float32) * scale + fresh[...]
        highest = jnp.maximum(jnp.max(s, axis=0, keepdims=True), jnp.max(sn, axis=0, keepdims=True))
        p = jnp.exp(s - highest)
        pn = jnp.exp(sn - highest)
        totals = jnp.sum(p, axis=0, keepdims=True) + jnp.sum(pn, axis=0, keepdims=True)
        summed = lax.dot_general(values, p.astype(jnp.bfloat16), down, preferred_element_type=jnp.float32)
        summed += lax.dot_general(kv[head + 8], pn.astype(jnp.bfloat16), down, preferred_element_type=jnp.float32)
        state = jnp.concatenate([highest, totals, jnp.zeros((6, 256), jnp.float32)], axis=0)
        g = head // 2

        @pl.when(head % 2 == c)
        def _():
            keep[g] = summed
            keep_ml[g] = state

        @pl.when(head % 2 != c)
        def _():
            lend[g] = summed.astype(jnp.bfloat16)
            lend_ml[g] = state

    def step(k, _):
        @pl.when(k < 8)
        def _():
            attend(head_of(k))

        def head_at(lag):
            return head_of(jnp.clip(k - lag, 0, 7))

        def due(lag, ours):
            mine = head_at(lag) % 2 == c
            return (k >= lag) & (k < 8 + lag) & (mine if ours else jnp.logical_not(mine))

        @pl.when(due(1, False))
        def _():
            begin(loans(head_at(1) // 2))

        @pl.when(due(3, True))
        def _():
            deal(head_at(3) // 2)

        @pl.when(due(2, True))
        def _():
            join(head_at(2) // 2)

        return 0

    lax.fori_loop(0, 11, step, 0)

    for chip in range(4):
        landed(ml_all.at[chip], ml_recv.at[chip])
        landed(o_all.at[chip], o_recv.at[chip])
    top = ml_all[0, 0:1]
    for chip in range(1, 4):
        top = jnp.maximum(top, ml_all[chip, 0:1])
    summed = jnp.zeros((128, 256), jnp.float32)
    total = jnp.zeros((1, 256), jnp.float32)
    for chip in range(4):
        factor = jnp.exp(ml_all[chip, 0:1] - top)
        total += factor * ml_all[chip, 1:2]
        summed += factor * o_all[chip].astype(jnp.float32)
    own[...] = (summed / total).astype(jnp.bfloat16)
    for head in range(HEADS):
        @pl.when(passes(head))
        def _():
            forward(head).wait_send()

    for g in range(4):
        finish(loans(g))

        @pl.when(g != zh)
        def _():
            finish(o_copies(g))

    copies = spread(own, att, req, seq, a_send, a_recv)
    copies += pass_on(att, req, seq, a_send, a_recv)

    product = lax.dot_general(
        att[...].reshape(1024, 256), wo[...].reshape(256, 1024), (((0,), (1,)), ((), ())), preferred_element_type=f32
    ).astype(jnp.bfloat16)
    out[...] = jnp.dot(product, pick_out[...], preferred_element_type=f32).astype(jnp.bfloat16)
    finish(copies)
    for j in range(3):
        slot = 3 * seq + j

        @pl.when(slot < HEADS)
        def _():
            finish(q_copies(j, slot))

        @pl.when(slot >= HEADS)
        def _():
            finish(kv_copies(j, slot - HEADS))

    out_weights.finish()
    mine = pl.ds(pl.multiple_of(256 * seq, 256), 256)
    copies = []
    for dp in (4, 3, 5, 2, 6, 1, 7):
        p = (seq + dp) % 8
        part = pl.ds(pl.multiple_of(32 * p, 32), 32)
        copies.append(remote(out.at[part], here.at[:, mine], h_send.at[dp], h_recv.at[seq], req, p))
    begin(copies)
    part = pl.ds(pl.multiple_of(32 * seq, 32), 32)
    pltpu.make_async_copy(out.at[part], here.at[:, mine], h_recv.at[seq]).start()
    for lane in range(8):
        landed(here.at[:, pl.ds(256 * lane, 256)], h_recv.at[lane])
    finish(copies)
    landed(far_table, table_recv)
    landed(raw.at[0, later], m_recv.at[0])
    for i in range(1, 8):
        landed(raw.at[i], m_recv.at[i])
    finish(migration)


def select_kernel(targets, here, there, after, out):
    req = lax.axis_index("req")
    out[...] = jnp.where(targets[req] != req, there[...], here[...])


def pages_kernel(table, lengths, targets, first, pool, out, buf, read_sem, write_sem):
    req, seq = place()
    length = jnp.where(targets[req] != req, lengths[(req + 16) % 32], 0)
    for j in range(8):

        @pl.when(length > (j * 8 + seq) * 128)
        def _():
            page = table[0, j]

            @pl.when(page > 0)
            def _():
                pltpu.make_async_copy(pool.at[page], buf.at[j], read_sem.at[j]).start()

            @pl.when(page == 0)
            def _():
                later = pl.ds(EARLY, 128 - EARLY)
                pltpu.make_async_copy(first, buf.at[j, pl.ds(0, EARLY)], read_sem.at[j]).start()
                pltpu.make_async_copy(pool.at[0, later], buf.at[j, later], read_sem.at[j]).start()

    for j in range(8):
        left = length - (j * 8 + seq) * 128

        @pl.when(left > 0)
        def _():
            pltpu.make_async_copy(pool.at[0], buf.at[j], read_sem.at[j]).wait()

        @pl.when((left > 0) & (left < 128))
        def _():
            row = lax.broadcasted_iota(jnp.int32, (128, 2048), 0)
            buf[j] = jnp.where(row < left, buf[j], jnp.zeros((128, 2048), jnp.bfloat16))

        @pl.when(left <= 0)
        def _():
            buf[j] = jnp.zeros((128, 2048), jnp.bfloat16)

        pltpu.make_async_copy(buf.at[j], out.at[j], write_sem.at[j]).start()
    for j in range(8):
        pltpu.make_async_copy(buf.at[j], out.at[j], write_sem.at[j]).wait()


def shape(dims, dtype=jnp.bfloat16):
    return jax.ShapeDtypeStruct(dims, dtype)


def vmem(*dims, dtype=jnp.bfloat16):
    return pltpu.VMEM(dims, dtype)


def tables():
    frequency = np.exp(-math.log(10000.0) * 2.0 * np.arange(64) / HEAD)
    frequency = np.concatenate([frequency, frequency])
    step = np.arange(256)[:, None] * frequency
    page = 256.0 * np.arange(40)[:, None] * frequency
    turns = np.stack([np.cos(step), np.sin(step)]).astype(np.float32)
    turns_page = np.stack([np.cos(page), np.sin(page)]).astype(np.float32)
    row = np.arange(256)
    slot, entry = row // 8, row % 8
    piece = slot // 16 * 16 + slot // 2 % 2 * 8 + slot // 4 % 4 * 2 + slot % 2
    columns = (
        piece * 12 + entry,
        np.where(entry < 4, piece * 12 + 8 + entry, -1),
        np.where(entry >= 4, piece * 12 + 4 + entry, -1),
    )
    pick = np.stack([column[:, None] == np.arange(384) for column in columns])
    pick_out = (piece * 8 + entry)[:, None] == np.arange(256)
    return turns, turns_page, pick, pick_out


def local(hidden, project_weight, output_weight, cache_pool, page_table, cache_length, target_slot):
    anywhere = pl.BlockSpec(memory_space=pl.ANY)
    scalars = pl.BlockSpec(memory_space=pltpu.SMEM)
    turns, turns_page, pick, pick_out = tables()
    f32 = jnp.float32
    pool = cache_pool.reshape(8, 128, 2048)
    swap = [(i, (i + 16) % 32) for i in range(32)]
    first = lax.ppermute(pool[0, :EARLY], "req", swap)
    here, raw, far_table = pl.pallas_call(
        layer_kernel,
        out_shape=(shape((32, 2048)), shape((8, 128, 2048)), shape((8, 128), jnp.int32)),
        in_specs=[VMEM] * 3 + [anywhere] + [scalars] * 2 + [anywhere] * 4,
        out_specs=(VMEM, anywhere, VMEM),
        scratch_shapes=[
            vmem(8, 3072), vmem(32, 2048), vmem(4, 8, 3072), vmem(4, 8, 1024),
            vmem(32, 8, 3072), vmem(32, 8, 1024), vmem(8, 32, 2048),
            vmem(3, 256, 256, dtype=f32), vmem(3, 256, 128), vmem(2, 256, 128, dtype=f32),
            vmem(2, 256, 128, dtype=f32), vmem(2, 40, 128, dtype=f32), vmem(3, 256, 384), vmem(256, 256),
            vmem(8, 128, 2048), vmem(1024, 1, dtype=f32), vmem(32, 256, dtype=f32),
            vmem(8, 256, 128), vmem(16, 32, 128),
            vmem(4, 128, 256, dtype=f32), vmem(4, 8, 256, dtype=f32),
            vmem(4, 128, 256), vmem(4, 8, 256, dtype=f32),
            vmem(4, 128, 256), vmem(4, 8, 256, dtype=f32),
            vmem(4, 128, 256), vmem(4, 8, 256, dtype=f32),
            vmem(4, 128, 256), vmem(4, 8, 256, dtype=f32),
            vmem(128, 256), vmem(8, 128, 256), vmem(256, 256),
            vmem(8, 128, dtype=jnp.int32), DMA((5,)), DMA, DMA,
            DMA((3,)), DMA((4,)), DMA((3,)), DMA((4,)), DMA((8,)), DMA((8,)), DMA((7,)), DMA((8,)),
            DMA((12,)), DMA((8,)), DMA((8,)), DMA((21,)), DMA((16,)),
            DMA((4,)), DMA((4,)), DMA((4,)), DMA((4,)), DMA((4,)), DMA((4,)), DMA((4,)), DMA((4,)),
            DMA((7,)), DMA((8,)), DMA((8,)), DMA((8,)),
        ] + WEIGHT_SEMS * 2,
        compiler_params=pltpu.CompilerParams(collective_id=1, has_side_effects=True),
        name="layer",
    )(
        hidden[0], project_weight.T, output_weight.T, pool,
        page_table, cache_length,
        jnp.asarray(turns), jnp.asarray(turns_page), jnp.asarray(pick, jnp.bfloat16), jnp.asarray(pick_out, jnp.bfloat16),
    )
    there = lax.ppermute(here, "req", swap)
    arrived = pl.pallas_call(
        pages_kernel,
        out_shape=shape((8, 128, 2048)),
        in_specs=[scalars] * 3 + [anywhere] * 2,
        out_specs=anywhere,
        scratch_shapes=[vmem(8, 128, 2048), DMA((8,)), DMA((8,))],
        cost_estimate=pl.CostEstimate(flops=0, bytes_accessed=4 * 8 * 128 * 2048, transcendentals=0),
        name="pages",
    )(far_table, cache_length, target_slot, first, raw)
    attention_out = pl.pallas_call(
        select_kernel,
        out_shape=shape((32, 2048)),
        in_specs=[scalars, VMEM, VMEM, anywhere],
        out_specs=VMEM,
        name="select",
    )(target_slot, here, there, arrived)
    return attention_out[None], arrived.reshape(1, 1024, 2048)


def solution(mesh):
    placed = (
        P("req", "seq", None),
        P(None, ("req", "seq")),
        P(None, ("req", "seq")),
        P("req", "seq", None, None, None),
        P("req", "seq"),
        P(),
        P(),
    )
    return jax.shard_map(
        local,
        mesh=mesh,
        in_specs=placed,
        out_specs=(P("req", "seq", None), P("req", "seq", None)),
        check_vma=False,
    )
```

```python
import functools
import math

import jax
import jax.numpy as jnp
import numpy as np
from jax import lax
from jax.experimental import pallas as pl
from jax.experimental.pallas import tpu as pltpu
from jax.sharding import PartitionSpec as P

HEAD = 128
HEADS = 8
MESH = pl.DeviceIdType.MESH
EPSILON = 1e-05
MASKED = -1e30
HELD = 1
VMEM = pl.BlockSpec(memory_space=pltpu.VMEM)
DMA = pltpu.SemaphoreType.DMA


def place():
    return lax.axis_index("req"), lax.axis_index("seq")


def greet(devices):
    barrier = pltpu.get_barrier_semaphore()
    for req, seq in devices:
        pl.semaphore_signal(barrier, inc=1, device_id=(req, seq), device_id_type=MESH)
    return lambda: pl.semaphore_wait(barrier, len(devices))


def remote(src, dst, send, recv, req, seq):
    return pltpu.make_async_remote_copy(
        src_ref=src, dst_ref=dst, send_sem=send, recv_sem=recv,
        device_id=(req, seq), device_id_type=MESH,
    )


def landed(dst, sem):
    pltpu.make_async_copy(dst, dst, sem).wait()


def begin(copies):
    for copy in copies:
        copy.start()
    return copies


def finish(copies):
    for copy in copies:
        copy.wait_send()


def spread(own, out, req, seq, send, recv, steps=(2, 1, 3), near=True):
    zh, c = seq // 2, seq % 2
    copies = [
        remote(own, out.at[seq], send.at[dz - 1], recv.at[seq], req, (zh + dz) % 4 * 2 + c)
        for dz in steps
    ]
    if near:
        copies.append(remote(own, out.at[seq], send.at[3], recv.at[seq], req, 2 * zh + 1 - c))
        pltpu.make_async_copy(own, out.at[seq], recv.at[seq]).start()
    return begin(copies)


def pass_on(out, req, seq, send, recv):
    zh, c = seq // 2, seq % 2
    copies = []
    for dz in (1, 3, 2):
        source = (zh + dz) % 4 * 2 + c
        landed(out.at[source], recv.at[source])
        copies += begin(
            [remote(out.at[source], out.at[source], send.at[3 + dz], recv.at[source], req, 2 * zh + 1 - c)]
        )
    for dz in (0, 1, 3, 2):
        source = (zh + dz) % 4 * 2 + 1 - c
        landed(out.at[source], recv.at[source])
    landed(out.at[seq], recv.at[seq])
    return copies


NEAREST = (0, 1, 3, 2)


class Weights:
    def __init__(self, pieces, w, z_send, z_recv, x_send, x_recv):
        self.pieces, self.w = pieces, w
        self.z_send, self.z_recv, self.x_send, self.x_recv = z_send, z_recv, x_send, x_recv
        self.req, self.seq = req, seq = place()
        self.y, self.x, self.zl = req // 8, req // 2 % 4, req % 2
        self.zh, self.c = seq // 2, seq % 2
        self.line = self.zh * 4 + self.zl * 2 + self.c
        self.slot = self.x % 2 * 16 + self.line

    def partners(self):
        found = [(self.y * 8 + (self.x + dx) % 4 * 2 + self.zl, self.seq) for dx in (1, 2, 3)]
        for k in range(1, 16):
            there = (self.zl * 8 + self.seq + k) % 16
            found.append((self.y * 8 + self.x * 2 + there // 8, there % 8))
        return found

    def z_copy(self, e, b):
        zh = (self.zh + e) % 4
        target = zh * 2 + self.x // 2
        there = self.y * 8 + self.x * 2 + (self.zl + b) % 2
        copy = remote(
            self.pieces.at[zh], self.w.at[self.slot], self.z_send.at[e * 2 + b], self.z_recv.at[self.line], there, target
        )
        return copy, target

    def along_z(self, y_recv):
        for e in NEAREST:
            zh = (self.zh + e) % 4
            landed(self.pieces.at[zh], y_recv.at[zh])
            copy, target = self.z_copy(e, 0)
            if e:
                copy.start()
            else:

                @pl.when(target == self.seq)
                def _():
                    pltpu.make_async_copy(
                        self.pieces.at[self.zh], self.w.at[self.slot], self.z_recv.at[self.line]
                    ).start()

                @pl.when(target != self.seq)
                def _():
                    copy.start()

            self.z_copy(e, 1)[0].start()

    def chunk(self, i):
        return (self.zh - NEAREST[i]) % 4

    def x_copy(self, h, i, step):
        k = self.chunk(i)
        block = self.w.at[pl.ds(h * 16 + 4 * k, 4)]
        there = self.y * 8 + (self.x + step) % 4 * 2 + self.zl
        return remote(block, block, self.x_send.at[(step + 1) // 2 * 8 + h * 4 + i], self.x_recv.at[h * 4 + k], there, self.seq)

    def arrived(self, h, i):
        k = self.chunk(i)
        landed(self.w.at[pl.ds(h * 16 + 4 * k, 4)], self.x_recv.at[h * 4 + k])

    def hops(self, h):
        return (self.x - 2 * self.c - h) % 4

    def along_x(self):
        for h in range(2):

            @pl.when(self.hops(h) == 0)
            def _():
                for i in range(4):
                    k = self.chunk(i)
                    for n in range(4):
                        landed(self.w.at[h * 16 + 4 * k + n], self.z_recv.at[4 * k + n])
                    self.x_copy(h, i, 1).start()
                    self.x_copy(h, i, -1).start()

        for i in range(4):
            step = 1 if i % 2 == 0 else -1
            for h in range(2):

                @pl.when((self.hops(h) == 1) | (self.hops(h) == 3))
                def _():
                    self.arrived(h, i)

                @pl.when(self.hops(h) == step % 4)
                def _():
                    self.x_copy(h, i, step).start()

        for h in range(2):

            @pl.when(self.hops(h) == 2)
            def _():
                for i in range(4):
                    self.arrived(h, i)

    def finish(self):
        for e in range(4):
            self.z_copy(e, 1)[0].wait_send()
            copy, target = self.z_copy(e, 0)
            if e:
                copy.wait_send()
            else:

                @pl.when(target != self.seq)
                def _():
                    copy.wait_send()

        for h in range(2):
            for i in range(4):
                step = 1 if i % 2 == 0 else -1

                @pl.when((self.hops(h) == 0) | (self.hops(h) == step % 4))
                def _():
                    self.x_copy(h, i, step).wait_send()

                @pl.when(self.hops(h) == 0)
                def _():
                    self.x_copy(h, i, -step).wait_send()


WEIGHT_SEMS = [DMA((8,)), DMA((16,)), DMA((16,)), DMA((8,))]


def layer_norm(row_block):
    row_mean = jnp.mean(row_block, axis=-1, keepdims=True)
    centred = row_block - row_mean
    variance = jnp.mean(centred * centred, axis=-1, keepdims=True)
    return centred / jnp.sqrt(variance + EPSILON)


def layer_kernel(
    hidden, project, out_project, pool, table, lengths, targets, turns_hbm, turns_page_hbm, pick_hbm, pick_out_hbm,
    result, raw, far_table,
    joint, normed, pieces, out_pieces, w, wo, toks, wide, qkv, spins, turns, turns_page, pick, pick_out,
    rows, bias, fresh, q, kv, keep, keep_ml, lend, lend_ml, lent, lent_ml, pair, pair_ml,
    o_all, ml_all, own, att, out, here, there, own_table, load_sem, table_send, table_recv, t_send, t_recv,
    y_send, y_recv, yo_send, yo_recv, m_send, m_recv, k_send, k_recv,
    q_send, f_send, q_recv, kv_send, kv_recv, l_send, l_recv, lm_send, lm_recv, o_send, o_recv, ml_send, ml_recv,
    a_send, a_recv, h_send, h_recv, *weight_sems,
):
    req, seq = place()
    y = req // 8
    zh, c = seq // 2, seq % 2
    other = 2 * zh + 1 - c
    far = (req + 16) % 32
    weights = Weights(pieces, w, *weight_sems[:4])
    out_weights = Weights(out_pieces, wo, *weight_sems[4:])
    met = greet(weights.partners() + [((req + 8 * d) % 32, seq) for d in (1, 2, 3)])
    stored = ((turns_hbm, turns), (turns_page_hbm, turns_page), (pick_hbm, pick), (pick_out_hbm, pick_out), (pool, rows))
    loads = [pltpu.make_async_copy(source, held, load_sem.at[i]) for i, (source, held) in enumerate(stored)]
    for load in loads:
        load.start()
    last = project[8:12].astype(jnp.float32)
    joint[...] = jnp.concatenate(
        [project[0:8].astype(jnp.float32), jnp.concatenate([last[:, :1024], last[:, 1024:]], axis=0)], axis=1
    ).astype(jnp.bfloat16)
    lane = lax.broadcasted_iota(jnp.int32, (8, 128), 1)
    entries = jnp.zeros((8, 128), jnp.int32)
    for j in range(8):
        entries = jnp.where(lane == j, table[0, j], entries)
    own_table[...] = entries
    met()

    order = (2, 1, 3)
    y_copies = begin(
        [remote(joint, pieces.at[y], y_send.at[d - 1], y_recv.at[y], (req + 8 * d) % 32, seq) for d in order]
        + [
            remote(out_project, out_pieces.at[y], yo_send.at[d - 1], yo_recv.at[y], (req + 8 * d) % 32, seq)
            for d in order
        ]
    )
    pages = [remote(pool.at[i], raw.at[i], m_send.at[i], m_recv.at[i], far, seq) for i in range(8)]
    migration = begin([remote(own_table, far_table, table_send, table_recv, far, seq)] + pages[: 8 - HELD])
    pltpu.make_async_copy(joint, pieces.at[y], y_recv.at[y]).start()
    pltpu.make_async_copy(out_project, out_pieces.at[y], yo_recv.at[y]).start()
    normed[...] = layer_norm(hidden[...].astype(jnp.float32)).astype(jnp.bfloat16)
    for load in loads[:4]:
        load.wait()
    length = lengths[req]
    for page in range(8):
        left = jnp.int32(0)
        for j in range(8):
            left = jnp.where(table[0, j] == page, jnp.maximum(left, length - (j * 8 + seq) * 128), left)
        bias[page * 128 : page * 128 + 128] = jnp.where(
            lax.broadcasted_iota(jnp.int32, (128, 1), 0) < left, 0.0, MASKED
        ).astype(jnp.float32)
    coarse, fine = length // 256, length % 256
    cosine_page, sine_page = turns_page[0, pl.ds(coarse, 1)], turns_page[1, pl.ds(coarse, 1)]
    cosine_row, sine_row = turns[0, pl.ds(fine, 1)], turns[1, pl.ds(fine, 1)]
    cosine_start = cosine_page * cosine_row - sine_page * sine_row
    sine_start = sine_page * cosine_row + cosine_page * sine_row
    spins[0] = cosine_start * turns[0] - sine_start * turns[1]
    sine = sine_start * turns[0] + cosine_start * turns[1]
    spins[1] = jnp.where(lax.broadcasted_iota(jnp.int32, (256, 128), 1) < 64, -sine, sine)
    token = seq * 32 + lax.broadcasted_iota(jnp.int32, (32, 256), 0)
    fresh[...] = jnp.where(token <= lax.broadcasted_iota(jnp.int32, (32, 256), 1), 0.0, MASKED).astype(jnp.float32)
    copies = spread(normed, toks, req, seq, k_send, k_recv, (1, 3))
    weights.along_z(y_recv)
    copies += spread(normed, toks, req, seq, k_send, k_recv, (2,), False)
    out_weights.along_z(yo_recv)
    weights.along_x()
    copies += pass_on(toks, req, seq, k_send, k_recv)

    across = (((1,), (1,)), ((), ()))
    down = (((0,), (0,)), ((), ()))
    f32 = jnp.float32

    def multiply(n, _):
        columns = pl.ds(pl.multiple_of(n * 128, 128), 128)
        some = pl.ds(n * 16, 16)
        tokens = toks[...].reshape(256, 2048)
        tail = w[some, :, 2048:3072].reshape(128, 1024)
        wide[0, :, columns] = lax.dot_general(
            tokens, w[some, :, 0:2048].reshape(128, 2048), across, preferred_element_type=f32
        )
        wide[1, :, columns] = lax.dot_general(tokens[:, :1024], tail, across, preferred_element_type=f32)
        wide[2, :, columns] = lax.dot_general(tokens[:, 1024:], tail, across, preferred_element_type=f32)
        return 0

    lax.fori_loop(0, 2, multiply, 0)
    projected = jnp.zeros((256, 384), f32)
    for part in range(3):
        whole = wide[part]
        high = whole.astype(jnp.bfloat16)
        rest = whole - high.astype(f32)
        middle = rest.astype(jnp.bfloat16)
        low = (rest - middle.astype(f32)).astype(jnp.bfloat16)
        picked = [jnp.dot(piece, pick[part], preferred_element_type=f32) for piece in (middle, low, high)]
        projected += picked[0] + picked[1] + picked[2]
    for j in range(3):
        block = projected[:, j * HEAD : (j + 1) * HEAD]
        turned = block * spins[0] + pltpu.roll(block, 64, 1) * spins[1]
        qkv[j] = jnp.where(3 * seq + j < 2 * HEADS, turned, block).astype(jnp.bfloat16)
    finish(copies)
    finish(y_copies)
    weights.finish()

    def q_copies(j, head):
        copies = [
            remote(qkv.at[j], q.at[head], q_send.at[j * 4 + dz - 1], q_recv.at[head], req, (zh + dz) % 4 * 2 + c)
            for dz in (2, 1, 3)
        ]
        return copies + [remote(qkv.at[j], q.at[head], q_send.at[j * 4 + 3], q_recv.at[head], req, other)]

    def kv_copies(j, slot):
        copies = []
        for dp in range(1, 8):
            p = (seq + dp) % 8
            part = pl.ds(pl.multiple_of(32 * p, 32), 32)
            copies.append(
                remote(qkv.at[j, part], kv.at[slot], kv_send.at[j * 7 + dp - 1], kv_recv.at[slot], req, p)
            )
        return copies

    for j in range(3):
        slot = 3 * seq + j

        @pl.when(slot < HEADS)
        def _():
            begin(q_copies(j, slot))
            pltpu.make_async_copy(qkv.at[j], q.at[slot], q_recv.at[slot]).start()

        @pl.when(slot >= HEADS)
        def _():
            begin(kv_copies(j, slot - HEADS))
            part = pl.ds(pl.multiple_of(32 * seq, 32), 32)
            pltpu.make_async_copy(qkv.at[j, part], kv.at[slot - HEADS], kv_recv.at[slot - HEADS]).start()

    out_weights.along_x()
    loads[4].wait()

    def head_of(k):
        return k % 3 * 3 + k // 3

    def forward(head):
        return remote(q.at[head], q.at[head], f_send.at[head], q_recv.at[head], req, other)

    def passes(head):
        owner = head // 3
        return (c == owner % 2) & (zh != owner // 2)

    def loans(g):
        return [
            remote(lend_ml.at[g], lent_ml.at[g], lm_send.at[g], lm_recv.at[g], req, other),
            remote(lend.at[g], lent.at[g], l_send.at[g], l_recv.at[g], req, other),
        ]

    def o_copies(g):
        lane = 2 * g + c
        return [
            remote(pair_ml.at[g], ml_all.at[zh], ml_send.at[g], ml_recv.at[zh], req, lane),
            remote(pair.at[g], o_all.at[zh], o_send.at[g], o_recv.at[zh], req, lane),
        ]

    def deal(g):
        @pl.when(g == zh)
        def _():
            pltpu.make_async_copy(pair_ml.at[g], ml_all.at[zh], ml_recv.at[zh]).start()
            pltpu.make_async_copy(pair.at[g], o_all.at[zh], o_recv.at[zh]).start()

        @pl.when(g != zh)
        def _():
            begin(o_copies(g))

    def join(g):
        landed(lent_ml.at[g], lm_recv.at[g])
        landed(lent.at[g], l_recv.at[g])
        first, second = keep_ml[g], lent_ml[g]
        top = jnp.maximum(first[0:1], second[0:1])
        mine, theirs = jnp.exp(first[0:1] - top), jnp.exp(second[0:1] - top)
        pair[g] = (mine * keep[g] + theirs * lent[g].astype(jnp.float32)).astype(jnp.bfloat16)
        pair_ml[g] = jnp.concatenate(
            [top, mine * first[1:2] + theirs * second[1:2], jnp.zeros((6, 256), jnp.float32)], axis=0
        )

    scale = HEAD ** (-0.5)

    def attend(head):
        landed(q.at[head], q_recv.at[head])

        @pl.when(passes(head))
        def _():
            forward(head).start()

        landed(kv.at[head], kv_recv.at[head])
        landed(kv.at[head + 8], kv_recv.at[head + 8])
        keys = rows[:, :, pl.ds(pl.multiple_of(head * 128, 128), 128)].reshape(1024, 128)
        values = rows[:, :, pl.ds(pl.multiple_of(head * 128 + 1024, 128), 128)].reshape(1024, 128)
        query = q[head]
        s = lax.dot_general(keys, query, across, preferred_element_type=jnp.float32) * scale + bias[...]
        sn = lax.dot_general(kv[head], query, across, preferred_element_type=jnp.float32) * scale + fresh[...]
        highest = jnp.maximum(jnp.max(s, axis=0, keepdims=True), jnp.max(sn, axis=0, keepdims=True))
        p = jnp.exp(s - highest)
        pn = jnp.exp(sn - highest)
        totals = jnp.sum(p, axis=0, keepdims=True) + jnp.sum(pn, axis=0, keepdims=True)
        summed = lax.dot_general(values, p.astype(jnp.bfloat16), down, preferred_element_type=jnp.float32)
        summed += lax.dot_general(kv[head + 8], pn.astype(jnp.bfloat16), down, preferred_element_type=jnp.float32)
        state = jnp.concatenate([highest, totals, jnp.zeros((6, 256), jnp.float32)], axis=0)
        g = head // 2

        @pl.when(head % 2 == c)
        def _():
            keep[g] = summed
            keep_ml[g] = state

        @pl.when(head % 2 != c)
        def _():
            lend[g] = summed.astype(jnp.bfloat16)
            lend_ml[g] = state

    def step(k, _):
        @pl.when(k < 8)
        def _():
            attend(head_of(k))

        def head_at(lag):
            return head_of(jnp.clip(k - lag, 0, 7))

        def due(lag, ours):
            mine = head_at(lag) % 2 == c
            return (k >= lag) & (k < 8 + lag) & (mine if ours else jnp.logical_not(mine))

        @pl.when(due(1, False))
        def _():
            begin(loans(head_at(1) // 2))

        @pl.when(due(3, True))
        def _():
            deal(head_at(3) // 2)

        @pl.when(due(2, True))
        def _():
            join(head_at(2) // 2)

        return 0

    lax.fori_loop(0, 11, step, 0)

    for chip in range(4):
        landed(ml_all.at[chip], ml_recv.at[chip])
        landed(o_all.at[chip], o_recv.at[chip])
    top = ml_all[0, 0:1]
    for chip in range(1, 4):
        top = jnp.maximum(top, ml_all[chip, 0:1])
    summed = jnp.zeros((128, 256), jnp.float32)
    total = jnp.zeros((1, 256), jnp.float32)
    for chip in range(4):
        factor = jnp.exp(ml_all[chip, 0:1] - top)
        total += factor * ml_all[chip, 1:2]
        summed += factor * o_all[chip].astype(jnp.float32)
    own[...] = (summed / total).astype(jnp.bfloat16)
    for head in range(HEADS):
        @pl.when(passes(head))
        def _():
            forward(head).wait_send()

    for g in range(4):
        finish(loans(g))

        @pl.when(g != zh)
        def _():
            finish(o_copies(g))

    copies = spread(own, att, req, seq, a_send, a_recv)
    copies += pass_on(att, req, seq, a_send, a_recv)

    product = lax.dot_general(
        att[...].reshape(1024, 256), wo[...].reshape(256, 1024), (((0,), (1,)), ((), ())), preferred_element_type=f32
    ).astype(jnp.bfloat16)
    out[...] = jnp.dot(product, pick_out[...], preferred_element_type=f32).astype(jnp.bfloat16)
    finish(copies)
    for j in range(3):
        slot = 3 * seq + j

        @pl.when(slot < HEADS)
        def _():
            finish(q_copies(j, slot))

        @pl.when(slot >= HEADS)
        def _():
            finish(kv_copies(j, slot - HEADS))

    out_weights.finish()
    mine = pl.ds(pl.multiple_of(256 * seq, 256), 256)
    copies = []
    for dp in (4, 3, 5, 2, 6, 1, 7):
        p = (seq + dp) % 8
        part = pl.ds(pl.multiple_of(32 * p, 32), 32)
        copies.append(remote(out.at[part], here.at[:, mine], h_send.at[dp], h_recv.at[seq], req, p))
    begin(copies)
    part = pl.ds(pl.multiple_of(32 * seq, 32), 32)
    pltpu.make_async_copy(out.at[part], here.at[:, mine], h_recv.at[seq]).start()
    for lane in range(8):
        landed(here.at[:, pl.ds(256 * lane, 256)], h_recv.at[lane])
    copies += begin([remote(here, there, t_send, t_recv, far, seq)])
    migration += begin(pages[8 - HELD :])
    finish(copies)
    landed(there, t_recv)
    result[...] = jnp.where(targets[req] != req, there[...], here[...])
    landed(far_table, table_recv)
    for i in range(8):
        landed(raw.at[i], m_recv.at[i])
    finish(migration)


def pages_kernel(table, lengths, targets, pages, out, buf, write_sem):
    req, seq = place()
    length = jnp.where(targets[req] != req, lengths[(req + 16) % 32], 0)
    for whole in range(2):
        for j in range(8):
            left = length - (j * 8 + seq) * 128
            page = table[0, j]
            if whole:

                @pl.when((left > 0) & (left < 128))
                def _():
                    row = lax.broadcasted_iota(jnp.int32, (128, 2048), 0)
                    buf[j] = jnp.where(row < left, pages[page], jnp.zeros((128, 2048), jnp.bfloat16))
                    pltpu.make_async_copy(buf.at[j], out.at[j], write_sem.at[j]).start()

                @pl.when(left <= 0)
                def _():
                    pltpu.make_async_copy(buf.at[8], out.at[j], write_sem.at[j]).start()

            else:

                @pl.when(left >= 128)
                def _():
                    pltpu.make_async_copy(pages.at[page], out.at[j], write_sem.at[j]).start()

        if not whole:
            buf[8] = jnp.zeros((128, 2048), jnp.bfloat16)
    for j in range(8):
        pltpu.make_async_copy(buf.at[8], out.at[j], write_sem.at[j]).wait()


def shape(dims, dtype=jnp.bfloat16):
    return jax.ShapeDtypeStruct(dims, dtype)


def vmem(*dims, dtype=jnp.bfloat16):
    return pltpu.VMEM(dims, dtype)


def tables():
    frequency = np.exp(-math.log(10000.0) * 2.0 * np.arange(64) / HEAD)
    frequency = np.concatenate([frequency, frequency])
    step = np.arange(256)[:, None] * frequency
    page = 256.0 * np.arange(40)[:, None] * frequency
    turns = np.stack([np.cos(step), np.sin(step)]).astype(np.float32)
    turns_page = np.stack([np.cos(page), np.sin(page)]).astype(np.float32)
    row = np.arange(256)
    slot, entry = row // 8, row % 8
    piece = slot // 16 * 16 + slot // 2 % 2 * 8 + slot // 4 % 4 * 2 + slot % 2
    columns = (
        piece * 12 + entry,
        np.where(entry < 4, piece * 12 + 8 + entry, -1),
        np.where(entry >= 4, piece * 12 + 4 + entry, -1),
    )
    pick = np.stack([column[:, None] == np.arange(384) for column in columns])
    pick_out = (piece * 8 + entry)[:, None] == np.arange(256)
    return turns, turns_page, pick, pick_out


def local(hidden, project_weight, output_weight, cache_pool, page_table, cache_length, target_slot):
    anywhere = pl.BlockSpec(memory_space=pl.ANY)
    scalars = pl.BlockSpec(memory_space=pltpu.SMEM)
    turns, turns_page, pick, pick_out = tables()
    f32 = jnp.float32
    attention_out, raw, far_table = pl.pallas_call(
        layer_kernel,
        out_shape=(shape((32, 2048)), vmem(8, 128, 2048), shape((8, 128), jnp.int32)),
        in_specs=[VMEM] * 3 + [anywhere] + [scalars] * 3 + [anywhere] * 4,
        out_specs=(VMEM, VMEM, VMEM),
        scratch_shapes=[
            vmem(8, 3072), vmem(32, 2048), vmem(4, 8, 3072), vmem(4, 8, 1024),
            vmem(32, 8, 3072), vmem(32, 8, 1024), vmem(8, 32, 2048),
            vmem(3, 256, 256, dtype=f32), vmem(3, 256, 128), vmem(2, 256, 128, dtype=f32),
            vmem(2, 256, 128, dtype=f32), vmem(2, 40, 128, dtype=f32), vmem(3, 256, 384), vmem(256, 256),
            vmem(8, 128, 2048), vmem(1024, 1, dtype=f32), vmem(32, 256, dtype=f32),
            vmem(8, 256, 128), vmem(16, 32, 128),
            vmem(4, 128, 256, dtype=f32), vmem(4, 8, 256, dtype=f32),
            vmem(4, 128, 256), vmem(4, 8, 256, dtype=f32),
            vmem(4, 128, 256), vmem(4, 8, 256, dtype=f32),
            vmem(4, 128, 256), vmem(4, 8, 256, dtype=f32),
            vmem(4, 128, 256), vmem(4, 8, 256, dtype=f32),
            vmem(128, 256), vmem(8, 128, 256), vmem(256, 256), vmem(32, 2048), vmem(32, 2048),
            vmem(8, 128, dtype=jnp.int32), DMA((5,)), DMA, DMA, DMA, DMA,
            DMA((3,)), DMA((4,)), DMA((3,)), DMA((4,)), DMA((8,)), DMA((8,)), DMA((7,)), DMA((8,)),
            DMA((12,)), DMA((8,)), DMA((8,)), DMA((21,)), DMA((16,)),
            DMA((4,)), DMA((4,)), DMA((4,)), DMA((4,)), DMA((4,)), DMA((4,)), DMA((4,)), DMA((4,)),
            DMA((7,)), DMA((8,)), DMA((8,)), DMA((8,)),
        ] + WEIGHT_SEMS * 2,
        compiler_params=pltpu.CompilerParams(
            collective_id=1, has_side_effects=True, vmem_limit_bytes=62650000
        ),
        name="layer",
    )(
        hidden[0], project_weight.T, output_weight.T, cache_pool.reshape(8, 128, 2048),
        page_table, cache_length, target_slot,
        jnp.asarray(turns), jnp.asarray(turns_page), jnp.asarray(pick, jnp.bfloat16), jnp.asarray(pick_out, jnp.bfloat16),
    )
    arrived = pl.pallas_call(
        pages_kernel,
        out_shape=shape((8, 128, 2048)),
        in_specs=[scalars] * 3 + [VMEM],
        out_specs=anywhere,
        scratch_shapes=[vmem(9, 128, 2048), DMA((8,))],
        compiler_params=pltpu.CompilerParams(vmem_limit_bytes=16 * 2**20),
        name="pages",
    )(far_table, cache_length, target_slot, pltpu.with_memory_space_constraint(raw, pltpu.VMEM))
    return attention_out[None], arrived.reshape(1, 1024, 2048)


def solution(mesh):
    placed = (
        P("req", "seq", None),
        P(None, ("req", "seq")),
        P(None, ("req", "seq")),
        P("req", "seq", None, None, None),
        P("req", "seq"),
        P(),
        P(),
    )
    return jax.shard_map(
        local,
        mesh=mesh,
        in_specs=placed,
        out_specs=(P("req", "seq", None), P("req", "seq", None)),
        check_vma=False,
    )
```

```python
import functools
import math

import jax
import jax.numpy as jnp
import numpy as np
from jax import lax
from jax.experimental import pallas as pl
from jax.experimental.pallas import tpu as pltpu
from jax.sharding import PartitionSpec as P

HEAD = 128
HEADS = 8
MESH = pl.DeviceIdType.MESH
EPSILON = 1e-05
MASKED = -1e30
HELD = 2
VMEM = pl.BlockSpec(memory_space=pltpu.VMEM)
DMA = pltpu.SemaphoreType.DMA


def place():
    return lax.axis_index("req"), lax.axis_index("seq")


def greet(devices):
    barrier = pltpu.get_barrier_semaphore()
    for req, seq in devices:
        pl.semaphore_signal(barrier, inc=1, device_id=(req, seq), device_id_type=MESH)
    return lambda: pl.semaphore_wait(barrier, len(devices))


def remote(src, dst, send, recv, req, seq):
    return pltpu.make_async_remote_copy(
        src_ref=src, dst_ref=dst, send_sem=send, recv_sem=recv,
        device_id=(req, seq), device_id_type=MESH,
    )


def landed(dst, sem):
    pltpu.make_async_copy(dst, dst, sem).wait()


def begin(copies):
    for copy in copies:
        copy.start()
    return copies


def finish(copies):
    for copy in copies:
        copy.wait_send()


def spread(own, out, req, seq, send, recv, steps=(2, 1, 3), near=True):
    zh, c = seq // 2, seq % 2
    copies = [
        remote(own, out.at[seq], send.at[dz - 1], recv.at[seq], req, (zh + dz) % 4 * 2 + c)
        for dz in steps
    ]
    if near:
        copies.append(remote(own, out.at[seq], send.at[3], recv.at[seq], req, 2 * zh + 1 - c))
        pltpu.make_async_copy(own, out.at[seq], recv.at[seq]).start()
    return begin(copies)


def pass_on(out, req, seq, send, recv):
    zh, c = seq // 2, seq % 2
    copies = []
    for dz in (1, 3, 2):
        source = (zh + dz) % 4 * 2 + c
        landed(out.at[source], recv.at[source])
        copies += begin(
            [remote(out.at[source], out.at[source], send.at[3 + dz], recv.at[source], req, 2 * zh + 1 - c)]
        )
    for dz in (0, 1, 3, 2):
        source = (zh + dz) % 4 * 2 + 1 - c
        landed(out.at[source], recv.at[source])
    landed(out.at[seq], recv.at[seq])
    return copies


NEAREST = (0, 1, 3, 2)


class Weights:
    def __init__(self, pieces, w, z_send, z_recv, x_send, x_recv):
        self.pieces, self.w = pieces, w
        self.z_send, self.z_recv, self.x_send, self.x_recv = z_send, z_recv, x_send, x_recv
        self.req, self.seq = req, seq = place()
        self.y, self.x, self.zl = req // 8, req // 2 % 4, req % 2
        self.zh, self.c = seq // 2, seq % 2
        self.line = self.zh * 4 + self.zl * 2 + self.c
        self.slot = self.x % 2 * 16 + self.line

    def partners(self):
        found = [(self.y * 8 + (self.x + dx) % 4 * 2 + self.zl, self.seq) for dx in (1, 2, 3)]
        for k in range(1, 16):
            there = (self.zl * 8 + self.seq + k) % 16
            found.append((self.y * 8 + self.x * 2 + there // 8, there % 8))
        return found

    def z_copy(self, e, b):
        zh = (self.zh + e) % 4
        target = zh * 2 + self.x // 2
        there = self.y * 8 + self.x * 2 + (self.zl + b) % 2
        copy = remote(
            self.pieces.at[zh], self.w.at[self.slot], self.z_send.at[e * 2 + b], self.z_recv.at[self.line], there, target
        )
        return copy, target

    def along_z(self, y_recv):
        for e in NEAREST:
            zh = (self.zh + e) % 4
            landed(self.pieces.at[zh], y_recv.at[zh])
            copy, target = self.z_copy(e, 0)
            if e:
                copy.start()
            else:

                @pl.when(target == self.seq)
                def _():
                    pltpu.make_async_copy(
                        self.pieces.at[self.zh], self.w.at[self.slot], self.z_recv.at[self.line]
                    ).start()

                @pl.when(target != self.seq)
                def _():
                    copy.start()

            self.z_copy(e, 1)[0].start()

    def chunk(self, i):
        return (self.zh - NEAREST[i]) % 4

    def x_copy(self, h, i, step):
        k = self.chunk(i)
        block = self.w.at[pl.ds(h * 16 + 4 * k, 4)]
        there = self.y * 8 + (self.x + step) % 4 * 2 + self.zl
        return remote(block, block, self.x_send.at[(step + 1) // 2 * 8 + h * 4 + i], self.x_recv.at[h * 4 + k], there, self.seq)

    def arrived(self, h, i):
        k = self.chunk(i)
        landed(self.w.at[pl.ds(h * 16 + 4 * k, 4)], self.x_recv.at[h * 4 + k])

    def hops(self, h):
        return (self.x - 2 * self.c - h) % 4

    def along_x(self):
        for h in range(2):

            @pl.when(self.hops(h) == 0)
            def _():
                for i in range(4):
                    k = self.chunk(i)
                    for n in range(4):
                        landed(self.w.at[h * 16 + 4 * k + n], self.z_recv.at[4 * k + n])
                    self.x_copy(h, i, 1).start()
                    self.x_copy(h, i, -1).start()

        for i in range(4):
            step = 1 if i % 2 == 0 else -1
            for h in range(2):

                @pl.when((self.hops(h) == 1) | (self.hops(h) == 3))
                def _():
                    self.arrived(h, i)

                @pl.when(self.hops(h) == step % 4)
                def _():
                    self.x_copy(h, i, step).start()

        for h in range(2):

            @pl.when(self.hops(h) == 2)
            def _():
                for i in range(4):
                    self.arrived(h, i)

    def finish(self):
        for e in range(4):
            self.z_copy(e, 1)[0].wait_send()
            copy, target = self.z_copy(e, 0)
            if e:
                copy.wait_send()
            else:

                @pl.when(target != self.seq)
                def _():
                    copy.wait_send()

        for h in range(2):
            for i in range(4):
                step = 1 if i % 2 == 0 else -1

                @pl.when((self.hops(h) == 0) | (self.hops(h) == step % 4))
                def _():
                    self.x_copy(h, i, step).wait_send()

                @pl.when(self.hops(h) == 0)
                def _():
                    self.x_copy(h, i, -step).wait_send()


WEIGHT_SEMS = [DMA((8,)), DMA((16,)), DMA((16,)), DMA((8,))]


def layer_norm(row_block):
    row_mean = jnp.mean(row_block, axis=-1, keepdims=True)
    centred = row_block - row_mean
    variance = jnp.mean(centred * centred, axis=-1, keepdims=True)
    return centred / jnp.sqrt(variance + EPSILON)


def layer_kernel(
    hidden, project, out_project, pool, table, lengths, targets, turns_hbm, turns_page_hbm, pick_hbm, pick_out_hbm,
    here, raw, far_table,
    joint, normed, pieces, out_pieces, w, wo, toks, wide, qkv, spins, turns, turns_page, pick, pick_out,
    rows, bias, fresh, q, kv, keep, keep_ml, lend, lend_ml, lent, lent_ml, pair, pair_ml,
    o_all, ml_all, own, theirs, chosen, att, out, own_table, load_sem, table_send, table_recv, t_send, t_recv,
    y_send, y_recv, yo_send, yo_recv, m_send, m_recv, k_send, k_recv,
    q_send, f_send, q_recv, kv_send, kv_recv, l_send, l_recv, lm_send, lm_recv, o_send, o_recv, ml_send, ml_recv,
    a_send, a_recv, h_send, h_recv, *weight_sems,
):
    req, seq = place()
    y = req // 8
    zh, c = seq // 2, seq % 2
    other = 2 * zh + 1 - c
    far = (req + 16) % 32
    weights = Weights(pieces, w, *weight_sems[:4])
    out_weights = Weights(out_pieces, wo, *weight_sems[4:])
    met = greet(weights.partners() + [((req + 8 * d) % 32, seq) for d in (1, 2, 3)])
    stored = ((turns_hbm, turns), (turns_page_hbm, turns_page), (pick_hbm, pick), (pick_out_hbm, pick_out), (pool, rows))
    loads = [pltpu.make_async_copy(source, held, load_sem.at[i]) for i, (source, held) in enumerate(stored)]
    for load in loads:
        load.start()
    last = project[8:12].astype(jnp.float32)
    joint[...] = jnp.concatenate(
        [project[0:8].astype(jnp.float32), jnp.concatenate([last[:, :1024], last[:, 1024:]], axis=0)], axis=1
    ).astype(jnp.bfloat16)
    lane = lax.broadcasted_iota(jnp.int32, (8, 128), 1)
    entries = jnp.zeros((8, 128), jnp.int32)
    for j in range(8):
        entries = jnp.where(lane == j, table[0, j], entries)
    own_table[...] = entries
    met()

    order = (2, 1, 3)
    y_copies = begin(
        [remote(joint, pieces.at[y], y_send.at[d - 1], y_recv.at[y], (req + 8 * d) % 32, seq) for d in order]
        + [
            remote(out_project, out_pieces.at[y], yo_send.at[d - 1], yo_recv.at[y], (req + 8 * d) % 32, seq)
            for d in order
        ]
    )
    pages = [remote(pool.at[i], raw.at[i], m_send.at[i], m_recv.at[i], far, seq) for i in range(8)]
    migration = begin([remote(own_table, far_table, table_send, table_recv, far, seq)] + pages[: 8 - HELD])
    pltpu.make_async_copy(joint, pieces.at[y], y_recv.at[y]).start()
    pltpu.make_async_copy(out_project, out_pieces.at[y], yo_recv.at[y]).start()
    normed[...] = layer_norm(hidden[...].astype(jnp.float32)).astype(jnp.bfloat16)
    for load in loads[:4]:
        load.wait()
    length = lengths[req]
    for page in range(8):
        left = jnp.int32(0)
        for j in range(8):
            left = jnp.where(table[0, j] == page, jnp.maximum(left, length - (j * 8 + seq) * 128), left)
        bias[page * 128 : page * 128 + 128] = jnp.where(
            lax.broadcasted_iota(jnp.int32, (128, 1), 0) < left, 0.0, MASKED
        ).astype(jnp.float32)
    coarse, fine = length // 256, length % 256
    cosine_page, sine_page = turns_page[0, pl.ds(coarse, 1)], turns_page[1, pl.ds(coarse, 1)]
    cosine_row, sine_row = turns[0, pl.ds(fine, 1)], turns[1, pl.ds(fine, 1)]
    cosine_start = cosine_page * cosine_row - sine_page * sine_row
    sine_start = sine_page * cosine_row + cosine_page * sine_row
    spins[0] = cosine_start * turns[0] - sine_start * turns[1]
    sine = sine_start * turns[0] + cosine_start * turns[1]
    spins[1] = jnp.where(lax.broadcasted_iota(jnp.int32, (256, 128), 1) < 64, -sine, sine)
    token = seq * 32 + lax.broadcasted_iota(jnp.int32, (32, 256), 0)
    fresh[...] = jnp.where(token <= lax.broadcasted_iota(jnp.int32, (32, 256), 1), 0.0, MASKED).astype(jnp.float32)
    copies = spread(normed, toks, req, seq, k_send, k_recv, (1, 3))
    weights.along_z(y_recv)
    copies += spread(normed, toks, req, seq, k_send, k_recv, (2,), False)
    out_weights.along_z(yo_recv)
    weights.along_x()
    copies += pass_on(toks, req, seq, k_send, k_recv)

    across = (((1,), (1,)), ((), ()))
    down = (((0,), (0,)), ((), ()))
    f32 = jnp.float32

    def multiply(n, _):
        columns = pl.ds(pl.multiple_of(n * 128, 128), 128)
        some = pl.ds(n * 16, 16)
        tokens = toks[...].reshape(256, 2048)
        tail = w[some, :, 2048:3072].reshape(128, 1024)
        wide[0, :, columns] = lax.dot_general(
            tokens, w[some, :, 0:2048].reshape(128, 2048), across, preferred_element_type=f32
        )
        wide[1, :, columns] = lax.dot_general(tokens[:, :1024], tail, across, preferred_element_type=f32)
        wide[2, :, columns] = lax.dot_general(tokens[:, 1024:], tail, across, preferred_element_type=f32)
        return 0

    lax.fori_loop(0, 2, multiply, 0)
    projected = jnp.zeros((256, 384), f32)
    for part in range(3):
        whole = wide[part]
        high = whole.astype(jnp.bfloat16)
        rest = whole - high.astype(f32)
        middle = rest.astype(jnp.bfloat16)
        low = (rest - middle.astype(f32)).astype(jnp.bfloat16)
        picked = [jnp.dot(piece, pick[part], preferred_element_type=f32) for piece in (middle, low, high)]
        projected += picked[0] + picked[1] + picked[2]
    for j in range(3):
        block = projected[:, j * HEAD : (j + 1) * HEAD]
        turned = block * spins[0] + pltpu.roll(block, 64, 1) * spins[1]
        qkv[j] = jnp.where(3 * seq + j < 2 * HEADS, turned, block).astype(jnp.bfloat16)
    finish(copies)
    finish(y_copies)
    weights.finish()

    def q_copies(j, head):
        copies = [
            remote(qkv.at[j], q.at[head], q_send.at[j * 4 + dz - 1], q_recv.at[head], req, (zh + dz) % 4 * 2 + c)
            for dz in (2, 1, 3)
        ]
        return copies + [remote(qkv.at[j], q.at[head], q_send.at[j * 4 + 3], q_recv.at[head], req, other)]

    def kv_copies(j, slot):
        copies = []
        for dp in range(1, 8):
            p = (seq + dp) % 8
            part = pl.ds(pl.multiple_of(32 * p, 32), 32)
            copies.append(
                remote(qkv.at[j, part], kv.at[slot], kv_send.at[j * 7 + dp - 1], kv_recv.at[slot], req, p)
            )
        return copies

    for j in range(3):
        slot = 3 * seq + j

        @pl.when(slot < HEADS)
        def _():
            begin(q_copies(j, slot))
            pltpu.make_async_copy(qkv.at[j], q.at[slot], q_recv.at[slot]).start()

        @pl.when(slot >= HEADS)
        def _():
            begin(kv_copies(j, slot - HEADS))
            part = pl.ds(pl.multiple_of(32 * seq, 32), 32)
            pltpu.make_async_copy(qkv.at[j, part], kv.at[slot - HEADS], kv_recv.at[slot - HEADS]).start()

    out_weights.along_x()
    loads[4].wait()

    def head_of(k):
        return k % 3 * 3 + k // 3

    def forward(head):
        return remote(q.at[head], q.at[head], f_send.at[head], q_recv.at[head], req, other)

    def passes(head):
        owner = head // 3
        return (c == owner % 2) & (zh != owner // 2)

    def loans(g):
        return [
            remote(lend_ml.at[g], lent_ml.at[g], lm_send.at[g], lm_recv.at[g], req, other),
            remote(lend.at[g], lent.at[g], l_send.at[g], l_recv.at[g], req, other),
        ]

    def o_copies(g):
        lane = 2 * g + c
        return [
            remote(pair_ml.at[g], ml_all.at[zh], ml_send.at[g], ml_recv.at[zh], req, lane),
            remote(pair.at[g], o_all.at[zh], o_send.at[g], o_recv.at[zh], req, lane),
        ]

    def deal(g):
        @pl.when(g == zh)
        def _():
            pltpu.make_async_copy(pair_ml.at[g], ml_all.at[zh], ml_recv.at[zh]).start()
            pltpu.make_async_copy(pair.at[g], o_all.at[zh], o_recv.at[zh]).start()

        @pl.when(g != zh)
        def _():
            begin(o_copies(g))

    def join(g):
        landed(lent_ml.at[g], lm_recv.at[g])
        landed(lent.at[g], l_recv.at[g])
        first, second = keep_ml[g], lent_ml[g]
        top = jnp.maximum(first[0:1], second[0:1])
        mine, theirs = jnp.exp(first[0:1] - top), jnp.exp(second[0:1] - top)
        pair[g] = (mine * keep[g] + theirs * lent[g].astype(jnp.float32)).astype(jnp.bfloat16)
        pair_ml[g] = jnp.concatenate(
            [top, mine * first[1:2] + theirs * second[1:2], jnp.zeros((6, 256), jnp.float32)], axis=0
        )

    scale = HEAD ** (-0.5)

    def attend(head):
        landed(q.at[head], q_recv.at[head])

        @pl.when(passes(head))
        def _():
            forward(head).start()

        landed(kv.at[head], kv_recv.at[head])
        landed(kv.at[head + 8], kv_recv.at[head + 8])
        keys = rows[:, :, pl.ds(pl.multiple_of(head * 128, 128), 128)].reshape(1024, 128)
        values = rows[:, :, pl.ds(pl.multiple_of(head * 128 + 1024, 128), 128)].reshape(1024, 128)
        query = q[head]
        s = lax.dot_general(keys, query, across, preferred_element_type=jnp.float32) * scale + bias[...]
        sn = lax.dot_general(kv[head], query, across, preferred_element_type=jnp.float32) * scale + fresh[...]
        highest = jnp.maximum(jnp.max(s, axis=0, keepdims=True), jnp.max(sn, axis=0, keepdims=True))
        p = jnp.exp(s - highest)
        pn = jnp.exp(sn - highest)
        totals = jnp.sum(p, axis=0, keepdims=True) + jnp.sum(pn, axis=0, keepdims=True)
        summed = lax.dot_general(values, p.astype(jnp.bfloat16), down, preferred_element_type=jnp.float32)
        summed += lax.dot_general(kv[head + 8], pn.astype(jnp.bfloat16), down, preferred_element_type=jnp.float32)
        state = jnp.concatenate([highest, totals, jnp.zeros((6, 256), jnp.float32)], axis=0)
        g = head // 2

        @pl.when(head % 2 == c)
        def _():
            keep[g] = summed
            keep_ml[g] = state

        @pl.when(head % 2 != c)
        def _():
            lend[g] = summed.astype(jnp.bfloat16)
            lend_ml[g] = state

    def step(k, _):
        @pl.when(k < 8)
        def _():
            attend(head_of(k))

        def head_at(lag):
            return head_of(jnp.clip(k - lag, 0, 7))

        def due(lag, ours):
            mine = head_at(lag) % 2 == c
            return (k >= lag) & (k < 8 + lag) & (mine if ours else jnp.logical_not(mine))

        @pl.when(due(1, False))
        def _():
            begin(loans(head_at(1) // 2))

        @pl.when(due(3, True))
        def _():
            deal(head_at(3) // 2)

        @pl.when(due(2, True))
        def _():
            join(head_at(2) // 2)

        return 0

    lax.fori_loop(0, 11, step, 0)

    for chip in range(4):
        landed(ml_all.at[chip], ml_recv.at[chip])
        landed(o_all.at[chip], o_recv.at[chip])
    top = ml_all[0, 0:1]
    for chip in range(1, 4):
        top = jnp.maximum(top, ml_all[chip, 0:1])
    summed = jnp.zeros((128, 256), jnp.float32)
    total = jnp.zeros((1, 256), jnp.float32)
    for chip in range(4):
        factor = jnp.exp(ml_all[chip, 0:1] - top)
        total += factor * ml_all[chip, 1:2]
        summed += factor * o_all[chip].astype(jnp.float32)
    own[...] = (summed / total).astype(jnp.bfloat16)
    for head in range(HEADS):
        @pl.when(passes(head))
        def _():
            forward(head).wait_send()

    for g in range(4):
        finish(loans(g))

        @pl.when(g != zh)
        def _():
            finish(o_copies(g))

    crossing = begin([remote(own, theirs, t_send, t_recv, far, seq)])
    migration += begin(pages[8 - HELD :])
    landed(theirs, t_recv)
    chosen[...] = jnp.where(targets[req] != req, theirs[...], own[...])
    finish(crossing)
    copies = spread(chosen, att, req, seq, a_send, a_recv)
    copies += pass_on(att, req, seq, a_send, a_recv)

    product = lax.dot_general(
        att[...].reshape(1024, 256), wo[...].reshape(256, 1024), (((0,), (1,)), ((), ())), preferred_element_type=f32
    ).astype(jnp.bfloat16)
    out[...] = jnp.dot(product, pick_out[...], preferred_element_type=f32).astype(jnp.bfloat16)
    finish(copies)
    for j in range(3):
        slot = 3 * seq + j

        @pl.when(slot < HEADS)
        def _():
            finish(q_copies(j, slot))

        @pl.when(slot >= HEADS)
        def _():
            finish(kv_copies(j, slot - HEADS))

    out_weights.finish()
    mine = pl.ds(pl.multiple_of(256 * seq, 256), 256)
    copies = []
    for dp in (4, 3, 5, 2, 6, 1, 7):
        p = (seq + dp) % 8
        part = pl.ds(pl.multiple_of(32 * p, 32), 32)
        copies.append(remote(out.at[part], here.at[:, mine], h_send.at[dp], h_recv.at[seq], req, p))
    begin(copies)
    part = pl.ds(pl.multiple_of(32 * seq, 32), 32)
    pltpu.make_async_copy(out.at[part], here.at[:, mine], h_recv.at[seq]).start()
    for lane in range(8):
        landed(here.at[:, pl.ds(256 * lane, 256)], h_recv.at[lane])
    finish(copies)
    landed(far_table, table_recv)
    for i in range(8):
        landed(raw.at[i], m_recv.at[i])
    finish(migration)


def pages_kernel(table, lengths, targets, pages, out, buf, write_sem):
    req, seq = place()
    length = jnp.where(targets[req] != req, lengths[(req + 16) % 32], 0)
    for whole in range(2):
        for j in range(8):
            left = length - (j * 8 + seq) * 128
            page = table[0, j]
            if whole:

                @pl.when((left > 0) & (left < 128))
                def _():
                    row = lax.broadcasted_iota(jnp.int32, (128, 2048), 0)
                    buf[j] = jnp.where(row < left, pages[page], jnp.zeros((128, 2048), jnp.bfloat16))
                    pltpu.make_async_copy(buf.at[j], out.at[j], write_sem.at[j]).start()

                @pl.when(left <= 0)
                def _():
                    pltpu.make_async_copy(buf.at[8], out.at[j], write_sem.at[j]).start()

            else:

                @pl.when(left >= 128)
                def _():
                    pltpu.make_async_copy(pages.at[page], out.at[j], write_sem.at[j]).start()

        if not whole:
            buf[8] = jnp.zeros((128, 2048), jnp.bfloat16)
    for j in range(8):
        pltpu.make_async_copy(buf.at[8], out.at[j], write_sem.at[j]).wait()


def shape(dims, dtype=jnp.bfloat16):
    return jax.ShapeDtypeStruct(dims, dtype)


def vmem(*dims, dtype=jnp.bfloat16):
    return pltpu.VMEM(dims, dtype)


def tables():
    frequency = np.exp(-math.log(10000.0) * 2.0 * np.arange(64) / HEAD)
    frequency = np.concatenate([frequency, frequency])
    step = np.arange(256)[:, None] * frequency
    page = 256.0 * np.arange(40)[:, None] * frequency
    turns = np.stack([np.cos(step), np.sin(step)]).astype(np.float32)
    turns_page = np.stack([np.cos(page), np.sin(page)]).astype(np.float32)
    row = np.arange(256)
    slot, entry = row // 8, row % 8
    piece = slot // 16 * 16 + slot // 2 % 2 * 8 + slot // 4 % 4 * 2 + slot % 2
    columns = (
        piece * 12 + entry,
        np.where(entry < 4, piece * 12 + 8 + entry, -1),
        np.where(entry >= 4, piece * 12 + 4 + entry, -1),
    )
    pick = np.stack([column[:, None] == np.arange(384) for column in columns])
    pick_out = (piece * 8 + entry)[:, None] == np.arange(256)
    return turns, turns_page, pick, pick_out


def local(hidden, project_weight, output_weight, cache_pool, page_table, cache_length, target_slot):
    anywhere = pl.BlockSpec(memory_space=pl.ANY)
    scalars = pl.BlockSpec(memory_space=pltpu.SMEM)
    turns, turns_page, pick, pick_out = tables()
    f32 = jnp.float32
    attention_out, raw, far_table = pl.pallas_call(
        layer_kernel,
        out_shape=(shape((32, 2048)), vmem(8, 128, 2048), vmem(8, 128, dtype=jnp.int32)),
        in_specs=[VMEM] * 3 + [anywhere] + [scalars] * 3 + [anywhere] * 4,
        out_specs=(VMEM, VMEM, VMEM),
        scratch_shapes=[
            vmem(8, 3072), vmem(32, 2048), vmem(4, 8, 3072), vmem(4, 8, 1024),
            vmem(32, 8, 3072), vmem(32, 8, 1024), vmem(8, 32, 2048),
            vmem(3, 256, 256, dtype=f32), vmem(3, 256, 128), vmem(2, 256, 128, dtype=f32),
            vmem(2, 256, 128, dtype=f32), vmem(2, 40, 128, dtype=f32), vmem(3, 256, 384), vmem(256, 256),
            vmem(8, 128, 2048), vmem(1024, 1, dtype=f32), vmem(32, 256, dtype=f32),
            vmem(8, 256, 128), vmem(16, 32, 128),
            vmem(4, 128, 256, dtype=f32), vmem(4, 8, 256, dtype=f32),
            vmem(4, 128, 256), vmem(4, 8, 256, dtype=f32),
            vmem(4, 128, 256), vmem(4, 8, 256, dtype=f32),
            vmem(4, 128, 256), vmem(4, 8, 256, dtype=f32),
            vmem(4, 128, 256), vmem(4, 8, 256, dtype=f32),
            vmem(128, 256), vmem(128, 256), vmem(128, 256), vmem(8, 128, 256), vmem(256, 256),
            vmem(8, 128, dtype=jnp.int32), DMA((5,)), DMA, DMA, DMA, DMA,
            DMA((3,)), DMA((4,)), DMA((3,)), DMA((4,)), DMA((8,)), DMA((8,)), DMA((7,)), DMA((8,)),
            DMA((12,)), DMA((8,)), DMA((8,)), DMA((21,)), DMA((16,)),
            DMA((4,)), DMA((4,)), DMA((4,)), DMA((4,)), DMA((4,)), DMA((4,)), DMA((4,)), DMA((4,)),
            DMA((7,)), DMA((8,)), DMA((8,)), DMA((8,)),
        ] + WEIGHT_SEMS * 2,
        compiler_params=pltpu.CompilerParams(
            collective_id=1, has_side_effects=True, vmem_limit_bytes=62650000
        ),
        name="layer",
    )(
        hidden[0], project_weight.T, output_weight.T, cache_pool.reshape(8, 128, 2048),
        page_table, cache_length, target_slot,
        jnp.asarray(turns), jnp.asarray(turns_page), jnp.asarray(pick, jnp.bfloat16), jnp.asarray(pick_out, jnp.bfloat16),
    )
    arrived = pl.pallas_call(
        pages_kernel,
        out_shape=shape((8, 128, 2048)),
        in_specs=[scalars] * 3 + [VMEM],
        out_specs=anywhere,
        scratch_shapes=[vmem(9, 128, 2048), DMA((8,))],
        compiler_params=pltpu.CompilerParams(vmem_limit_bytes=16 * 2**20),
        name="pages",
    )(far_table, cache_length, target_slot, pltpu.with_memory_space_constraint(raw, pltpu.VMEM))
    return attention_out[None], arrived.reshape(1, 1024, 2048)


def solution(mesh):
    placed = (
        P("req", "seq", None),
        P(None, ("req", "seq")),
        P(None, ("req", "seq")),
        P("req", "seq", None, None, None),
        P("req", "seq"),
        P(),
        P(),
    )
    return jax.shard_map(
        local,
        mesh=mesh,
        in_specs=placed,
        out_specs=(P("req", "seq", None), P("req", "seq", None)),
        check_vma=False,
    )
```

```python
import functools
import math

import jax
import jax.numpy as jnp
import numpy as np
from jax import lax
from jax.experimental import pallas as pl
from jax.experimental.pallas import tpu as pltpu
from jax.sharding import PartitionSpec as P

HEAD = 128
HEADS = 8
MESH = pl.DeviceIdType.MESH
EPSILON = 1e-05
MASKED = -1e30
HELD = 2
VMEM = pl.BlockSpec(memory_space=pltpu.VMEM)
DMA = pltpu.SemaphoreType.DMA


def place():
    return lax.axis_index("req"), lax.axis_index("seq")


def greet(devices):
    barrier = pltpu.get_barrier_semaphore()
    for req, seq in devices:
        pl.semaphore_signal(barrier, inc=1, device_id=(req, seq), device_id_type=MESH)
    return lambda: pl.semaphore_wait(barrier, len(devices))


def remote(src, dst, send, recv, req, seq):
    return pltpu.make_async_remote_copy(
        src_ref=src, dst_ref=dst, send_sem=send, recv_sem=recv,
        device_id=(req, seq), device_id_type=MESH,
    )


def landed(dst, sem):
    pltpu.make_async_copy(dst, dst, sem).wait()


def begin(copies):
    for copy in copies:
        copy.start()
    return copies


def finish(copies):
    for copy in copies:
        copy.wait_send()


def spread(own, out, req, seq, send, recv, steps=(2, 1, 3), near=True):
    zh, c = seq // 2, seq % 2
    copies = [
        remote(own, out.at[seq], send.at[dz - 1], recv.at[seq], req, (zh + dz) % 4 * 2 + c)
        for dz in steps
    ]
    if near:
        copies.append(remote(own, out.at[seq], send.at[3], recv.at[seq], req, 2 * zh + 1 - c))
        pltpu.make_async_copy(own, out.at[seq], recv.at[seq]).start()
    return begin(copies)


def pass_on(out, req, seq, send, recv):
    zh, c = seq // 2, seq % 2
    copies = []
    for dz in (1, 3, 2):
        source = (zh + dz) % 4 * 2 + c
        landed(out.at[source], recv.at[source])
        copies += begin(
            [remote(out.at[source], out.at[source], send.at[3 + dz], recv.at[source], req, 2 * zh + 1 - c)]
        )
    for dz in (0, 1, 3, 2):
        source = (zh + dz) % 4 * 2 + 1 - c
        landed(out.at[source], recv.at[source])
    landed(out.at[seq], recv.at[seq])
    return copies


NEAREST = (0, 1, 3, 2)


class Weights:
    def __init__(self, pieces, w, z_send, z_recv, x_send, x_recv):
        self.pieces, self.w = pieces, w
        self.z_send, self.z_recv, self.x_send, self.x_recv = z_send, z_recv, x_send, x_recv
        self.req, self.seq = req, seq = place()
        self.y, self.x, self.zl = req // 8, req // 2 % 4, req % 2
        self.zh, self.c = seq // 2, seq % 2
        self.line = self.zh * 4 + self.zl * 2 + self.c
        self.slot = self.x % 2 * 16 + self.line

    def partners(self):
        found = [(self.y * 8 + (self.x + dx) % 4 * 2 + self.zl, self.seq) for dx in (1, 2, 3)]
        for k in range(1, 16):
            there = (self.zl * 8 + self.seq + k) % 16
            found.append((self.y * 8 + self.x * 2 + there // 8, there % 8))
        return found

    def z_copy(self, e, b):
        zh = (self.zh + e) % 4
        target = zh * 2 + self.x // 2
        there = self.y * 8 + self.x * 2 + (self.zl + b) % 2
        copy = remote(
            self.pieces.at[zh], self.w.at[self.slot], self.z_send.at[e * 2 + b], self.z_recv.at[self.line], there, target
        )
        return copy, target

    def along_z(self, y_recv):
        for e in NEAREST:
            zh = (self.zh + e) % 4
            landed(self.pieces.at[zh], y_recv.at[zh])
            copy, target = self.z_copy(e, 0)
            if e:
                copy.start()
            else:

                @pl.when(target == self.seq)
                def _():
                    pltpu.make_async_copy(
                        self.pieces.at[self.zh], self.w.at[self.slot], self.z_recv.at[self.line]
                    ).start()

                @pl.when(target != self.seq)
                def _():
                    copy.start()

            self.z_copy(e, 1)[0].start()

    def chunk(self, i):
        return (self.zh - NEAREST[i]) % 4

    def x_copy(self, h, i, step):
        k = self.chunk(i)
        block = self.w.at[pl.ds(h * 16 + 4 * k, 4)]
        there = self.y * 8 + (self.x + step) % 4 * 2 + self.zl
        return remote(block, block, self.x_send.at[(step + 1) // 2 * 8 + h * 4 + i], self.x_recv.at[h * 4 + k], there, self.seq)

    def arrived(self, h, i):
        k = self.chunk(i)
        landed(self.w.at[pl.ds(h * 16 + 4 * k, 4)], self.x_recv.at[h * 4 + k])

    def hops(self, h):
        return (self.x - 2 * self.c - h) % 4

    def along_x(self):
        for h in range(2):

            @pl.when(self.hops(h) == 0)
            def _():
                for i in range(4):
                    k = self.chunk(i)
                    for n in range(4):
                        landed(self.w.at[h * 16 + 4 * k + n], self.z_recv.at[4 * k + n])
                    self.x_copy(h, i, 1).start()
                    self.x_copy(h, i, -1).start()

        for i in range(4):
            step = 1 if i % 2 == 0 else -1
            for h in range(2):

                @pl.when((self.hops(h) == 1) | (self.hops(h) == 3))
                def _():
                    self.arrived(h, i)

                @pl.when(self.hops(h) == step % 4)
                def _():
                    self.x_copy(h, i, step).start()

        for h in range(2):

            @pl.when(self.hops(h) == 2)
            def _():
                for i in range(4):
                    self.arrived(h, i)

    def finish(self):
        for e in range(4):
            self.z_copy(e, 1)[0].wait_send()
            copy, target = self.z_copy(e, 0)
            if e:
                copy.wait_send()
            else:

                @pl.when(target != self.seq)
                def _():
                    copy.wait_send()

        for h in range(2):
            for i in range(4):
                step = 1 if i % 2 == 0 else -1

                @pl.when((self.hops(h) == 0) | (self.hops(h) == step % 4))
                def _():
                    self.x_copy(h, i, step).wait_send()

                @pl.when(self.hops(h) == 0)
                def _():
                    self.x_copy(h, i, -step).wait_send()


WEIGHT_SEMS = [DMA((8,)), DMA((16,)), DMA((16,)), DMA((8,))]


def layer_norm(row_block):
    row_mean = jnp.mean(row_block, axis=-1, keepdims=True)
    centred = row_block - row_mean
    variance = jnp.mean(centred * centred, axis=-1, keepdims=True)
    return centred / jnp.sqrt(variance + EPSILON)


def layer_kernel(
    hidden, project, out_project, pool, table, lengths, targets, turns_hbm, turns_page_hbm, pick_hbm, pick_out_hbm,
    here, raw, far_table,
    joint, normed, pieces, out_pieces, w, wo, toks, wide, qkv, spins, turns, turns_page, pick, pick_out,
    rows, bias, fresh, q, kv, keep, keep_ml, lend, lend_ml, lent, lent_ml, pair, pair_ml,
    o_all, ml_all, own, theirs, chosen, att, out, own_table, load_sem, table_send, table_recv, t_send, t_recv,
    y_send, y_recv, yo_send, yo_recv, m_send, m_recv, k_send, k_recv,
    q_send, f_send, q_recv, kv_send, kv_recv, l_send, l_recv, lm_send, lm_recv, o_send, o_recv, ml_send, ml_recv,
    a_send, a_recv, h_send, h_recv, *weight_sems,
):
    req, seq = place()
    y = req // 8
    zh, c = seq // 2, seq % 2
    other = 2 * zh + 1 - c
    far = (req + 16) % 32
    weights = Weights(pieces, w, *weight_sems[:4])
    out_weights = Weights(out_pieces, wo, *weight_sems[4:])
    met = greet(weights.partners() + [((req + 8 * d) % 32, seq) for d in (1, 2, 3)])
    stored = ((turns_hbm, turns), (turns_page_hbm, turns_page), (pick_hbm, pick), (pick_out_hbm, pick_out), (pool, rows))
    loads = [pltpu.make_async_copy(source, held, load_sem.at[i]) for i, (source, held) in enumerate(stored)]
    for load in loads:
        load.start()
    last = project[8:12].astype(jnp.float32)
    joint[...] = jnp.concatenate(
        [project[0:8].astype(jnp.float32), jnp.concatenate([last[:, :1024], last[:, 1024:]], axis=0)], axis=1
    ).astype(jnp.bfloat16)
    lane = lax.broadcasted_iota(jnp.int32, (8, 128), 1)
    entries = jnp.zeros((8, 128), jnp.int32)
    for j in range(8):
        entries = jnp.where(lane == j, table[0, j], entries)
    own_table[...] = entries
    met()

    order = (2, 1, 3)
    y_copies = begin(
        [remote(joint, pieces.at[y], y_send.at[d - 1], y_recv.at[y], (req + 8 * d) % 32, seq) for d in order]
        + [
            remote(out_project, out_pieces.at[y], yo_send.at[d - 1], yo_recv.at[y], (req + 8 * d) % 32, seq)
            for d in order
        ]
    )
    pages = [remote(pool.at[i], raw.at[i], m_send.at[i], m_recv.at[i], far, seq) for i in range(8)]
    migration = begin([remote(own_table, far_table, table_send, table_recv, far, seq)] + pages[: 8 - HELD])
    pltpu.make_async_copy(joint, pieces.at[y], y_recv.at[y]).start()
    pltpu.make_async_copy(out_project, out_pieces.at[y], yo_recv.at[y]).start()
    normed[...] = layer_norm(hidden[...].astype(jnp.float32)).astype(jnp.bfloat16)
    for load in loads[:4]:
        load.wait()
    length = lengths[req]
    for page in range(8):
        left = jnp.int32(0)
        for j in range(8):
            left = jnp.where(table[0, j] == page, jnp.maximum(left, length - (j * 8 + seq) * 128), left)
        bias[page * 128 : page * 128 + 128] = jnp.where(
            lax.broadcasted_iota(jnp.int32, (128, 1), 0) < left, 0.0, MASKED
        ).astype(jnp.float32)
    coarse, fine = length // 256, length % 256
    cosine_page, sine_page = turns_page[0, pl.ds(coarse, 1)], turns_page[1, pl.ds(coarse, 1)]
    cosine_row, sine_row = turns[0, pl.ds(fine, 1)], turns[1, pl.ds(fine, 1)]
    cosine_start = cosine_page * cosine_row - sine_page * sine_row
    sine_start = sine_page * cosine_row + cosine_page * sine_row
    spins[0] = cosine_start * turns[0] - sine_start * turns[1]
    sine = sine_start * turns[0] + cosine_start * turns[1]
    spins[1] = jnp.where(lax.broadcasted_iota(jnp.int32, (256, 128), 1) < 64, -sine, sine)
    token = seq * 32 + lax.broadcasted_iota(jnp.int32, (32, 256), 0)
    fresh[...] = jnp.where(token <= lax.broadcasted_iota(jnp.int32, (32, 256), 1), 0.0, MASKED).astype(jnp.float32)
    copies = spread(normed, toks, req, seq, k_send, k_recv, (1, 3))
    weights.along_z(y_recv)
    copies += spread(normed, toks, req, seq, k_send, k_recv, (2,), False)
    out_weights.along_z(yo_recv)
    weights.along_x()
    copies += pass_on(toks, req, seq, k_send, k_recv)

    across = (((1,), (1,)), ((), ()))
    down = (((0,), (0,)), ((), ()))
    f32 = jnp.float32

    def multiply(n, _):
        columns = pl.ds(pl.multiple_of(n * 128, 128), 128)
        some = pl.ds(n * 16, 16)
        tokens = toks[...].reshape(256, 2048)
        tail = w[some, :, 2048:3072].reshape(128, 1024)
        wide[0, :, columns] = lax.dot_general(
            tokens, w[some, :, 0:2048].reshape(128, 2048), across, preferred_element_type=f32
        )
        wide[1, :, columns] = lax.dot_general(tokens[:, :1024], tail, across, preferred_element_type=f32)
        wide[2, :, columns] = lax.dot_general(tokens[:, 1024:], tail, across, preferred_element_type=f32)
        return 0

    lax.fori_loop(0, 2, multiply, 0)
    projected = jnp.zeros((256, 384), f32)
    for part in range(3):
        whole = wide[part]
        high = whole.astype(jnp.bfloat16)
        rest = whole - high.astype(f32)
        middle = rest.astype(jnp.bfloat16)
        low = (rest - middle.astype(f32)).astype(jnp.bfloat16)
        picked = [jnp.dot(piece, pick[part], preferred_element_type=f32) for piece in (middle, low, high)]
        projected += picked[0] + picked[1] + picked[2]
    for j in range(3):
        block = projected[:, j * HEAD : (j + 1) * HEAD]
        turned = block * spins[0] + pltpu.roll(block, 64, 1) * spins[1]
        qkv[j] = jnp.where(3 * seq + j < 2 * HEADS, turned, block).astype(jnp.bfloat16)
    finish(copies)
    finish(y_copies)
    weights.finish()

    def q_copies(j, head):
        copies = [
            remote(qkv.at[j], q.at[head], q_send.at[j * 4 + dz - 1], q_recv.at[head], req, (zh + dz) % 4 * 2 + c)
            for dz in (2, 1, 3)
        ]
        return copies + [remote(qkv.at[j], q.at[head], q_send.at[j * 4 + 3], q_recv.at[head], req, other)]

    def kv_copies(j, slot):
        copies = []
        for dp in range(1, 8):
            p = (seq + dp) % 8
            part = pl.ds(pl.multiple_of(32 * p, 32), 32)
            copies.append(
                remote(qkv.at[j, part], kv.at[slot], kv_send.at[j * 7 + dp - 1], kv_recv.at[slot], req, p)
            )
        return copies

    for j in range(3):
        slot = 3 * seq + j

        @pl.when(slot < HEADS)
        def _():
            begin(q_copies(j, slot))
            pltpu.make_async_copy(qkv.at[j], q.at[slot], q_recv.at[slot]).start()

        @pl.when(slot >= HEADS)
        def _():
            begin(kv_copies(j, slot - HEADS))
            part = pl.ds(pl.multiple_of(32 * seq, 32), 32)
            pltpu.make_async_copy(qkv.at[j, part], kv.at[slot - HEADS], kv_recv.at[slot - HEADS]).start()

    out_weights.along_x()
    loads[4].wait()

    def head_of(k):
        return k % 3 * 3 + k // 3

    def forward(head):
        return remote(q.at[head], q.at[head], f_send.at[head], q_recv.at[head], req, other)

    def passes(head):
        owner = head // 3
        return (c == owner % 2) & (zh != owner // 2)

    def loans(g):
        return [
            remote(lend_ml.at[g], lent_ml.at[g], lm_send.at[g], lm_recv.at[g], req, other),
            remote(lend.at[g], lent.at[g], l_send.at[g], l_recv.at[g], req, other),
        ]

    def o_copies(g):
        lane = 2 * g + c
        return [
            remote(pair_ml.at[g], ml_all.at[zh], ml_send.at[g], ml_recv.at[zh], req, lane),
            remote(pair.at[g], o_all.at[zh], o_send.at[g], o_recv.at[zh], req, lane),
        ]

    def deal(g):
        @pl.when(g == zh)
        def _():
            pltpu.make_async_copy(pair_ml.at[g], ml_all.at[zh], ml_recv.at[zh]).start()
            pltpu.make_async_copy(pair.at[g], o_all.at[zh], o_recv.at[zh]).start()

        @pl.when(g != zh)
        def _():
            begin(o_copies(g))

    def join(g):
        landed(lent_ml.at[g], lm_recv.at[g])
        landed(lent.at[g], l_recv.at[g])
        first, second = keep_ml[g], lent_ml[g]
        top = jnp.maximum(first[0:1], second[0:1])
        mine, theirs = jnp.exp(first[0:1] - top), jnp.exp(second[0:1] - top)
        pair[g] = (mine * keep[g] + theirs * lent[g].astype(jnp.float32)).astype(jnp.bfloat16)
        pair_ml[g] = jnp.concatenate(
            [top, mine * first[1:2] + theirs * second[1:2], jnp.zeros((6, 256), jnp.float32)], axis=0
        )

    scale = HEAD ** (-0.5)

    def attend(head):
        landed(q.at[head], q_recv.at[head])

        @pl.when(passes(head))
        def _():
            forward(head).start()

        landed(kv.at[head], kv_recv.at[head])
        landed(kv.at[head + 8], kv_recv.at[head + 8])
        keys = rows[:, :, pl.ds(pl.multiple_of(head * 128, 128), 128)].reshape(1024, 128)
        values = rows[:, :, pl.ds(pl.multiple_of(head * 128 + 1024, 128), 128)].reshape(1024, 128)
        query = q[head]
        s = lax.dot_general(keys, query, across, preferred_element_type=jnp.float32) * scale + bias[...]
        sn = lax.dot_general(kv[head], query, across, preferred_element_type=jnp.float32) * scale + fresh[...]
        highest = jnp.maximum(jnp.max(s, axis=0, keepdims=True), jnp.max(sn, axis=0, keepdims=True))
        p = jnp.exp(s - highest)
        pn = jnp.exp(sn - highest)
        totals = jnp.sum(p, axis=0, keepdims=True) + jnp.sum(pn, axis=0, keepdims=True)
        summed = lax.dot_general(values, p.astype(jnp.bfloat16), down, preferred_element_type=jnp.float32)
        summed += lax.dot_general(kv[head + 8], pn.astype(jnp.bfloat16), down, preferred_element_type=jnp.float32)
        state = jnp.concatenate([highest, totals, jnp.zeros((6, 256), jnp.float32)], axis=0)
        g = head // 2

        @pl.when(head % 2 == c)
        def _():
            keep[g] = summed
            keep_ml[g] = state

        @pl.when(head % 2 != c)
        def _():
            lend[g] = summed.astype(jnp.bfloat16)
            lend_ml[g] = state

    def step(k, _):
        @pl.when(k < 8)
        def _():
            attend(head_of(k))

        def head_at(lag):
            return head_of(jnp.clip(k - lag, 0, 7))

        def due(lag, ours):
            mine = head_at(lag) % 2 == c
            return (k >= lag) & (k < 8 + lag) & (mine if ours else jnp.logical_not(mine))

        @pl.when(due(1, False))
        def _():
            begin(loans(head_at(1) // 2))

        @pl.when(due(3, True))
        def _():
            deal(head_at(3) // 2)

        @pl.when(due(2, True))
        def _():
            join(head_at(2) // 2)

        return 0

    lax.fori_loop(0, 11, step, 0)

    for chip in range(4):
        landed(ml_all.at[chip], ml_recv.at[chip])
        landed(o_all.at[chip], o_recv.at[chip])
    top = ml_all[0, 0:1]
    for chip in range(1, 4):
        top = jnp.maximum(top, ml_all[chip, 0:1])
    summed = jnp.zeros((128, 256), jnp.float32)
    total = jnp.zeros((1, 256), jnp.float32)
    for chip in range(4):
        factor = jnp.exp(ml_all[chip, 0:1] - top)
        total += factor * ml_all[chip, 1:2]
        summed += factor * o_all[chip].astype(jnp.float32)
    own[...] = (summed / total).astype(jnp.bfloat16)
    for head in range(HEADS):
        @pl.when(passes(head))
        def _():
            forward(head).wait_send()

    for g in range(4):
        finish(loans(g))

        @pl.when(g != zh)
        def _():
            finish(o_copies(g))

    crossing = begin([remote(own, theirs, t_send, t_recv, far, seq)])
    migration += begin(pages[8 - HELD :])
    landed(theirs, t_recv)
    chosen[...] = jnp.where(targets[req] != req, theirs[...], own[...])
    finish(crossing)
    copies = spread(chosen, att, req, seq, a_send, a_recv)
    copies += pass_on(att, req, seq, a_send, a_recv)

    product = lax.dot_general(
        att[...].reshape(1024, 256), wo[...].reshape(256, 1024), (((0,), (1,)), ((), ())), preferred_element_type=f32
    ).astype(jnp.bfloat16)
    out[...] = jnp.dot(product, pick_out[...], preferred_element_type=f32).astype(jnp.bfloat16)
    finish(copies)
    for j in range(3):
        slot = 3 * seq + j

        @pl.when(slot < HEADS)
        def _():
            finish(q_copies(j, slot))

        @pl.when(slot >= HEADS)
        def _():
            finish(kv_copies(j, slot - HEADS))

    out_weights.finish()
    mine = pl.ds(pl.multiple_of(256 * seq, 256), 256)
    copies = []
    for dp in (4, 3, 5, 2, 6, 1, 7):
        p = (seq + dp) % 8
        part = pl.ds(pl.multiple_of(32 * p, 32), 32)
        copies.append(remote(out.at[part], here.at[:, mine], h_send.at[dp], h_recv.at[seq], req, p))
    begin(copies)
    part = pl.ds(pl.multiple_of(32 * seq, 32), 32)
    pltpu.make_async_copy(out.at[part], here.at[:, mine], h_recv.at[seq]).start()
    for lane in range(8):
        landed(here.at[:, pl.ds(256 * lane, 256)], h_recv.at[lane])
    finish(copies)
    landed(far_table, table_recv)
    for i in range(8):
        landed(raw.at[i], m_recv.at[i])
    finish(migration)


def pages_kernel(table, lengths, targets, rows, pages, out_rows, out, buf, write_sem, rows_sem):
    req, seq = place()
    pltpu.make_async_copy(rows, out_rows, rows_sem).start()
    length = jnp.where(targets[req] != req, lengths[(req + 16) % 32], 0)
    for whole in range(2):
        for j in range(8):
            left = length - (j * 8 + seq) * 128
            page = table[0, j]
            if whole:

                @pl.when((left > 0) & (left < 128))
                def _():
                    row = lax.broadcasted_iota(jnp.int32, (128, 2048), 0)
                    buf[j] = jnp.where(row < left, pages[page], jnp.zeros((128, 2048), jnp.bfloat16))
                    pltpu.make_async_copy(buf.at[j], out.at[j], write_sem.at[j]).start()

                @pl.when(left <= 0)
                def _():
                    pltpu.make_async_copy(buf.at[8], out.at[j], write_sem.at[j]).start()

            else:

                @pl.when(left >= 128)
                def _():
                    pltpu.make_async_copy(pages.at[page], out.at[j], write_sem.at[j]).start()

        if not whole:
            buf[8] = jnp.zeros((128, 2048), jnp.bfloat16)
    for j in range(8):
        pltpu.make_async_copy(buf.at[8], out.at[j], write_sem.at[j]).wait()
    pltpu.make_async_copy(rows, out_rows, rows_sem).wait()


def shape(dims, dtype=jnp.bfloat16):
    return jax.ShapeDtypeStruct(dims, dtype)


def vmem(*dims, dtype=jnp.bfloat16):
    return pltpu.VMEM(dims, dtype)


def tables():
    frequency = np.exp(-math.log(10000.0) * 2.0 * np.arange(64) / HEAD)
    frequency = np.concatenate([frequency, frequency])
    step = np.arange(256)[:, None] * frequency
    page = 256.0 * np.arange(40)[:, None] * frequency
    turns = np.stack([np.cos(step), np.sin(step)]).astype(np.float32)
    turns_page = np.stack([np.cos(page), np.sin(page)]).astype(np.float32)
    row = np.arange(256)
    slot, entry = row // 8, row % 8
    piece = slot // 16 * 16 + slot // 2 % 2 * 8 + slot // 4 % 4 * 2 + slot % 2
    columns = (
        piece * 12 + entry,
        np.where(entry < 4, piece * 12 + 8 + entry, -1),
        np.where(entry >= 4, piece * 12 + 4 + entry, -1),
    )
    pick = np.stack([column[:, None] == np.arange(384) for column in columns])
    pick_out = (piece * 8 + entry)[:, None] == np.arange(256)
    return turns, turns_page, pick, pick_out


def local(hidden, project_weight, output_weight, cache_pool, page_table, cache_length, target_slot):
    anywhere = pl.BlockSpec(memory_space=pl.ANY)
    scalars = pl.BlockSpec(memory_space=pltpu.SMEM)
    turns, turns_page, pick, pick_out = tables()
    f32 = jnp.float32
    here, raw, far_table = pl.pallas_call(
        layer_kernel,
        out_shape=(vmem(32, 2048), vmem(8, 128, 2048), vmem(8, 128, dtype=jnp.int32)),
        in_specs=[VMEM] * 3 + [anywhere] + [scalars] * 3 + [anywhere] * 4,
        out_specs=(VMEM, VMEM, VMEM),
        scratch_shapes=[
            vmem(8, 3072), vmem(32, 2048), vmem(4, 8, 3072), vmem(4, 8, 1024),
            vmem(32, 8, 3072), vmem(32, 8, 1024), vmem(8, 32, 2048),
            vmem(3, 256, 256, dtype=f32), vmem(3, 256, 128), vmem(2, 256, 128, dtype=f32),
            vmem(2, 256, 128, dtype=f32), vmem(2, 40, 128, dtype=f32), vmem(3, 256, 384), vmem(256, 256),
            vmem(8, 128, 2048), vmem(1024, 1, dtype=f32), vmem(32, 256, dtype=f32),
            vmem(8, 256, 128), vmem(16, 32, 128),
            vmem(4, 128, 256, dtype=f32), vmem(4, 8, 256, dtype=f32),
            vmem(4, 128, 256), vmem(4, 8, 256, dtype=f32),
            vmem(4, 128, 256), vmem(4, 8, 256, dtype=f32),
            vmem(4, 128, 256), vmem(4, 8, 256, dtype=f32),
            vmem(4, 128, 256), vmem(4, 8, 256, dtype=f32),
            vmem(128, 256), vmem(128, 256), vmem(128, 256), vmem(8, 128, 256), vmem(256, 256),
            vmem(8, 128, dtype=jnp.int32), DMA((5,)), DMA, DMA, DMA, DMA,
            DMA((3,)), DMA((4,)), DMA((3,)), DMA((4,)), DMA((8,)), DMA((8,)), DMA((7,)), DMA((8,)),
            DMA((12,)), DMA((8,)), DMA((8,)), DMA((21,)), DMA((16,)),
            DMA((4,)), DMA((4,)), DMA((4,)), DMA((4,)), DMA((4,)), DMA((4,)), DMA((4,)), DMA((4,)),
            DMA((7,)), DMA((8,)), DMA((8,)), DMA((8,)),
        ] + WEIGHT_SEMS * 2,
        compiler_params=pltpu.CompilerParams(
            collective_id=1, has_side_effects=True, vmem_limit_bytes=62650000
        ),
        name="layer",
    )(
        hidden[0], project_weight.T, output_weight.T, cache_pool.reshape(8, 128, 2048),
        page_table, cache_length, target_slot,
        jnp.asarray(turns), jnp.asarray(turns_page), jnp.asarray(pick, jnp.bfloat16), jnp.asarray(pick_out, jnp.bfloat16),
    )
    attention_out, arrived = pl.pallas_call(
        pages_kernel,
        out_shape=(shape((32, 2048)), shape((8, 128, 2048))),
        in_specs=[scalars] * 3 + [VMEM] * 2,
        out_specs=(anywhere, anywhere),
        scratch_shapes=[vmem(9, 128, 2048), DMA((8,)), DMA],
        compiler_params=pltpu.CompilerParams(vmem_limit_bytes=16 * 2**20),
        name="pages",
    )(far_table, cache_length, target_slot, *(pltpu.with_memory_space_constraint(a, pltpu.VMEM) for a in (here, raw)))
    return attention_out[None], arrived.reshape(1, 1024, 2048)


def solution(mesh):
    placed = (
        P("req", "seq", None),
        P(None, ("req", "seq")),
        P(None, ("req", "seq")),
        P("req", "seq", None, None, None),
        P("req", "seq"),
        P(),
        P(),
    )
    return jax.shard_map(
        local,
        mesh=mesh,
        in_specs=placed,
        out_specs=(P("req", "seq", None), P("req", "seq", None)),
        check_vma=False,
    )
```
